32 devices in a mesh: dp: 4 (over z), expert: 8 (over y, x, core).
Axes of the slice: x: 2, y: 2, z: 4, core: 2. Of those that a mesh axis runs over, the one named last changes fastest.
Arguments:
- tokens: bfloat16 [6304, 768], P(('dp', 'expert')), may hold values from -6 to 6
- cotangent: bfloat16 [6304, 768], P(('dp', 'expert')), may hold values from -6 to 6
- routes: int32 [6304, 2], P(('dp', 'expert')), may hold values from 0 to 7, all different within a row; in each aligned block of 197 rows (0 to 196, 197 to 393, ...) at most 50 rows name the same one
- priority: int32 [32, 197], P(('dp', 'expert')), may hold values from 0 to 196, each once within a row
- ln_gains: float32 [2, 768], replicated, may hold values from 0.5 to 1.5
- ln_biases: float32 [2, 768], replicated, may hold values from -2 to 2
- qkv_weight: bfloat16 [768, 2304], P('expert'), may hold values from -0.21875 to 0.21875
- out_weight: bfloat16 [768, 768], P('expert'), may hold values from -1.25 to 1.25
- router: float32 [768, 8], replicated, may hold values from -0.21875 to 0.21875
- w_in: bfloat16 [8, 768, 1536], P('expert'), may hold values from -0.21875 to 0.21875
- w_out: bfloat16 [8, 768, 1536], P('expert'), may hold values from -0.21875 to 0.21875
- norm_momentum: float32 [4, 768], replicated, may hold values from -128 to 128
- router_momentum: float32 [768, 8], replicated, may hold values from -6000 to 6000
- qkv_momentum: float32 [768, 2304], P('expert'), may hold values from -1200 to 1200
- out_momentum: float32 [768, 768], P('expert'), may hold values from -600 to 600
- w_in_momentum: float32 [8, 768, 1536], P('expert', 'dp'), may hold values from -180 to 180
- w_out_momentum: float32 [8, 768, 1536], P('expert', 'dp'), may hold values from -180 to 180
Outputs:
- block_out: float32 [6304, 768], P(('dp', 'expert'))
- grad_tokens: float32 [6304, 768], P(('dp', 'expert'))
- grad_norm: float32 [4, 768], replicated
- grad_router: float32 [768, 8], replicated
- grad_qkv: float32 [768, 2304], P('expert')
- grad_out: float32 [768, 768], P('expert')
- grad_w_in: float32 [8, 768, 1536], P('expert', 'dp')
- grad_w_out: float32 [8, 768, 1536], P('expert', 'dp')
- new_norm: float32 [4, 768], replicated
- new_norm_momentum: float32 [4, 768], replicated
- new_router: float32 [768, 8], replicated
- new_router_momentum: float32 [768, 8], replicated
- new_qkv: float32 [768, 2304], P('expert')
- new_qkv_momentum: float32 [768, 2304], P('expert')
- new_out: float32 [768, 768], P('expert')
- new_out_momentum: float32 [768, 768], P('expert')
- new_w_in: float32 [8, 768, 1536], P('expert', 'dp')
- new_w_in_momentum: float32 [8, 768, 1536], P('expert', 'dp')
- new_w_out: float32 [8, 768, 1536], P('expert', 'dp')
- new_w_out_momentum: float32 [8, 768, 1536], P('expert', 'dp')
The draws below stay inside these ranges and needn't reach their ends.
Inputs may be any that keep to these rules, and one draw needn't show every extreme that they name: `routes`: each row names two different experts. In the rows of one device no expert is named more than 2 * 25 times. `priority`: each row is an ordering of the 197 tokens of one block.
All inputs are finite; a program needn't handle non-finite values.
Results may differ from the reference program's by a relative error of at most 0.011.
Values may be sent and summed in bfloat16 or wider, within the bound.
A program may use at most 128 MiB of HBM per device.

```python
import math
import jax
import jax.numpy as jnp
import numpy as np
from jax import lax

D = 768
HEADS = 12
FF = 1536
NS_STEPS = 5
SEQ = 197
TOK_DEV = 197
EXPERTS = 8
TOKENS = 6304
CAPACITY = 25
N_DP = 4
N_EXPERT = 8


def scaled_values(key, leading, row_count, col_count, spread):
    subkeys = jax.random.split(key, 3)
    rising = jnp.exp(jnp.log(3.0) * jnp.arange(row_count, dtype=jnp.float32) / row_count)
    row_scale = rising[None, :, None] * jnp.exp(jax.random.uniform(subkeys[0], (leading, row_count, 1), minval=0.0, maxval=1.3862944))
    col_scale = jnp.exp(jax.random.uniform(subkeys[1], (leading, 1, col_count), minval=0.0, maxval=2.3025851))
    values = jnp.clip(jax.random.normal(subkeys[2], (leading, row_count, col_count)), -4.0, 4.0)
    return spread * 0.125 * row_scale * col_scale * values


def draw_router_momentum(key, part):
    return scaled_values(jax.random.fold_in(key, 11), 1, D, EXPERTS, 100.0)[0]


def draw_qkv_momentum(key, part):
    return scaled_values(jax.random.fold_in(key, 14), 1, D, 3 * D, 20.0)[0]


def draw_out_momentum(key, part):
    return scaled_values(jax.random.fold_in(key, 15), 1, D, D, 10.0)[0]


def draw_w_in_momentum(key, part):
    return scaled_values(jax.random.fold_in(key, 12), EXPERTS, D, FF, 3.0)


def draw_w_out_momentum(key, part):
    return scaled_values(jax.random.fold_in(key, 13), EXPERTS, D, FF, 3.0)


def levels(stream_key, shape, shards, smallest, largest):
    level, own = 1.0, jax.random.fold_in(stream_key, 6)
    for position, blocks in shards:
        heights = jnp.exp(jax.random.uniform(jax.random.fold_in(own, position), (blocks,), jnp.float32, smallest / len(shards), largest / len(shards)))
        level = level * jnp.repeat(heights, shape[position] // blocks).reshape([-1 if axis == position else 1 for axis in range(len(shape))])
    return level


def assign_block(key, own, number, rows, amount, top, limit, slope):
    order = jax.random.permutation(key, amount)
    crowded, ordinary = portions_of(amount, rows * top, limit, slope, True), portions_of(amount, rows * top, limit, slope, False)
    places = jnp.arange(amount)

    def named(tallies, turn):
        used = int((tallies > 0).sum())
        fixed = max(1, used // 4)
        moved = fixed + (places - fixed + turn * (used - fixed)) % max(1, amount - fixed)
        return jnp.zeros((amount,), jnp.int32).at[order[jnp.where(places < fixed, places, moved)]].set(jnp.asarray(tallies, jnp.int32))

    tallies = jnp.where(number % 4 == 0, named(crowded, number // 4), named(ordinary, number - number // 4 - 1))
    mixed = jax.random.permutation(jax.random.fold_in(own, 3), amount)
    donor, receiver = mixed[0:amount // 2 * 2:2], mixed[1:amount // 2 * 2:2]
    room = jnp.minimum(tallies[donor] - 1, limit - tallies[receiver]) // 2
    room = jnp.where((donor == order[0]) | (receiver == order[0]) | (tallies[receiver] == 0), 0, jnp.maximum(room, 0))
    moved = jax.random.randint(jax.random.fold_in(own, 4), (amount // 2,), 0, 1 << 20) % (room + 1)
    tallies = tallies.at[donor].add(-moved).at[receiver].add(moved)
    items = jnp.searchsorted(jnp.cumsum(tallies), jnp.arange(rows * top), side="right").astype(jnp.int32)
    grid = items.reshape(top, rows).T
    grid = grid[jax.random.permutation(jax.random.fold_in(own, 1), rows)]
    turn = jax.random.randint(jax.random.fold_in(own, 2), (rows, 1), 0, top)
    return jnp.take_along_axis(grid, (jnp.arange(top)[None, :] + turn) % top, axis=1)


def portions_of(count, total, bound, skew, full):
    loads = [(1 << 20) // math.isqrt(grade ** skew) + 1 for grade in range(1, count + 1)]
    largest = bound if full else min(bound, max(-(-total // count), total * loads[0] // sum(loads)))
    least = 1 if total - largest >= count - 1 else 0
    holding, rest = [largest] + [least] * (count - 1), total - largest - least * (count - 1)
    while rest > 0:
        candidates = [i for i in range(1, count) if holding[i] < largest] or [i for i in range(1, count) if holding[i] < bound]
        whole, remaining = sum([loads[i] for i in candidates]), rest
        for i in candidates:
            addition = min(bound - holding[i], max(1, remaining * loads[i] // whole), rest)
            holding[i] = holding[i] + addition
            rest = rest - addition
    return np.array(holding)


def noise(own_key, dims, scale, bound, cuts=(), kind=jnp.bfloat16):
    drawn = jax.random.normal(own_key, dims, jnp.float32) * scale
    if len(cuts) > 0:
        drawn = levels(own_key, dims, cuts, -0.22, 0.18) * drawn
    return jnp.clip(drawn, min=-bound, max=bound).astype(kind)


def setup_inputs(seed: int = 0) -> dict:
    splits = jax.random.split(jax.random.key(seed), 18)
    tokens = noise(splits[0], (TOKENS, D), 1.0, 6.0, ((0, 32),))
    cotangent = noise(splits[1], (TOKENS, D), 1.0, 6.0, ((0, 32),))
    routes_keys = jax.random.split(jax.random.fold_in(splits[2], 1), TOKENS // TOK_DEV)
    routes_turns = jax.random.permutation(jax.random.fold_in(splits[2], 3), TOKENS // TOK_DEV)
    routes = jax.vmap(lambda own, number: assign_block(jax.random.fold_in(splits[2], 2), own, number, TOK_DEV, EXPERTS, 2, 2 * CAPACITY, 2))(routes_keys, routes_turns).reshape((TOKENS, 2))
    priority = jax.vmap(lambda own: jax.random.permutation(own, TOK_DEV))(jax.random.split(splits[3], (N_DP * N_EXPERT))).reshape((N_DP * N_EXPERT, TOK_DEV)).astype(jnp.int32)
    ln_gains = jnp.clip(1.0 + 0.1 * jax.random.normal(splits[4], (2, D), jnp.float32), 0.5, 1.5)
    ln_biases = noise(splits[5], (2, D), 0.3, 2.0, (), jnp.float32)
    qkv_weight = noise(splits[6], (D, 3 * D), D ** -0.5, 0.21875, ((0, 8),))
    out_weight = noise(splits[7], (D, D), (D // 32) ** -0.5, 1.25, ((0, 8),))
    router = noise(splits[8], (D, EXPERTS), D ** -0.5, 0.21875, (), jnp.float32)
    w_in = noise(splits[9], (EXPERTS, D, FF), D ** -0.5, 0.21875, ((0, 8),))
    w_out = noise(splits[10], (EXPERTS, D, FF), (FF // 2) ** -0.5, 0.21875, ((0, 8),))
    norm_momentum = noise(splits[11], (4, D), 20.0, 128.0, (), jnp.float32)
    router_momentum = draw_router_momentum(jax.random.fold_in(splits[17], 71), 0)
    qkv_momentum = draw_qkv_momentum(jax.random.fold_in(splits[17], 71), 0)
    out_momentum = draw_out_momentum(jax.random.fold_in(splits[17], 71), 0)
    w_in_momentum = draw_w_in_momentum(jax.random.fold_in(splits[17], 71), 0)
    w_out_momentum = draw_w_out_momentum(jax.random.fold_in(splits[17], 71), 0)
    return dict(tokens=tokens, cotangent=cotangent, routes=routes, priority=priority, ln_gains=ln_gains, ln_biases=ln_biases, qkv_weight=qkv_weight, out_weight=out_weight, router=router, w_in=w_in, w_out=w_out, norm_momentum=norm_momentum, router_momentum=router_momentum, qkv_momentum=qkv_momentum, out_momentum=out_momentum, w_in_momentum=w_in_momentum, w_out_momentum=w_out_momentum)


quintic_one = 3.4445
quintic_two = -4.775
quintic_three = 2.0315
decay_rate = 0.9
matrix_rate = 0.2
norm_rate = 0.004
norm_eps = 1e-06
frob_eps = 1e-07
highest = lax.Precision.HIGHEST
contract_last = (((1,), (1,)), ((), ()))
contract_first = (((0,), (0,)), ((), ()))

def rounded(values):
    return lax.optimization_barrier(values.astype(jnp.bfloat16)).astype(jnp.float32)

def gelu_slope(preact):
    return 0.5 * (1.0 + lax.erf(preact * 0.7071067811865476)) + preact * jnp.exp(-0.5 * preact * preact) * 0.3989422804014327

def layer_stats(token_rows, gain, bias):
    centre = token_rows - lax.optimization_barrier(jnp.mean(token_rows, axis=-1, keepdims=True))
    inverse = lax.rsqrt(lax.optimization_barrier(jnp.mean(centre * centre, axis=-1, keepdims=True)) + norm_eps)
    scaled = centre * inverse
    return (scaled, inverse, scaled * gain + bias)

def slot_index(choice_ids, order_rows, experts, capacity):
    token_count = choice_ids.shape[0]
    ranked = jnp.take(choice_ids, order_rows, axis=0)
    entries = jnp.concatenate([ranked[:, 0], ranked[:, 1]])
    onehot = (entries[:, None] == jnp.arange(experts, dtype=jnp.int32)[None, :]).astype(jnp.int32)
    before = jnp.cumsum(onehot, axis=0) - onehot
    ranked_slots = lax.optimization_barrier(jnp.sum(before * onehot, axis=1)).reshape(2, token_count).T
    slot_values = jnp.zeros((token_count, 2), jnp.int32).at[order_rows].set(ranked_slots)
    return jnp.where(slot_values < capacity, choice_ids * capacity + slot_values, experts * capacity).astype(jnp.int32)

def gates_of(logits, choice_ids):
    chosen = jnp.take_along_axis(logits, choice_ids, axis=1)
    first_gate = jax.nn.sigmoid(chosen[:, 0] - chosen[:, 1])
    return jnp.stack([first_gate, 1.0 - first_gate], axis=1)

def input_grad(base_grad, normed_grad, scaled, inverse, gain):
    lifted = normed_grad * gain
    centred = lifted - lax.optimization_barrier(jnp.mean(lifted, axis=-1, keepdims=True)) - scaled * lax.optimization_barrier(jnp.mean(lifted * scaled, axis=-1, keepdims=True))
    return base_grad + inverse * centred

def ortho_wide(matrix):
    iterate = (matrix / (jnp.sqrt(jnp.sum(matrix * matrix)) + frob_eps)).astype(jnp.bfloat16)
    for iteration in range(NS_STEPS):
        gram_matrix = lax.dot_general(iterate, iterate, contract_last, preferred_element_type=jnp.float32).astype(jnp.bfloat16)
        mixer_matrix = (quintic_two * gram_matrix.astype(jnp.float32) + quintic_three * jnp.dot(gram_matrix, gram_matrix, preferred_element_type=jnp.float32)).astype(jnp.bfloat16)
        iterate = (quintic_one * iterate.astype(jnp.float32) + jnp.dot(mixer_matrix, iterate, preferred_element_type=jnp.float32)).astype(jnp.bfloat16)
    return iterate

def ortho_tall(matrix):
    iterate = (matrix / (jnp.sqrt(jnp.sum(matrix * matrix)) + frob_eps)).astype(jnp.bfloat16)
    for iteration in range(NS_STEPS):
        gram_matrix = lax.dot_general(iterate, iterate, contract_first, preferred_element_type=jnp.float32).astype(jnp.bfloat16)
        mixer_matrix = (quintic_two * gram_matrix.astype(jnp.float32) + quintic_three * jnp.dot(gram_matrix, gram_matrix, preferred_element_type=jnp.float32)).astype(jnp.bfloat16)
        iterate = (quintic_one * iterate.astype(jnp.float32) + jnp.dot(iterate, mixer_matrix, preferred_element_type=jnp.float32)).astype(jnp.bfloat16)
    return iterate

def split_heads(qkv_rows):
    shaped = qkv_rows.astype(jnp.float32).reshape(-1, SEQ, 3, HEADS, D // HEADS)
    return (shaped[:, :, 0], shaped[:, :, 1], shaped[:, :, 2])

def attend_forward(qkv_rows):
    query_rows, key_rows, value_rows = split_heads(qkv_rows)
    score_scale = 1.0 / math.sqrt(D // HEADS)
    scores = jnp.einsum('ishd,ithd->ihst', query_rows, key_rows) * score_scale
    log_total = jnp.log(lax.optimization_barrier(jnp.sum(jnp.exp(scores), axis=3, keepdims=True)))
    attn_probs = rounded(jnp.exp(scores - log_total))
    mixed_rows = jnp.einsum('ihst,ithd->ishd', attn_probs, value_rows).astype(jnp.bfloat16).reshape(-1, D)
    return (mixed_rows, log_total)

def attend_backward(qkv_rows, log_total, mixed_grad):
    query_rows, key_rows, value_rows = split_heads(qkv_rows)
    score_scale = 1.0 / math.sqrt(D // HEADS)
    scores = jnp.einsum('ishd,ithd->ihst', query_rows, key_rows) * score_scale
    attn_probs = rounded(jnp.exp(scores - log_total))
    grad_heads = mixed_grad.astype(jnp.float32).reshape(-1, SEQ, HEADS, D // HEADS)
    value_grad = jnp.einsum('ihst,ishd->ithd', attn_probs, grad_heads)
    prob_grad = jnp.einsum('ishd,ithd->ihst', grad_heads, value_rows)
    row_delta = lax.optimization_barrier(jnp.sum(attn_probs * prob_grad, axis=3, keepdims=True))
    score_grad = rounded(attn_probs * (prob_grad - row_delta) * score_scale)
    query_grad = jnp.einsum('ihst,ithd->ishd', score_grad, key_rows)
    key_grad = jnp.einsum('ihst,ishd->ithd', score_grad, query_rows)
    return jnp.stack([query_grad, key_grad, value_grad], axis=2).astype(jnp.bfloat16).reshape(-1, 3 * D)

def reference(tokens, cotangent, routes, priority, ln_gains, ln_biases, qkv_weight, out_weight, router, w_in, w_out, norm_momentum, router_momentum, qkv_momentum, out_momentum, w_in_momentum, w_out_momentum):
    members = EXPERTS
    groups = TOKENS // (TOK_DEV * EXPERTS)
    slots_all = EXPERTS * CAPACITY
    first_weight = w_in.astype(jnp.float32)
    second_weight = w_out.astype(jnp.float32)

    def dispatch_part(middle_rows, choice_ids, order_rows):
        slot_flat = slot_index(choice_ids, order_rows, EXPERTS, CAPACITY)
        scaled, inverse, normed = layer_stats(middle_rows, ln_gains[1], ln_biases[1])
        logits = jnp.dot(normed, router, precision=highest)
        gate_values = gates_of(logits, choice_ids)
        dispatch = jnp.zeros((slots_all, D), jnp.bfloat16).at[slot_flat.reshape(-1)].set(jnp.repeat(normed.astype(jnp.bfloat16), 2, axis=0), mode='drop')
        return (slot_flat, scaled, inverse, normed, gate_values, dispatch)

    def to_experts(buffers):
        return buffers.reshape(members, EXPERTS, CAPACITY, -1).transpose(1, 0, 2, 3).reshape(EXPERTS, members * CAPACITY, -1)

    def from_experts(expert_rows):
        return expert_rows.reshape(EXPERTS, members, CAPACITY, -1).transpose(1, 0, 2, 3).reshape(members, slots_all, -1)

    def combine_part(middle_rows, cot_rows, choice_ids, slot_flat, gate_values, back_rows):
        picked = jnp.take(back_rows, slot_flat.reshape(-1), axis=0, mode='fill', fill_value=0).reshape(TOK_DEV, 2, D).astype(jnp.float32)
        cot_float = cot_rows.astype(jnp.float32)
        block_rows = middle_rows + lax.optimization_barrier(jnp.sum(gate_values[:, :, None] * picked, axis=1))
        gate_grad = lax.optimization_barrier(jnp.sum(picked * cot_float[:, None, :], axis=2))
        logit_step = gate_values[:, 0] * gate_values[:, 1] * (gate_grad[:, 0] - gate_grad[:, 1])
        columns = jnp.arange(EXPERTS, dtype=jnp.int32)[None, :]
        logit_grad = ((choice_ids[:, 0:1] == columns).astype(jnp.float32) - (choice_ids[:, 1:2] == columns).astype(jnp.float32)) * logit_step[:, None]
        weighted = (gate_values[:, :, None] * cot_float[:, None, :]).reshape(-1, D)
        sent_grad = jnp.zeros((slots_all, D), jnp.float32).at[slot_flat.reshape(-1)].set(weighted, mode='drop').astype(jnp.bfloat16)
        return (block_rows, logit_grad, sent_grad)

    def finish_part(cot_rows, slot_flat, scaled, inverse, normed, logit_grad, back_grad):
        gathered = jnp.take(back_grad, slot_flat.reshape(-1), axis=0, mode='fill', fill_value=0).reshape(TOK_DEV, 2, D).astype(jnp.float32)
        normed_grad = lax.optimization_barrier(jnp.sum(gathered, axis=1)) + lax.dot_general(logit_grad, router, contract_last, precision=highest)
        router_local = lax.dot_general(normed, logit_grad, contract_first, precision=highest)
        norm_local = jnp.stack([lax.optimization_barrier(jnp.sum(normed_grad * scaled, axis=0)), lax.optimization_barrier(jnp.sum(normed_grad, axis=0))])
        middle_grad = input_grad(cot_rows.astype(jnp.float32), normed_grad, scaled, inverse, ln_gains[1])
        return (middle_grad, router_local, norm_local)

    def group_step(running, inputs):
        token_rows, cot_rows, choice_ids, order_rows = inputs
        flat_tokens = token_rows.reshape(members * TOK_DEV, D).astype(jnp.float32)
        scaled_one, inverse_one, normed_one = layer_stats(flat_tokens, ln_gains[0], ln_biases[0])
        attn_in = normed_one.astype(jnp.bfloat16)
        qkv_rows = jnp.dot(attn_in, qkv_weight, preferred_element_type=jnp.float32).astype(jnp.bfloat16)
        mixed_rows, log_total = attend_forward(qkv_rows)
        middle_rows = flat_tokens + jnp.dot(mixed_rows, out_weight, preferred_element_type=jnp.float32)
        member_rows = middle_rows.reshape(members, TOK_DEV, D)
        slot_flat, scaled, inverse, normed, gate_values, dispatch = jax.vmap(dispatch_part)(member_rows, choice_ids, order_rows)
        expert_rows = to_experts(dispatch)
        preact = jnp.einsum('erd,edf->erf', expert_rows.astype(jnp.float32), first_weight)
        active = jax.nn.gelu(preact, approximate=False).astype(jnp.bfloat16)
        result = jnp.einsum('erf,edf->erd', active.astype(jnp.float32), second_weight).astype(jnp.bfloat16)
        block_rows, logit_grad, sent_grad = jax.vmap(combine_part)(member_rows, cot_rows, choice_ids, slot_flat, gate_values, from_experts(result))
        grad_rows = to_experts(sent_grad)
        act_grad = jnp.einsum('erd,edf->erf', grad_rows.astype(jnp.float32), second_weight)
        pre_grad = (act_grad * gelu_slope(preact)).astype(jnp.bfloat16)
        row_grad = jnp.einsum('erf,edf->erd', pre_grad.astype(jnp.float32), first_weight).astype(jnp.bfloat16)
        first_grad = jnp.einsum('erd,erf->edf', expert_rows.astype(jnp.float32), pre_grad.astype(jnp.float32))
        second_grad = jnp.einsum('erd,erf->edf', grad_rows.astype(jnp.float32), active.astype(jnp.float32))
        middle_grad, router_local, norm_local = jax.vmap(finish_part)(cot_rows, slot_flat, scaled, inverse, normed, logit_grad, from_experts(row_grad))
        middle_flat = middle_grad.reshape(members * TOK_DEV, D)
        middle_rounded = middle_flat.astype(jnp.bfloat16)
        mixed_grad = lax.dot_general(middle_rounded, out_weight, contract_last, preferred_element_type=jnp.float32).astype(jnp.bfloat16)
        qkv_grad = attend_backward(qkv_rows, log_total, mixed_grad)
        attn_in_grad = lax.dot_general(qkv_grad, qkv_weight, contract_last, preferred_element_type=jnp.float32)
        tokens_grad = input_grad(middle_flat, attn_in_grad, scaled_one, inverse_one, ln_gains[0])
        qkv_term = lax.dot_general(attn_in, qkv_grad, contract_first, preferred_element_type=jnp.float32)
        out_term = lax.dot_general(mixed_rows, middle_rounded, contract_first, preferred_element_type=jnp.float32)
        second_norm = lax.optimization_barrier(jnp.sum(norm_local, axis=0))
        norm_rows = jnp.stack([lax.optimization_barrier(jnp.sum(attn_in_grad * scaled_one, axis=0)), second_norm[0], lax.optimization_barrier(jnp.sum(attn_in_grad, axis=0)), second_norm[1]])
        total_first, total_second, total_router, total_norm, total_qkv, total_out = running
        running = (total_first + first_grad, total_second + second_grad, total_router + lax.optimization_barrier(jnp.sum(router_local, axis=0)), total_norm + norm_rows, total_qkv + qkv_term, total_out + out_term)
        return (running, (block_rows.reshape(members * TOK_DEV, D), tokens_grad))
    initial = (jnp.zeros((EXPERTS, D, FF), jnp.float32), jnp.zeros((EXPERTS, D, FF), jnp.float32), jnp.zeros((D, EXPERTS), jnp.float32), jnp.zeros((4, D), jnp.float32), jnp.zeros((D, 3 * D), jnp.float32), jnp.zeros((D, D), jnp.float32))
    inputs = (tokens.reshape(groups, members, TOK_DEV, D), cotangent.reshape(groups, members, TOK_DEV, D), routes.reshape(groups, members, TOK_DEV, 2), priority.reshape(groups, members, TOK_DEV))
    totals, stacked = lax.scan(group_step, initial, inputs)
    grad_w_in, grad_w_out, grad_router, grad_norm, grad_qkv, grad_out = totals
    block_out = stacked[0].reshape(TOKENS, D)
    grad_tokens = stacked[1].reshape(TOKENS, D)
    new_norm_momentum = decay_rate * norm_momentum + grad_norm
    new_norm = jnp.concatenate([ln_gains, ln_biases], axis=0) - norm_rate * new_norm_momentum
    new_router_momentum = decay_rate * router_momentum + grad_router
    new_router = router - matrix_rate * ortho_tall(new_router_momentum).astype(jnp.float32)
    new_qkv_momentum = decay_rate * qkv_momentum + grad_qkv
    new_qkv = qkv_weight.astype(jnp.float32) - matrix_rate * math.sqrt(3.0) * ortho_wide(new_qkv_momentum).astype(jnp.float32)
    new_out_momentum = decay_rate * out_momentum + grad_out
    new_out = out_weight.astype(jnp.float32) - matrix_rate * ortho_wide(new_out_momentum).astype(jnp.float32)
    widen_factor = math.sqrt(max(1.0, FF / D))

    def expert_update(members_tuple):
        first_weight_e, first_moment, first_grad, second_weight_e, second_moment, second_grad = members_tuple
        first_new_moment = decay_rate * first_moment + first_grad
        second_new_moment = decay_rate * second_moment + second_grad
        first_new = first_weight_e.astype(jnp.float32) - matrix_rate * widen_factor * ortho_wide(first_new_moment).astype(jnp.float32)
        second_new = second_weight_e.astype(jnp.float32) - matrix_rate * ortho_wide(second_new_moment).astype(jnp.float32)
        return (first_new, first_new_moment, second_new, second_new_moment)
    new_w_in, new_w_in_momentum, new_w_out, new_w_out_momentum = lax.map(expert_update, (w_in, w_in_momentum, grad_w_in, w_out, w_out_momentum, grad_w_out))
    return (block_out, grad_tokens, grad_norm, grad_router, grad_qkv, grad_out, grad_w_in, grad_w_out, new_norm, new_norm_momentum, new_router, new_router_momentum, new_qkv, new_qkv_momentum, new_out, new_out_momentum, new_w_in, new_w_in_momentum, new_w_out, new_w_out_momentum)
```

```python
import functools
import math

import jax
import jax.numpy as jnp
from jax import lax
from jax.experimental import pallas as pl
from jax.experimental.pallas import tpu as pltpu
from jax.sharding import PartitionSpec as P

HEADS = 12
NS_STEPS = 5
SEQ = 197


quintic_one = 3.4445
quintic_two = -4.775
quintic_three = 2.0315
decay_rate = 0.9
matrix_rate = 0.2
norm_rate = 0.004
norm_eps = 1e-06
frob_eps = 1e-07
highest = lax.Precision.HIGHEST
contract_last = (((1,), (1,)), ((), ()))
contract_first = (((0,), (0,)), ((), ()))


def gelu_slope(preact):
    return (
        0.5 * (1.0 + lax.erf(preact * 0.7071067811865476))
        + preact * jnp.exp(-0.5 * preact * preact) * 0.3989422804014327
    )


def layer_stats(token_rows, gain, bias):
    centre = token_rows - jnp.mean(token_rows, axis=-1, keepdims=True)
    inverse = lax.rsqrt(jnp.mean(centre * centre, axis=-1, keepdims=True) + norm_eps)
    scaled = centre * inverse
    return (scaled, inverse, scaled * gain + bias)


def slot_index(choice_ids, order_rows, experts, capacity):
    token_count = choice_ids.shape[0]
    ranks = jnp.arange(token_count, dtype=jnp.int32)
    turn = jnp.sum(
        jnp.where(order_rows[:, None] == ranks[None, :], ranks[:, None], 0), axis=0, dtype=jnp.int32
    )
    earlier = (turn[None, :] < turn[:, None]).astype(jnp.bfloat16)
    columns = jnp.arange(experts, dtype=jnp.int32)[None, :]
    first = (choice_ids[:, 0:1] == columns).astype(jnp.bfloat16)
    second = (choice_ids[:, 1:2] == columns).astype(jnp.bfloat16)
    counts = jnp.dot(
        earlier, jnp.concatenate([first, second], axis=1), preferred_element_type=jnp.float32
    )
    first_float, second_float = first.astype(jnp.float32), second.astype(jnp.float32)
    first_slot = jnp.sum(counts[:, :experts] * first_float, axis=1)
    second_slot = jnp.sum(
        (counts[:, experts:] + jnp.sum(first_float, axis=0, keepdims=True)) * second_float, axis=1
    )
    slot_values = jnp.stack([first_slot, second_slot], axis=1).astype(jnp.int32)
    return jnp.where(
        slot_values < capacity, choice_ids * capacity + slot_values, experts * capacity
    )


def gates_of(logits, choice_ids):
    columns = jnp.arange(logits.shape[1], dtype=jnp.int32)[None, :]
    first_logit = jnp.sum(jnp.where(choice_ids[:, 0:1] == columns, logits, 0.0), axis=1)
    second_logit = jnp.sum(jnp.where(choice_ids[:, 1:2] == columns, logits, 0.0), axis=1)
    first_gate = jax.nn.sigmoid(first_logit - second_logit)
    return jnp.stack([first_gate, 1.0 - first_gate], axis=1)


def input_grad(base_grad, normed_grad, scaled, inverse, gain):
    lifted = normed_grad * gain
    centred = (
        lifted
        - jnp.mean(lifted, axis=-1, keepdims=True)
        - scaled * jnp.mean(lifted * scaled, axis=-1, keepdims=True)
    )
    return base_grad + inverse * centred


def ortho_tall(matrix):
    iterate = (matrix / (jnp.sqrt(jnp.sum(matrix * matrix)) + frob_eps)).astype(jnp.bfloat16)
    for iteration in range(NS_STEPS):
        gram_matrix = lax.dot_general(
            iterate, iterate, contract_first, preferred_element_type=jnp.float32
        ).astype(jnp.bfloat16)
        mixer_matrix = (
            quintic_two * gram_matrix.astype(jnp.float32)
            + quintic_three * jnp.dot(gram_matrix, gram_matrix, preferred_element_type=jnp.float32)
        ).astype(jnp.bfloat16)
        iterate = (
            quintic_one * iterate.astype(jnp.float32)
            + jnp.dot(iterate, mixer_matrix, preferred_element_type=jnp.float32)
        ).astype(jnp.bfloat16)
    return iterate


def ortho_kernel(block, tile, row_count, base_ref, moment_ref, out_ref, iterate, gram, mixer):
    rows, cols = moment_ref.shape
    tiles = cols // tile

    def squares(index, total):
        part = moment_ref[:, pl.ds(pl.multiple_of(index * tile, tile), tile)].astype(jnp.float32)
        return total + jnp.sum(part * part, axis=0, keepdims=True)

    total = lax.fori_loop(0, tiles, squares, jnp.zeros((1, tile), jnp.float32))
    norm = jnp.sqrt(jnp.sum(total)) + frob_eps

    @pl.loop(0, tiles)
    def _(index):
        span = pl.ds(pl.multiple_of(index * tile, tile), tile)
        iterate[:, span] = (moment_ref[:, span].astype(jnp.float32) / norm).astype(jnp.bfloat16)

    def mirror(target, part, index):
        target[index * block : (index + 1) * block, 0 : (index + 1) * block] = part
        for other in range(index):
            target[other * block : (other + 1) * block, index * block : (index + 1) * block] = part[
                :, other * block : (other + 1) * block
            ].T

    def make_gram():
        for index in range(rows // block):
            mirror(
                gram,
                lax.dot_general(
                    iterate[index * block : (index + 1) * block, :],
                    iterate[0 : (index + 1) * block, :],
                    contract_last,
                    preferred_element_type=jnp.float32,
                ).astype(jnp.bfloat16),
                index,
            )

    def mix(gram_rows, gram_part, gram_columns):
        return (
            quintic_two * gram_part.astype(jnp.float32)
            + quintic_three * jnp.dot(gram_rows, gram_columns, preferred_element_type=jnp.float32)
        ).astype(jnp.bfloat16)

    def apply(mixer_rows, part, columns):
        return (
            quintic_one * part.astype(jnp.float32)
            + jnp.dot(mixer_rows, columns, preferred_element_type=jnp.float32)
        ).astype(jnp.bfloat16)

    @pl.loop(0, NS_STEPS - 1)
    def _(step):
        make_gram()
        for index in range(rows // block):
            span = pl.ds(index * block, block)
            reach = (index + 1) * block
            mirror(mixer, mix(gram[span, :], gram[span, 0:reach], gram[:, 0:reach]), index)

        @pl.loop(0, tiles)
        def _(index):
            span = pl.ds(pl.multiple_of(index * tile, tile), tile)
            columns = iterate[:, span]
            iterate[:, span] = apply(mixer[...], columns, columns)

    make_gram()
    if row_count == rows:
        own = pl.ds(0, rows)
    else:
        own = pl.ds(pl.multiple_of(base_ref[0], row_count), row_count)
    mixer[0:row_count, :] = mix(gram[own, :], gram[own, :], gram[...])

    @pl.loop(0, tiles)
    def _(index):
        span = pl.ds(pl.multiple_of(index * tile, tile), tile)
        out_ref[:, span] = apply(mixer[0:row_count, :], iterate[own, span], iterate[:, span])


def ortho_rows(moment, row_start, row_count):
    rows, cols = moment.shape
    block = next(size for size in (256, 128, rows) if rows % size == 0)
    tile = next(size for size in (768, 512, 256, 128, cols) if cols % size == 0)
    whole = row_count % 16 != 0
    kept = rows if whole else row_count
    flops = 2 * NS_STEPS * rows * rows * (2 * cols + rows)
    rows_out = pl.pallas_call(
        functools.partial(ortho_kernel, block, tile, kept),
        out_shape=jax.ShapeDtypeStruct((kept, cols), jnp.bfloat16),
        in_specs=[
            pl.BlockSpec(memory_space=pltpu.SMEM),
            pl.BlockSpec(memory_space=pltpu.VMEM),
        ],
        out_specs=pl.BlockSpec(memory_space=pltpu.VMEM),
        scratch_shapes=[
            pltpu.VMEM((rows, cols), jnp.bfloat16),
            pltpu.VMEM((rows, rows), jnp.bfloat16),
            pltpu.VMEM((rows, rows), jnp.bfloat16),
        ],
        compiler_params=pltpu.CompilerParams(vmem_limit_bytes=40 << 20),
        cost_estimate=pl.CostEstimate(
            flops=flops, bytes_accessed=4 * rows * cols, transcendentals=0
        ),
    )(jnp.reshape(row_start, (1,)).astype(jnp.int32), moment)
    if whole:
        rows_out = lax.dynamic_slice_in_dim(rows_out, row_start, row_count, 0)
    return rows_out


def split_heads(qkv_rows, image_count, head_width):
    shaped = qkv_rows.reshape(image_count, SEQ, 3, HEADS, head_width)
    return (shaped[:, :, 0], shaped[:, :, 1], shaped[:, :, 2])


def attention_scores(query_rows, key_rows, score_scale):
    return (
        jnp.einsum("ishd,ithd->ihst", query_rows, key_rows, preferred_element_type=jnp.float32)
        * score_scale
    )


def body(
    tokens,
    cotangent,
    routes,
    priority,
    ln_gains,
    ln_biases,
    qkv_weight,
    out_weight,
    router,
    w_in,
    w_out,
    norm_momentum,
    router_momentum,
    qkv_momentum,
    out_momentum,
    w_in_momentum,
    w_out_momentum,
):
    token_count, model_width = tokens.shape
    experts = router.shape[1]
    hidden_units = w_in.shape[2]
    capacity = (token_count + experts - 1) // experts
    slots_all = experts * capacity
    dp_share = model_width // lax.axis_size("dp")
    image_count = token_count // SEQ
    head_width = model_width // HEADS
    score_scale = 1.0 / math.sqrt(head_width)
    first_weight = w_in[0]
    second_weight = w_out[0]
    cot_float = cotangent.astype(jnp.float32)
    full_qkv, full_out = (
        lax.all_gather(qkv_weight, "expert", axis=0, tiled=True),
        lax.all_gather(out_weight, "expert", axis=0, tiled=True),
    )
    dp_size = lax.axis_size("dp")
    dp_index = lax.axis_index("dp")
    takes_second = dp_index % 2
    first_slice = w_in_momentum[0].astype(jnp.bfloat16)
    second_slice = w_out_momentum[0].astype(jnp.bfloat16)
    moment_parts = []
    for shift in range(dp_size):
        wanted = jnp.where((dp_index + shift) % 2 == 1, second_slice, first_slice)
        if shift:
            wanted = lax.ppermute(
                wanted, "dp", [(i, (i + shift) % dp_size) for i in range(dp_size)]
            )
        moment_parts.append(wanted)
    token_float = tokens.astype(jnp.float32)
    scaled_one, inverse_one, normed_one = layer_stats(token_float, ln_gains[0], ln_biases[0])
    attn_in = normed_one.astype(jnp.bfloat16)
    qkv_rows = jnp.dot(attn_in, full_qkv, preferred_element_type=jnp.float32).astype(jnp.bfloat16)
    query_rows, key_rows, value_rows = split_heads(qkv_rows, image_count, head_width)
    scores = attention_scores(query_rows, key_rows, score_scale)
    log_total = jnp.log(jnp.sum(jnp.exp(scores), axis=3, keepdims=True))
    attn_probs = jnp.exp(scores - log_total).astype(jnp.bfloat16)
    mixed_rows = (
        jnp.einsum("ihst,ithd->ishd", attn_probs, value_rows, preferred_element_type=jnp.float32)
        .astype(jnp.bfloat16)
        .reshape(token_count, model_width)
    )
    middle_rows = token_float + jnp.dot(mixed_rows, full_out, preferred_element_type=jnp.float32)
    slot_flat = slot_index(routes, priority[0], experts, capacity)
    scaled, inverse, normed = layer_stats(middle_rows, ln_gains[1], ln_biases[1])
    logits = jnp.dot(normed, router, precision=highest)
    gate_values = gates_of(logits, routes)
    position = jnp.arange(slots_all, dtype=jnp.int32)[:, None]
    pick_first = (slot_flat[:, 0][None, :] == position).astype(jnp.float32)
    pick_second = (slot_flat[:, 1][None, :] == position).astype(jnp.float32)
    placing = (pick_first + pick_second).astype(jnp.bfloat16)
    lean_first, lean_second = (pick_first.astype(jnp.bfloat16), pick_second.astype(jnp.bfloat16))
    gated = jnp.concatenate(
        [
            (gate_values[:, 0:1] * cot_float).astype(jnp.bfloat16),
            (gate_values[:, 1:2] * cot_float).astype(jnp.bfloat16),
        ],
        axis=0,
    )
    dispatch = jnp.dot(
        placing, normed.astype(jnp.bfloat16), preferred_element_type=jnp.float32
    ).astype(jnp.bfloat16)
    sent_grad = jnp.dot(
        jnp.concatenate([lean_first, lean_second], axis=1),
        gated,
        preferred_element_type=jnp.float32,
    ).astype(jnp.bfloat16)

    def to_blocks(rows_one, rows_two):
        return jnp.concatenate(
            [
                rows_one.reshape(experts, capacity, model_width),
                rows_two.reshape(experts, capacity, model_width),
            ],
            axis=2,
        )

    arrived = lax.all_to_all(
        to_blocks(dispatch, sent_grad), "expert", split_axis=0, concat_axis=0, tiled=True
    ).reshape(slots_all, 2 * model_width)
    every_pair = lax.all_gather(arrived, "dp", axis=0, tiled=True)
    arrived_rows = arrived[:, :model_width]
    grad_rows = arrived[:, model_width:]
    preact_first = jnp.dot(arrived_rows, first_weight, preferred_element_type=jnp.float32)
    active_first = jax.nn.gelu(preact_first, approximate=False).astype(jnp.bfloat16)
    result = lax.dot_general(
        active_first, second_weight, contract_last, preferred_element_type=jnp.float32
    ).astype(jnp.bfloat16)
    act_grad = jnp.dot(grad_rows, second_weight, preferred_element_type=jnp.float32)
    expert_pre_grad = (act_grad * gelu_slope(preact_first)).astype(jnp.bfloat16)
    row_grad = lax.dot_general(
        expert_pre_grad, first_weight, contract_last, preferred_element_type=jnp.float32
    ).astype(jnp.bfloat16)
    returned = lax.all_to_all(
        to_blocks(result, row_grad), "expert", split_axis=0, concat_axis=0, tiled=True
    ).reshape(slots_all, 2 * model_width)
    back_first = lax.dot_general(
        lean_first, returned, contract_first, preferred_element_type=jnp.float32
    )
    back_second = lax.dot_general(
        lean_second, returned, contract_first, preferred_element_type=jnp.float32
    )
    picked_first, picked_second = (back_first[:, :model_width], back_second[:, :model_width])
    block_out = middle_rows + (
        gate_values[:, 0:1] * picked_first + gate_values[:, 1:2] * picked_second
    )
    grad_gap = jnp.sum(picked_first * cot_float, axis=1) - jnp.sum(picked_second * cot_float, axis=1)
    logit_step = gate_values[:, 0] * gate_values[:, 1] * grad_gap
    columns = jnp.arange(experts, dtype=jnp.int32)[None, :]
    logit_grad = (
        (routes[:, 0:1] == columns).astype(jnp.float32)
        - (routes[:, 1:2] == columns).astype(jnp.float32)
    ) * logit_step[:, None]
    gathered = back_first[:, model_width:] + back_second[:, model_width:]
    normed_grad = gathered + lax.dot_general(
        logit_grad, router, contract_last, precision=highest
    )
    router_local = lax.dot_general(normed, logit_grad, contract_first, precision=highest)
    middle_grad = input_grad(cot_float, normed_grad, scaled, inverse, ln_gains[1])
    middle_rounded = middle_grad.astype(jnp.bfloat16)
    mixed_grad = lax.dot_general(
        middle_rounded, full_out, contract_last, preferred_element_type=jnp.float32
    ).astype(jnp.bfloat16)
    scores_again = attention_scores(query_rows, key_rows, score_scale)
    probs_again = jnp.exp(scores_again - log_total).astype(jnp.bfloat16)
    grad_heads = mixed_grad.reshape(image_count, SEQ, HEADS, head_width)
    value_grad = jnp.einsum(
        "ihst,ishd->ithd", probs_again, grad_heads, preferred_element_type=jnp.float32
    )
    prob_grad = jnp.einsum(
        "ishd,ithd->ihst", grad_heads, value_rows, preferred_element_type=jnp.float32
    )
    prob_float = probs_again.astype(jnp.float32)
    row_delta = jnp.sum(prob_float * prob_grad, axis=3, keepdims=True)
    score_grad = (prob_float * (prob_grad - row_delta) * score_scale).astype(jnp.bfloat16)
    query_grad = jnp.einsum(
        "ihst,ithd->ishd", score_grad, key_rows, preferred_element_type=jnp.float32
    )
    key_grad = jnp.einsum(
        "ihst,ishd->ithd", score_grad, query_rows, preferred_element_type=jnp.float32
    )
    qkv_grad = (
        jnp.stack([query_grad, key_grad, value_grad], axis=2)
        .astype(jnp.bfloat16)
        .reshape(token_count, 3 * model_width)
    )
    attn_in_grad = lax.dot_general(
        qkv_grad, full_qkv, contract_last, preferred_element_type=jnp.float32
    )
    grad_tokens = input_grad(middle_grad, attn_in_grad, scaled_one, inverse_one, ln_gains[0])
    qkv_term = lax.dot_general(
        attn_in, qkv_grad, contract_first, preferred_element_type=jnp.float32
    )
    out_term = lax.dot_general(
        mixed_rows, middle_rounded, contract_first, preferred_element_type=jnp.float32
    )
    attention_share = lax.psum_scatter(
        jnp.concatenate([qkv_term, out_term], axis=1).astype(jnp.bfloat16),
        "expert",
        scatter_dimension=0,
        tiled=True,
    )
    norm_local = jnp.stack(
        [
            jnp.sum(attn_in_grad * scaled_one, axis=0),
            jnp.sum(normed_grad * scaled, axis=0),
            jnp.sum(attn_in_grad, axis=0),
            jnp.sum(normed_grad, axis=0),
        ]
    )
    attention_total = lax.psum(attention_share, "dp").astype(jnp.float32)
    small_parts = lax.all_gather(
        jnp.concatenate([router_local.T, norm_local], axis=0), ("dp", "expert"), axis=0
    )
    small_total = jnp.sum(small_parts, axis=0)
    grad_router = small_total[:experts].T
    grad_norm = small_total[experts:]
    grad_qkv = attention_total[:, : 3 * model_width]
    grad_out = attention_total[:, 3 * model_width :]
    moment_qkv = decay_rate * qkv_momentum + grad_qkv
    moment_out = decay_rate * out_momentum + grad_out
    whole_qkv = lax.all_gather(moment_qkv.astype(jnp.bfloat16), "expert", axis=0, tiled=True)
    whole_out = lax.all_gather(moment_out.astype(jnp.bfloat16), "expert", axis=0, tiled=True)
    row_base = dp_index * dp_share
    every_row = every_pair[:, :model_width]
    every_grad = every_pair[:, model_width:]
    every_preact = jnp.dot(every_row, first_weight, preferred_element_type=jnp.float32)
    every_active = jax.nn.gelu(every_preact, approximate=False).astype(jnp.bfloat16)
    every_act_grad = jnp.dot(every_grad, second_weight, preferred_element_type=jnp.float32)
    every_pre_grad = (every_act_grad * gelu_slope(every_preact)).astype(jnp.bfloat16)
    own_left, other_left = (
        jnp.where(takes_second == 1, every_grad, every_row),
        jnp.where(takes_second == 1, every_row, every_grad),
    )
    own_right, other_right = (
        jnp.where(takes_second == 1, every_active, every_pre_grad),
        jnp.where(takes_second == 1, every_pre_grad, every_active),
    )
    whole_own = lax.dot_general(
        own_left, own_right, contract_first, preferred_element_type=jnp.float32
    )
    part_own = lax.dynamic_slice_in_dim(whole_own, row_base, dp_share, 0)
    part_other = lax.dot_general(
        lax.dynamic_slice_in_dim(other_left, row_base, dp_share, 1),
        other_right,
        contract_first,
        preferred_element_type=jnp.float32,
    )
    grad_first = jnp.where(takes_second == 1, part_other, part_own)
    grad_second = jnp.where(takes_second == 1, part_own, part_other)
    moment_first = decay_rate * w_in_momentum[0] + grad_first
    moment_second = decay_rate * w_out_momentum[0] + grad_second
    shifted = jnp.concatenate(moment_parts[:1] + moment_parts[:0:-1], axis=0)
    every_moment = jnp.roll(shifted, row_base, axis=0)
    pair_share = 2 * dp_share
    iter_pair = ortho_rows(
        decay_rate * every_moment.astype(jnp.float32) + whole_own,
        (dp_index // 2) * pair_share,
        pair_share,
    )
    iter_low, iter_high = iter_pair[:dp_share], iter_pair[dp_share:]
    iter_own = jnp.where(takes_second == 1, iter_high, iter_low)
    iter_other = lax.ppermute(
        jnp.where(takes_second == 1, iter_low, iter_high),
        "dp",
        [(i, i ^ 1) for i in range(dp_size)],
    )
    iter_first = jnp.where(takes_second == 1, iter_other, iter_own)
    iter_second = jnp.where(takes_second == 1, iter_own, iter_other)
    expert_share = qkv_weight.shape[0]
    expert_base = lax.axis_index("expert") * expert_share
    iter_out = ortho_rows(whole_out, expert_base, expert_share)
    iter_qkv = ortho_rows(whole_qkv, expert_base, expert_share)
    new_norm_momentum = decay_rate * norm_momentum + grad_norm
    new_norm = jnp.concatenate([ln_gains, ln_biases], axis=0) - norm_rate * new_norm_momentum
    new_router_momentum = decay_rate * router_momentum + grad_router
    new_router = router - matrix_rate * ortho_tall(new_router_momentum).astype(jnp.float32)

    rows_first = lax.dynamic_slice_in_dim(first_weight, row_base, dp_share, 0).astype(jnp.float32)
    rows_second = lax.dynamic_slice_in_dim(second_weight, row_base, dp_share, 0).astype(jnp.float32)
    widen_factor = math.sqrt(max(1.0, hidden_units / model_width))
    new_first = rows_first - matrix_rate * widen_factor * iter_first.astype(jnp.float32)
    new_second = rows_second - matrix_rate * iter_second.astype(jnp.float32)
    new_qkv = qkv_weight.astype(jnp.float32) - matrix_rate * math.sqrt(3.0) * iter_qkv.astype(
        jnp.float32
    )
    new_out = out_weight.astype(jnp.float32) - matrix_rate * iter_out.astype(jnp.float32)
    return (
        block_out,
        grad_tokens,
        grad_norm,
        grad_router,
        grad_qkv,
        grad_out,
        grad_first[None],
        grad_second[None],
        new_norm,
        new_norm_momentum,
        new_router,
        new_router_momentum,
        new_qkv,
        moment_qkv,
        new_out,
        moment_out,
        new_first[None],
        moment_first[None],
        new_second[None],
        moment_second[None],
    )


def solution(mesh):
    in_specs = (
        P(("dp", "expert"), None),
        P(("dp", "expert"), None),
        P(("dp", "expert"), None),
        P(("dp", "expert"), None),
        P(),
        P(),
        P("expert", None),
        P("expert", None),
        P(),
        P("expert", None, None),
        P("expert", None, None),
        P(),
        P(),
        P("expert", None),
        P("expert", None),
        P("expert", "dp", None),
        P("expert", "dp", None),
    )
    out_specs = (
        P(("dp", "expert"), None),
        P(("dp", "expert"), None),
        P(),
        P(),
        P("expert", None),
        P("expert", None),
        P("expert", "dp", None),
        P("expert", "dp", None),
        P(),
        P(),
        P(),
        P(),
        P("expert", None),
        P("expert", None),
        P("expert", None),
        P("expert", None),
        P("expert", "dp", None),
        P("expert", "dp", None),
        P("expert", "dp", None),
        P("expert", "dp", None),
    )
    return jax.shard_map(body, mesh=mesh, in_specs=in_specs, out_specs=out_specs, check_vma=False)
```

```python
import functools
import math

import jax
import jax.numpy as jnp
from jax import lax
from jax.experimental import pallas as pl
from jax.experimental.pallas import tpu as pltpu
from jax.sharding import PartitionSpec as P

HEADS = 12
NS_STEPS = 5
SEQ = 197


quintic_one = 3.4445
quintic_two = -4.775
quintic_three = 2.0315
decay_rate = 0.9
matrix_rate = 0.2
norm_rate = 0.004
norm_eps = 1e-06
frob_eps = 1e-07
highest = lax.Precision.HIGHEST
contract_last = (((1,), (1,)), ((), ()))
contract_first = (((0,), (0,)), ((), ()))


def gelu_slope(preact):
    return (
        0.5 * (1.0 + lax.erf(preact * 0.7071067811865476))
        + preact * jnp.exp(-0.5 * preact * preact) * 0.3989422804014327
    )


def layer_stats(token_rows, gain, bias):
    centre = token_rows - jnp.mean(token_rows, axis=-1, keepdims=True)
    inverse = lax.rsqrt(jnp.mean(centre * centre, axis=-1, keepdims=True) + norm_eps)
    scaled = centre * inverse
    return (scaled, inverse, scaled * gain + bias)


def slot_index(choice_ids, order_rows, experts, capacity):
    token_count = choice_ids.shape[0]
    ranks = jnp.arange(token_count, dtype=jnp.int32)
    turn = jnp.sum(
        jnp.where(order_rows[:, None] == ranks[None, :], ranks[:, None], 0), axis=0, dtype=jnp.int32
    )
    earlier = (turn[None, :] < turn[:, None]).astype(jnp.bfloat16)
    columns = jnp.arange(experts, dtype=jnp.int32)[None, :]
    first = (choice_ids[:, 0:1] == columns).astype(jnp.bfloat16)
    second = (choice_ids[:, 1:2] == columns).astype(jnp.bfloat16)
    counts = jnp.dot(
        earlier, jnp.concatenate([first, second], axis=1), preferred_element_type=jnp.float32
    )
    first_float, second_float = first.astype(jnp.float32), second.astype(jnp.float32)
    first_slot = jnp.sum(counts[:, :experts] * first_float, axis=1)
    second_slot = jnp.sum(
        (counts[:, experts:] + jnp.sum(first_float, axis=0, keepdims=True)) * second_float, axis=1
    )
    slot_values = jnp.stack([first_slot, second_slot], axis=1).astype(jnp.int32)
    return jnp.where(
        slot_values < capacity, choice_ids * capacity + slot_values, experts * capacity
    )


def gates_of(logits, choice_ids):
    columns = jnp.arange(logits.shape[1], dtype=jnp.int32)[None, :]
    first_logit = jnp.sum(jnp.where(choice_ids[:, 0:1] == columns, logits, 0.0), axis=1)
    second_logit = jnp.sum(jnp.where(choice_ids[:, 1:2] == columns, logits, 0.0), axis=1)
    first_gate = jax.nn.sigmoid(first_logit - second_logit)
    return jnp.stack([first_gate, 1.0 - first_gate], axis=1)


def input_grad(base_grad, normed_grad, scaled, inverse, gain):
    lifted = normed_grad * gain
    centred = (
        lifted
        - jnp.mean(lifted, axis=-1, keepdims=True)
        - scaled * jnp.mean(lifted * scaled, axis=-1, keepdims=True)
    )
    return base_grad + inverse * centred


def ortho_tall(matrix):
    iterate = (matrix / (jnp.sqrt(jnp.sum(matrix * matrix)) + frob_eps)).astype(jnp.bfloat16)
    for iteration in range(NS_STEPS):
        gram_matrix = lax.dot_general(
            iterate, iterate, contract_first, preferred_element_type=jnp.float32
        ).astype(jnp.bfloat16)
        mixer_matrix = (
            quintic_two * gram_matrix.astype(jnp.float32)
            + quintic_three * jnp.dot(gram_matrix, gram_matrix, preferred_element_type=jnp.float32)
        ).astype(jnp.bfloat16)
        iterate = (
            quintic_one * iterate.astype(jnp.float32)
            + jnp.dot(iterate, mixer_matrix, preferred_element_type=jnp.float32)
        ).astype(jnp.bfloat16)
    return iterate


def ortho_kernel(block, tile, row_count, base_ref, moment_ref, out_ref, iterate, gram, mixer):
    rows, cols = moment_ref.shape
    tiles = cols // tile

    def squares(index, total):
        part = moment_ref[:, pl.ds(pl.multiple_of(index * tile, tile), tile)].astype(jnp.float32)
        return total + jnp.sum(part * part, axis=0, keepdims=True)

    total = lax.fori_loop(0, tiles, squares, jnp.zeros((1, tile), jnp.float32))
    norm = jnp.sqrt(jnp.sum(total)) + frob_eps

    @pl.loop(0, tiles)
    def _(index):
        span = pl.ds(pl.multiple_of(index * tile, tile), tile)
        iterate[:, span] = (moment_ref[:, span].astype(jnp.float32) / norm).astype(jnp.bfloat16)

    def mirror(target, part, index):
        target[index * block : (index + 1) * block, 0 : (index + 1) * block] = part
        for other in range(index):
            target[other * block : (other + 1) * block, index * block : (index + 1) * block] = part[
                :, other * block : (other + 1) * block
            ].T

    def make_gram():
        for index in range(rows // block):
            mirror(
                gram,
                lax.dot_general(
                    iterate[index * block : (index + 1) * block, :],
                    iterate[0 : (index + 1) * block, :],
                    contract_last,
                    preferred_element_type=jnp.float32,
                ).astype(jnp.bfloat16),
                index,
            )

    def mix(gram_rows, gram_part, gram_columns):
        return (
            quintic_two * gram_part.astype(jnp.float32)
            + quintic_three * jnp.dot(gram_rows, gram_columns, preferred_element_type=jnp.float32)
        ).astype(jnp.bfloat16)

    def apply(mixer_rows, part, columns):
        return (
            quintic_one * part.astype(jnp.float32)
            + jnp.dot(mixer_rows, columns, preferred_element_type=jnp.float32)
        ).astype(jnp.bfloat16)

    @pl.loop(0, NS_STEPS - 1)
    def _(step):
        make_gram()
        for index in range(rows // block):
            span = pl.ds(index * block, block)
            reach = (index + 1) * block
            mirror(mixer, mix(gram[span, :], gram[span, 0:reach], gram[:, 0:reach]), index)

        @pl.loop(0, tiles)
        def _(index):
            span = pl.ds(pl.multiple_of(index * tile, tile), tile)
            columns = iterate[:, span]
            iterate[:, span] = apply(mixer[...], columns, columns)

    make_gram()
    if row_count == rows:
        own = pl.ds(0, rows)
    else:
        own = pl.ds(pl.multiple_of(base_ref[0], row_count), row_count)
    mixer[0:row_count, :] = mix(gram[own, :], gram[own, :], gram[...])

    @pl.loop(0, tiles)
    def _(index):
        span = pl.ds(pl.multiple_of(index * tile, tile), tile)
        out_ref[:, span] = apply(mixer[0:row_count, :], iterate[own, span], iterate[:, span])


def ortho_rows(moment, row_start, row_count):
    rows, cols = moment.shape
    block = next(size for size in (256, 128, rows) if rows % size == 0)
    tile = next(size for size in (768, 512, 256, 128, cols) if cols % size == 0)
    whole = row_count % 16 != 0
    kept = rows if whole else row_count
    flops = 2 * NS_STEPS * rows * rows * (2 * cols + rows)
    rows_out = pl.pallas_call(
        functools.partial(ortho_kernel, block, tile, kept),
        out_shape=jax.ShapeDtypeStruct((kept, cols), jnp.bfloat16),
        in_specs=[
            pl.BlockSpec(memory_space=pltpu.SMEM),
            pl.BlockSpec(memory_space=pltpu.VMEM),
        ],
        out_specs=pl.BlockSpec(memory_space=pltpu.VMEM),
        scratch_shapes=[
            pltpu.VMEM((rows, cols), jnp.bfloat16),
            pltpu.VMEM((rows, rows), jnp.bfloat16),
            pltpu.VMEM((rows, rows), jnp.bfloat16),
        ],
        compiler_params=pltpu.CompilerParams(vmem_limit_bytes=40 << 20),
        cost_estimate=pl.CostEstimate(
            flops=flops, bytes_accessed=4 * rows * cols, transcendentals=0
        ),
    )(jnp.reshape(row_start, (1,)).astype(jnp.int32), moment)
    if whole:
        rows_out = lax.dynamic_slice_in_dim(rows_out, row_start, row_count, 0)
    return rows_out


MESH = pl.DeviceIdType.MESH


def at_expert(index):
    return {"expert": index}


def at_dp(index):
    return {"dp": index}


def remote(source, target, send_sem, recv_sem, device):
    return pltpu.make_async_remote_copy(
        src_ref=source,
        dst_ref=target,
        send_sem=send_sem,
        recv_sem=recv_sem,
        device_id=device,
        device_id_type=MESH,
    )


def greet(devices):
    barrier = pltpu.get_barrier_semaphore()
    for device in devices:
        pl.semaphore_signal(barrier, inc=1, device_id=device, device_id_type=MESH)
    pl.semaphore_wait(barrier, len(devices))


def neighbours(chips, planes):
    me = lax.axis_index("expert")
    core, chip = lax.rem(me, 2), lax.div(me, 2)
    plane = lax.axis_index("dp")
    ahead = [2 * lax.rem(chip + shift, chips) + core for shift in range(1, chips)]
    behind = [2 * lax.rem(chip + chips - shift, chips) + core for shift in range(1, chips)]
    above = [lax.rem(plane + shift, planes) for shift in range(1, planes)]
    return me, core, chip, plane, me + 1 - 2 * core, ahead, behind, above


def spread_start(piece, me, partner, ahead, sems, lane):
    copies = [remote(piece(me), piece(me), sems.at[0, lane, 0], sems.at[1, lane, 0], at_expert(partner))]
    for shift, peer in enumerate(ahead, 1):
        copies.append(
            remote(piece(me), piece(me), sems.at[0, lane, shift], sems.at[1, lane, shift], at_expert(peer))
        )
    for copy in copies:
        copy.start()
    return copies


def spread_relay(piece, copies, partner, behind, sems, lane):
    relays = []
    for shift, source in enumerate(behind, 1):
        copies[shift].wait_recv()
        relay = remote(
            piece(source), piece(source), sems.at[2, lane, shift], sems.at[3, lane, shift], at_expert(partner)
        )
        relay.start()
        relays.append(relay)
    return relays


def spread_finish(copies, relays):
    copies[0].wait_recv()
    for relay in relays:
        relay.wait_recv()
    for copy in copies + relays:
        copy.wait_send()


def weights_kernel(
    chips, planes, qkv_ref, out_ref, moments_ref, qkv_all, out_all, moments_all, spread_sems, moment_sems, local_sems
):
    me, core, chip, plane, partner, ahead, behind, above = neighbours(chips, planes)
    greet([at_expert(i) for i in [partner] + ahead] + [at_dp(i) for i in above])
    own_copies = [
        pltpu.make_async_copy(qkv_ref, qkv_all.at[me], local_sems.at[0]),
        pltpu.make_async_copy(out_ref, out_all.at[me], local_sems.at[1]),
    ]
    lanes = []
    for lane, (source, target) in enumerate(((qkv_ref, qkv_all), (out_ref, out_all))):
        copies = [
            remote(
                source,
                target.at[me],
                spread_sems.at[0, lane, shift],
                spread_sems.at[1, lane, shift],
                at_expert(peer),
            )
            for shift, peer in enumerate([partner] + ahead)
        ]
        for copy in copies[1:] + copies[:1]:
            copy.start()
        lanes.append((lane, target, copies))
    keepers = (planes // 2 - 1, planes // 2)
    for which, keeper in enumerate(keepers):

        @pl.when(plane != keeper)
        def _():
            remote(
                moments_ref.at[which],
                moments_all.at[plane],
                moment_sems.at[0, which],
                moment_sems.at[1, plane],
                at_dp(keeper),
            ).start()

        @pl.when(plane == keeper)
        def _():
            pltpu.make_async_copy(
                moments_ref.at[which], moments_all.at[plane], local_sems.at[2]
            ).start()

    for copy in own_copies:
        copy.start()
    relayed = [
        (copies, spread_relay(lambda i: target.at[i], copies, partner, behind, spread_sems, lane))
        for lane, target, copies in lanes
    ]
    for copies, relays in relayed:
        spread_finish(copies, relays)
    for copy in own_copies:
        copy.wait()
    for which, keeper in enumerate(keepers):

        @pl.when(plane != keeper)
        def _():
            remote(
                moments_ref.at[which],
                moments_all.at[plane],
                moment_sems.at[0, which],
                moment_sems.at[1, plane],
                at_dp(keeper),
            ).wait_send()

        @pl.when(plane == keeper)
        def _():
            pltpu.make_async_copy(
                moments_ref.at[which], moments_all.at[plane], local_sems.at[2]
            ).wait()
            for source in range(planes):
                if source != keeper:
                    remote(
                        moments_ref.at[which],
                        moments_all.at[source],
                        moment_sems.at[0, which],
                        moment_sems.at[1, source],
                        at_dp(source),
                    ).wait_recv()


def gather_weights(qkv_weight, out_weight, moments):
    members, planes = lax.axis_size("expert"), lax.axis_size("dp")
    chips = members // 2
    anywhere = pl.BlockSpec(memory_space=pl.ANY)
    return pl.pallas_call(
        functools.partial(weights_kernel, chips, planes),
        out_shape=(
            jax.ShapeDtypeStruct((members,) + qkv_weight.shape, jnp.bfloat16),
            jax.ShapeDtypeStruct((members,) + out_weight.shape, jnp.bfloat16),
            jax.ShapeDtypeStruct((planes,) + moments.shape[1:], jnp.bfloat16),
        ),
        in_specs=[anywhere] * 3,
        out_specs=[anywhere] * 3,
        scratch_shapes=[
            pltpu.SemaphoreType.DMA((4, 2, chips)),
            pltpu.SemaphoreType.DMA((2, max(2, planes))),
            pltpu.SemaphoreType.DMA((3,)),
        ],
        compiler_params=pltpu.CompilerParams(collective_id=1, has_side_effects=True),
    )(qkv_weight, out_weight, moments)


def attention_kernel(
    chips,
    planes,
    split,
    qkv_term,
    out_term,
    qkv_moment,
    out_moment,
    small_ref,
    rows_ref,
    grad_qkv,
    grad_out,
    new_qkv_moment,
    new_out_moment,
    small_out,
    qkv_all,
    out_all,
    rows_all,
    crossed,
    leaving,
    landed,
    plane_out,
    plane_in,
    plane_all,
    small_pair,
    small_chip,
    small_plane,
    cross_sems,
    chip_sems,
    plane_sems,
    share_sems,
    spread_sems,
    rows_sems,
    small_sems,
    local_sems,
):
    width = out_term.shape[2]
    lanes = qkv_term.shape[2] // width + 1
    me, core, chip, plane, partner, ahead, behind, above = neighbours(chips, planes)
    greet([at_expert(i) for i in [partner] + ahead] + [at_dp(i) for i in above])

    def cut(pair, lane):
        if lane == lanes - 1:
            return pair[1], pl.ds(0, width)
        return pair[0], pl.ds(lane * width, width)

    def term(lane, index):
        ref, columns = cut((qkv_term, out_term), lane)
        return ref[index, :, columns].astype(jnp.float32)

    order = [lanes - 1] + list(range(lanes - 1))
    crosses = {}
    for lane in order:
        for shift in range(chips):
            target = lax.rem(chip + shift, chips)
            ref, columns = cut((qkv_term, out_term), lane)
            crosses[lane, shift] = remote(
                ref.at[2 * target + 1 - core, :, columns],
                crossed.at[lane, target],
                cross_sems.at[0, lane, shift],
                cross_sems.at[1, lane, shift],
                at_expert(partner),
            )
        for shift in list(range(1, chips)) + [0]:
            crosses[lane, shift].start()
    small_copy = remote(small_ref, small_pair, small_sems.at[0, 0], small_sems.at[1, 0], at_expert(partner))
    small_copy.start()
    sends = list(crosses.values()) + [small_copy]
    rows_copies = [
        remote(rows_ref, rows_all.at[plane], rows_sems.at[0, i], rows_sems.at[1, i], at_dp(peer))
        for i, peer in enumerate(above)
    ]
    own_rows = pltpu.make_async_copy(rows_ref, rows_all.at[plane], local_sems.at[0])
    for copy in rows_copies + [own_rows]:
        copy.start()

    chip_copies = {}

    def to_chips(lane):
        for shift in range(1, chips):
            target = lax.rem(chip + shift, chips)
            crosses[lane, shift].wait_recv()
            leaving[lane, shift - 1] = (
                term(lane, 2 * target + core) + crossed[lane, target].astype(jnp.float32)
            ).astype(jnp.bfloat16)
            copy = remote(
                leaving.at[lane, shift - 1],
                landed.at[lane, shift - 1],
                chip_sems.at[0, lane, shift - 1],
                chip_sems.at[1, lane, shift - 1],
                at_expert(ahead[shift - 1]),
            )
            copy.start()
            chip_copies[lane, shift] = copy
            sends.append(copy)

    small_chip_copies = []

    def small_to_chips():
        small_copy.wait_recv()
        small_chip[chip] = small_ref[...] + small_pair[...]
        for shift, peer in enumerate(ahead, 1):
            copy = remote(
                small_chip.at[chip],
                small_chip.at[chip],
                small_sems.at[0, shift],
                small_sems.at[1, shift],
                at_expert(peer),
            )
            copy.start()
            small_chip_copies.append(copy)
            sends.append(copy)

    small_plane_copies = []

    def small_to_planes():
        for copy in small_chip_copies:
            copy.wait_recv()
        small_plane[plane] = sum(small_chip[i] for i in range(chips))
        for i, peer in enumerate(above):
            copy = remote(
                small_plane.at[plane],
                small_plane.at[plane],
                small_sems.at[0, chips + i],
                small_sems.at[1, chips + i],
                at_dp(peer),
            )
            copy.start()
            small_plane_copies.append(copy)
            sends.append(copy)

    def small_finish():
        for copy in small_plane_copies:
            copy.wait_recv()
        small_out[...] = sum(small_plane[i] for i in range(planes))

    part = plane_out.shape[2]
    plane_copies = {}

    def to_planes(lane):
        crosses[lane, 0].wait_recv()
        total = term(lane, me) + crossed[lane, chip].astype(jnp.float32)
        for shift in range(1, chips):
            chip_copies[lane, shift].wait_recv()
            total = total + landed[lane, shift - 1].astype(jnp.float32)
        if split:
            for i in range(planes):
                plane_out[lane, i] = total[i * part : (i + 1) * part].astype(jnp.bfloat16)
        else:
            plane_in[lane, plane] = total.astype(jnp.bfloat16)
        plane_copies[lane] = []
        for i, peer in enumerate(above):
            copy = remote(
                plane_out.at[lane, peer] if split else plane_in.at[lane, plane],
                plane_in.at[lane, plane],
                plane_sems.at[0, lane, i],
                plane_sems.at[1, lane, i],
                at_dp(peer),
            )
            copy.start()
            plane_copies[lane].append(copy)
            sends.append(copy)

    share_copies = {}

    def share_planes(lane):
        share_copies[lane] = []
        if not split:
            return
        for copy in plane_copies[lane]:
            copy.wait_recv()
        plane_in[lane, plane] = plane_out[lane, plane]
        total = plane_in[lane, 0].astype(jnp.float32)
        for i in range(1, planes):
            total = total + plane_in[lane, i].astype(jnp.float32)
        plane_all[lane, plane] = total.astype(jnp.bfloat16)
        for i, peer in enumerate(above):
            copy = remote(
                plane_all.at[lane, plane],
                plane_all.at[lane, plane],
                share_sems.at[0, lane, i],
                share_sems.at[1, lane, i],
                at_dp(peer),
            )
            copy.start()
            share_copies[lane].append(copy)
            sends.append(copy)

    def piece_of(lane):
        ref, columns = cut((qkv_all, out_all), lane)
        return lambda index: ref.at[index, :, columns]

    spreads, relays = {}, {}

    def make_moment(lane):
        moment, columns = cut((qkv_moment, out_moment), lane)
        grad_target, _ = cut((grad_qkv, grad_out), lane)
        moment_target, _ = cut((new_qkv_moment, new_out_moment), lane)
        whole, _ = cut((qkv_all, out_all), lane)
        if split:
            for copy in share_copies[lane]:
                copy.wait_recv()
            grad = jnp.concatenate(
                [plane_all[lane, i].astype(jnp.float32) for i in range(planes)], axis=0
            )
        else:
            for copy in plane_copies[lane]:
                copy.wait_recv()
            grad = sum(plane_in[lane, i].astype(jnp.float32) for i in range(planes))
        fresh = decay_rate * moment[:, columns] + grad
        grad_target[:, columns] = grad
        moment_target[:, columns] = fresh
        whole[me, :, columns] = fresh.astype(jnp.bfloat16)
        spreads[lane] = spread_start(piece_of(lane), me, partner, ahead, spread_sems, lane)

    def relay(lane):
        relays[lane] = spread_relay(piece_of(lane), spreads[lane], partner, behind, spread_sems, lane)

    for lane in order:
        to_chips(lane)
        if lane == order[0]:
            small_to_chips()
    stages = [to_planes, share_planes, make_moment, relay]
    for step in range(lanes + len(stages) - 1):
        for number in range(len(stages) - 1, -1, -1):
            if 0 <= step - number < lanes:
                stages[number](order[step - number])
        if step == 0:
            small_to_planes()
    small_finish()
    for lane in order:
        spread_finish(spreads[lane], relays[lane])
    for copy in sends:
        copy.wait_send()
    for copy in rows_copies:
        copy.wait()
    own_rows.wait()


def reduce_attention(qkv_term, out_term, qkv_moment, out_moment, small, rows):
    members, planes = lax.axis_size("expert"), lax.axis_size("dp")
    chips = members // 2
    share, width = out_moment.shape
    qkv_width = qkv_moment.shape[1]
    lanes = qkv_width // width + 1
    split = share % (8 * planes) == 0
    part = share // planes if split else share
    anywhere = pl.BlockSpec(memory_space=pl.ANY)
    local = pl.BlockSpec(memory_space=pltpu.VMEM)
    dma = pltpu.SemaphoreType.DMA
    wide = jnp.bfloat16
    return pl.pallas_call(
        functools.partial(attention_kernel, chips, planes, split),
        out_shape=(
            jax.ShapeDtypeStruct(qkv_moment.shape, jnp.float32),
            jax.ShapeDtypeStruct(out_moment.shape, jnp.float32),
            jax.ShapeDtypeStruct(qkv_moment.shape, jnp.float32),
            jax.ShapeDtypeStruct(out_moment.shape, jnp.float32),
            jax.ShapeDtypeStruct(small.shape, jnp.float32),
            jax.ShapeDtypeStruct((members, share, qkv_width), wide),
            jax.ShapeDtypeStruct((members, share, width), wide),
            jax.ShapeDtypeStruct((planes,) + rows.shape, wide),
        ),
        in_specs=[local] * 5 + [anywhere],
        out_specs=[local] * 7 + [anywhere],
        scratch_shapes=[
            pltpu.VMEM((lanes, chips, share, width), wide),
            pltpu.VMEM((lanes, chips - 1, share, width), wide),
            pltpu.VMEM((lanes, chips - 1, share, width), wide),
            pltpu.VMEM((lanes, planes, part, width) if split else (1, 1, part, width), wide),
            pltpu.VMEM((lanes, planes, part, width), wide),
            pltpu.VMEM((lanes, planes, part, width) if split else (1, 1, part, width), wide),
            pltpu.VMEM(small.shape, jnp.float32),
            pltpu.VMEM((chips,) + small.shape, jnp.float32),
            pltpu.VMEM((planes,) + small.shape, jnp.float32),
            dma((2, lanes, chips)),
            dma((2, lanes, chips - 1)),
            dma((2, lanes, planes - 1)),
            dma((2, lanes, planes - 1)),
            dma((4, lanes, chips)),
            dma((2, planes - 1)),
            dma((2, chips + planes - 1)),
            dma((1,)),
        ],
        compiler_params=pltpu.CompilerParams(
            collective_id=2, has_side_effects=True, vmem_limit_bytes=48 << 20
        ),
    )(qkv_term, out_term, qkv_moment, out_moment, small, rows)


def split_heads(qkv_rows, image_count, head_width):
    shaped = qkv_rows.reshape(image_count, SEQ, 3, HEADS, head_width)
    return (shaped[:, :, 0], shaped[:, :, 1], shaped[:, :, 2])


def attention_scores(query_rows, key_rows, score_scale):
    return (
        jnp.einsum("ishd,ithd->ihst", query_rows, key_rows, preferred_element_type=jnp.float32)
        * score_scale
    )


def body(
    tokens,
    cotangent,
    routes,
    priority,
    ln_gains,
    ln_biases,
    qkv_weight,
    out_weight,
    router,
    w_in,
    w_out,
    norm_momentum,
    router_momentum,
    qkv_momentum,
    out_momentum,
    w_in_momentum,
    w_out_momentum,
):
    token_count, model_width = tokens.shape
    experts = router.shape[1]
    hidden_units = w_in.shape[2]
    capacity = (token_count + experts - 1) // experts
    slots_all = experts * capacity
    dp_share = model_width // lax.axis_size("dp")
    image_count = token_count // SEQ
    head_width = model_width // HEADS
    score_scale = 1.0 / math.sqrt(head_width)
    first_weight = w_in[0]
    second_weight = w_out[0]
    cot_float = cotangent.astype(jnp.float32)
    dp_size = lax.axis_size("dp")
    dp_index = lax.axis_index("dp")
    members = lax.axis_size("expert")
    keep_first, keep_second = (dp_size // 2 - 1, dp_size // 2)
    keeps_first = dp_index == keep_first
    keeps = keeps_first | (dp_index == keep_second)
    full_qkv, full_out, every_moment = gather_weights(
        qkv_weight, out_weight, jnp.concatenate([w_in_momentum, w_out_momentum]).astype(jnp.bfloat16)
    )
    full_qkv = full_qkv.reshape(model_width, 3 * model_width)
    full_out = full_out.reshape(model_width, model_width)
    every_moment = every_moment.reshape(model_width, hidden_units)
    token_float = tokens.astype(jnp.float32)
    scaled_one, inverse_one, normed_one = layer_stats(token_float, ln_gains[0], ln_biases[0])
    attn_in = normed_one.astype(jnp.bfloat16)
    qkv_rows = jnp.dot(attn_in, full_qkv, preferred_element_type=jnp.float32).astype(jnp.bfloat16)
    query_rows, key_rows, value_rows = split_heads(qkv_rows, image_count, head_width)
    scores = attention_scores(query_rows, key_rows, score_scale)
    log_total = jnp.log(jnp.sum(jnp.exp(scores), axis=3, keepdims=True))
    attn_probs = jnp.exp(scores - log_total).astype(jnp.bfloat16)
    mixed_rows = (
        jnp.einsum("ihst,ithd->ishd", attn_probs, value_rows, preferred_element_type=jnp.float32)
        .astype(jnp.bfloat16)
        .reshape(token_count, model_width)
    )
    middle_rows = token_float + jnp.dot(mixed_rows, full_out, preferred_element_type=jnp.float32)
    slot_flat = slot_index(routes, priority[0], experts, capacity)
    scaled, inverse, normed = layer_stats(middle_rows, ln_gains[1], ln_biases[1])
    logits = jnp.dot(normed, router, precision=highest)
    gate_values = gates_of(logits, routes)
    position = jnp.arange(slots_all, dtype=jnp.int32)[:, None]
    pick_first = (slot_flat[:, 0][None, :] == position).astype(jnp.float32)
    pick_second = (slot_flat[:, 1][None, :] == position).astype(jnp.float32)
    placing = (pick_first + pick_second).astype(jnp.bfloat16)
    lean_first, lean_second = (pick_first.astype(jnp.bfloat16), pick_second.astype(jnp.bfloat16))
    gated = jnp.concatenate(
        [
            (gate_values[:, 0:1] * cot_float).astype(jnp.bfloat16),
            (gate_values[:, 1:2] * cot_float).astype(jnp.bfloat16),
        ],
        axis=0,
    )
    dispatch = jnp.dot(
        placing, normed.astype(jnp.bfloat16), preferred_element_type=jnp.float32
    ).astype(jnp.bfloat16)
    sent_grad = jnp.dot(
        jnp.concatenate([lean_first, lean_second], axis=1),
        gated,
        preferred_element_type=jnp.float32,
    ).astype(jnp.bfloat16)

    def to_blocks(rows_one, rows_two):
        return jnp.concatenate(
            [
                rows_one.reshape(experts, capacity, model_width),
                rows_two.reshape(experts, capacity, model_width),
            ],
            axis=2,
        )

    arrived = lax.all_to_all(
        to_blocks(dispatch, sent_grad), "expert", split_axis=0, concat_axis=0, tiled=True
    ).reshape(slots_all, 2 * model_width)
    arrived_rows = arrived[:, :model_width]
    grad_rows = arrived[:, model_width:]
    preact_first = jnp.dot(arrived_rows, first_weight, preferred_element_type=jnp.float32)
    active_first = jax.nn.gelu(preact_first, approximate=False).astype(jnp.bfloat16)
    result = lax.dot_general(
        active_first, second_weight, contract_last, preferred_element_type=jnp.float32
    ).astype(jnp.bfloat16)
    act_grad = jnp.dot(grad_rows, second_weight, preferred_element_type=jnp.float32)
    expert_pre_grad = (act_grad * gelu_slope(preact_first)).astype(jnp.bfloat16)
    row_grad = lax.dot_general(
        expert_pre_grad, first_weight, contract_last, preferred_element_type=jnp.float32
    ).astype(jnp.bfloat16)
    returned = lax.all_to_all(
        to_blocks(result, row_grad), "expert", split_axis=0, concat_axis=0, tiled=True
    ).reshape(slots_all, 2 * model_width)
    back_first = lax.dot_general(
        lean_first, returned, contract_first, preferred_element_type=jnp.float32
    )
    back_second = lax.dot_general(
        lean_second, returned, contract_first, preferred_element_type=jnp.float32
    )
    picked_first, picked_second = (back_first[:, :model_width], back_second[:, :model_width])
    block_out = middle_rows + (
        gate_values[:, 0:1] * picked_first + gate_values[:, 1:2] * picked_second
    )
    grad_gap = jnp.sum(picked_first * cot_float, axis=1) - jnp.sum(picked_second * cot_float, axis=1)
    logit_step = gate_values[:, 0] * gate_values[:, 1] * grad_gap
    columns = jnp.arange(experts, dtype=jnp.int32)[None, :]
    logit_grad = (
        (routes[:, 0:1] == columns).astype(jnp.float32)
        - (routes[:, 1:2] == columns).astype(jnp.float32)
    ) * logit_step[:, None]
    gathered = back_first[:, model_width:] + back_second[:, model_width:]
    normed_grad = gathered + lax.dot_general(
        logit_grad, router, contract_last, precision=highest
    )
    router_local = lax.dot_general(normed, logit_grad, contract_first, precision=highest)
    middle_grad = input_grad(cot_float, normed_grad, scaled, inverse, ln_gains[1])
    middle_rounded = middle_grad.astype(jnp.bfloat16)
    mixed_grad = lax.dot_general(
        middle_rounded, full_out, contract_last, preferred_element_type=jnp.float32
    ).astype(jnp.bfloat16)
    scores_again = attention_scores(query_rows, key_rows, score_scale)
    probs_again = jnp.exp(scores_again - log_total).astype(jnp.bfloat16)
    grad_heads = mixed_grad.reshape(image_count, SEQ, HEADS, head_width)
    value_grad = jnp.einsum(
        "ihst,ishd->ithd", probs_again, grad_heads, preferred_element_type=jnp.float32
    )
    prob_grad = jnp.einsum(
        "ishd,ithd->ihst", grad_heads, value_rows, preferred_element_type=jnp.float32
    )
    prob_float = probs_again.astype(jnp.float32)
    row_delta = jnp.sum(prob_float * prob_grad, axis=3, keepdims=True)
    score_grad = (prob_float * (prob_grad - row_delta) * score_scale).astype(jnp.bfloat16)
    query_grad = jnp.einsum(
        "ihst,ithd->ishd", score_grad, key_rows, preferred_element_type=jnp.float32
    )
    key_grad = jnp.einsum(
        "ihst,ishd->ithd", score_grad, query_rows, preferred_element_type=jnp.float32
    )
    qkv_grad = (
        jnp.stack([query_grad, key_grad, value_grad], axis=2)
        .astype(jnp.bfloat16)
        .reshape(token_count, 3 * model_width)
    )
    attn_in_grad = lax.dot_general(
        qkv_grad, full_qkv, contract_last, preferred_element_type=jnp.float32
    )
    grad_tokens = input_grad(middle_grad, attn_in_grad, scaled_one, inverse_one, ln_gains[0])
    qkv_term = lax.dot_general(
        attn_in, qkv_grad, contract_first, preferred_element_type=jnp.float32
    )
    out_term = lax.dot_general(
        mixed_rows, middle_rounded, contract_first, preferred_element_type=jnp.float32
    )
    norm_local = jnp.stack(
        [
            jnp.sum(attn_in_grad * scaled_one, axis=0),
            jnp.sum(normed_grad * scaled, axis=0),
            jnp.sum(attn_in_grad, axis=0),
            jnp.sum(normed_grad, axis=0),
        ]
    )
    small = jnp.concatenate([router_local.T, norm_local], axis=0)
    small_rows = experts + 4
    slot_pad = -slots_all % 16
    (
        grad_qkv,
        grad_out,
        moment_qkv,
        moment_out,
        small_total,
        whole_qkv,
        whole_out,
        every_pair,
    ) = reduce_attention(
        qkv_term.astype(jnp.bfloat16).reshape(members, -1, 3 * model_width),
        out_term.astype(jnp.bfloat16).reshape(members, -1, model_width),
        qkv_momentum,
        out_momentum,
        jnp.pad(small, ((0, -small_rows % 8), (0, 0))),
        jnp.pad(arrived, ((0, slot_pad), (0, 0))),
    )
    every_pair = every_pair.reshape(dp_size * (slots_all + slot_pad), 2 * model_width)
    whole_qkv = whole_qkv.reshape(model_width, 3 * model_width)
    whole_out = whole_out.reshape(model_width, model_width)
    grad_router = small_total[:experts].T
    grad_norm = small_total[experts:small_rows]
    row_base = dp_index * dp_share
    every_row = every_pair[:, :model_width]
    every_grad = every_pair[:, model_width:]
    every_preact = jnp.dot(every_row, first_weight, preferred_element_type=jnp.float32)
    every_active = jax.nn.gelu(every_preact, approximate=False).astype(jnp.bfloat16)
    every_act_grad = jnp.dot(every_grad, second_weight, preferred_element_type=jnp.float32)
    every_pre_grad = (every_act_grad * gelu_slope(every_preact)).astype(jnp.bfloat16)
    own_left, other_left = (
        jnp.where(keeps_first, every_row, every_grad),
        jnp.where(keeps_first, every_grad, every_row),
    )
    own_right, other_right = (
        jnp.where(keeps_first, every_pre_grad, every_active),
        jnp.where(keeps_first, every_active, every_pre_grad),
    )
    whole_own = lax.dot_general(
        own_left, own_right, contract_first, preferred_element_type=jnp.float32
    )
    part_own = lax.dynamic_slice_in_dim(whole_own, row_base, dp_share, 0)
    part_other = lax.dot_general(
        lax.dynamic_slice_in_dim(other_left, row_base, dp_share, 1),
        other_right,
        contract_first,
        preferred_element_type=jnp.float32,
    )
    grad_first = jnp.where(keeps_first, part_own, part_other)
    grad_second = jnp.where(keeps_first, part_other, part_own)
    moment_first = decay_rate * w_in_momentum[0] + grad_first
    moment_second = decay_rate * w_out_momentum[0] + grad_second
    iter_whole = ortho_rows(
        jnp.where(keeps, decay_rate * every_moment.astype(jnp.float32) + whole_own, 0.0),
        jnp.zeros((), jnp.int32),
        model_width,
    )
    iter_slices = [
        lax.dynamic_slice_in_dim(iter_whole, ((dp_index + i) % dp_size) * dp_share, dp_share, 0)
        for i in range(dp_size)
    ]
    iter_first, iter_second = (iter_slices[0], iter_slices[0])
    for shift in range(1, dp_size):
        received = lax.ppermute(
            iter_slices[shift],
            "dp",
            [(i, (i + shift) % dp_size) for i in (keep_first, keep_second)],
        )
        iter_first = jnp.where(dp_index == (keep_first + shift) % dp_size, received, iter_first)
        iter_second = jnp.where(dp_index == (keep_second + shift) % dp_size, received, iter_second)
    expert_share = qkv_weight.shape[0]
    expert_base = lax.axis_index("expert") * expert_share
    iter_out = ortho_rows(whole_out, expert_base, expert_share)
    iter_qkv = ortho_rows(whole_qkv, expert_base, expert_share)
    new_norm_momentum = decay_rate * norm_momentum + grad_norm
    new_norm = jnp.concatenate([ln_gains, ln_biases], axis=0) - norm_rate * new_norm_momentum
    new_router_momentum = decay_rate * router_momentum + grad_router
    new_router = router - matrix_rate * ortho_tall(new_router_momentum).astype(jnp.float32)

    rows_first = lax.dynamic_slice_in_dim(first_weight, row_base, dp_share, 0).astype(jnp.float32)
    rows_second = lax.dynamic_slice_in_dim(second_weight, row_base, dp_share, 0).astype(jnp.float32)
    widen_factor = math.sqrt(max(1.0, hidden_units / model_width))
    new_first = rows_first - matrix_rate * widen_factor * iter_first.astype(jnp.float32)
    new_second = rows_second - matrix_rate * iter_second.astype(jnp.float32)
    new_qkv = qkv_weight.astype(jnp.float32) - matrix_rate * math.sqrt(3.0) * iter_qkv.astype(
        jnp.float32
    )
    new_out = out_weight.astype(jnp.float32) - matrix_rate * iter_out.astype(jnp.float32)
    return (
        block_out,
        grad_tokens,
        grad_norm,
        grad_router,
        grad_qkv,
        grad_out,
        grad_first[None],
        grad_second[None],
        new_norm,
        new_norm_momentum,
        new_router,
        new_router_momentum,
        new_qkv,
        moment_qkv,
        new_out,
        moment_out,
        new_first[None],
        moment_first[None],
        new_second[None],
        moment_second[None],
    )


def solution(mesh):
    in_specs = (
        P(("dp", "expert"), None),
        P(("dp", "expert"), None),
        P(("dp", "expert"), None),
        P(("dp", "expert"), None),
        P(),
        P(),
        P("expert", None),
        P("expert", None),
        P(),
        P("expert", None, None),
        P("expert", None, None),
        P(),
        P(),
        P("expert", None),
        P("expert", None),
        P("expert", "dp", None),
        P("expert", "dp", None),
    )
    out_specs = (
        P(("dp", "expert"), None),
        P(("dp", "expert"), None),
        P(),
        P(),
        P("expert", None),
        P("expert", None),
        P("expert", "dp", None),
        P("expert", "dp", None),
        P(),
        P(),
        P(),
        P(),
        P("expert", None),
        P("expert", None),
        P("expert", None),
        P("expert", None),
        P("expert", "dp", None),
        P("expert", "dp", None),
        P("expert", "dp", None),
        P("expert", "dp", None),
    )
    return jax.shard_map(body, mesh=mesh, in_specs=in_specs, out_specs=out_specs, check_vma=False)
```

```python
import functools
import math

import jax
import jax.numpy as jnp
from jax import lax
from jax.experimental import pallas as pl
from jax.experimental.pallas import tpu as pltpu
from jax.sharding import PartitionSpec as P

HEADS = 12
NS_STEPS = 5
SEQ = 197


quintic_one = 3.4445
quintic_two = -4.775
quintic_three = 2.0315
decay_rate = 0.9
matrix_rate = 0.2
norm_rate = 0.004
norm_eps = 1e-06
frob_eps = 1e-07
highest = lax.Precision.HIGHEST
contract_last = (((1,), (1,)), ((), ()))
contract_first = (((0,), (0,)), ((), ()))


def gelu_slope(preact):
    return (
        0.5 * (1.0 + lax.erf(preact * 0.7071067811865476))
        + preact * jnp.exp(-0.5 * preact * preact) * 0.3989422804014327
    )


def layer_stats(token_rows, gain, bias):
    centre = token_rows - jnp.mean(token_rows, axis=-1, keepdims=True)
    inverse = lax.rsqrt(jnp.mean(centre * centre, axis=-1, keepdims=True) + norm_eps)
    scaled = centre * inverse
    return (scaled, inverse, scaled * gain + bias)


def slot_index(choice_ids, order_rows, experts, capacity):
    token_count = choice_ids.shape[0]
    ranks = jnp.arange(token_count, dtype=jnp.int32)
    turn = jnp.sum(
        jnp.where(order_rows[:, None] == ranks[None, :], ranks[:, None], 0), axis=0, dtype=jnp.int32
    )
    earlier = (turn[None, :] < turn[:, None]).astype(jnp.bfloat16)
    columns = jnp.arange(experts, dtype=jnp.int32)[None, :]
    first = (choice_ids[:, 0:1] == columns).astype(jnp.bfloat16)
    second = (choice_ids[:, 1:2] == columns).astype(jnp.bfloat16)
    counts = jnp.dot(
        earlier, jnp.concatenate([first, second], axis=1), preferred_element_type=jnp.float32
    )
    first_float, second_float = first.astype(jnp.float32), second.astype(jnp.float32)
    first_slot = jnp.sum(counts[:, :experts] * first_float, axis=1)
    second_slot = jnp.sum(
        (counts[:, experts:] + jnp.sum(first_float, axis=0, keepdims=True)) * second_float, axis=1
    )
    slot_values = jnp.stack([first_slot, second_slot], axis=1).astype(jnp.int32)
    return jnp.where(
        slot_values < capacity, choice_ids * capacity + slot_values, experts * capacity
    )


def gates_of(logits, choice_ids):
    columns = jnp.arange(logits.shape[1], dtype=jnp.int32)[None, :]
    first_logit = jnp.sum(jnp.where(choice_ids[:, 0:1] == columns, logits, 0.0), axis=1)
    second_logit = jnp.sum(jnp.where(choice_ids[:, 1:2] == columns, logits, 0.0), axis=1)
    first_gate = jax.nn.sigmoid(first_logit - second_logit)
    return jnp.stack([first_gate, 1.0 - first_gate], axis=1)


def input_grad(base_grad, normed_grad, scaled, inverse, gain):
    lifted = normed_grad * gain
    centred = (
        lifted
        - jnp.mean(lifted, axis=-1, keepdims=True)
        - scaled * jnp.mean(lifted * scaled, axis=-1, keepdims=True)
    )
    return base_grad + inverse * centred


def ortho_tall(matrix):
    iterate = (matrix / (jnp.sqrt(jnp.sum(matrix * matrix)) + frob_eps)).astype(jnp.bfloat16)
    for iteration in range(NS_STEPS):
        gram_matrix = lax.dot_general(
            iterate, iterate, contract_first, preferred_element_type=jnp.float32
        ).astype(jnp.bfloat16)
        mixer_matrix = (
            quintic_two * gram_matrix.astype(jnp.float32)
            + quintic_three * jnp.dot(gram_matrix, gram_matrix, preferred_element_type=jnp.float32)
        ).astype(jnp.bfloat16)
        iterate = (
            quintic_one * iterate.astype(jnp.float32)
            + jnp.dot(iterate, mixer_matrix, preferred_element_type=jnp.float32)
        ).astype(jnp.bfloat16)
    return iterate


def ortho_steps(moment, block, tile, iterate, gram, mixer):
    rows, cols = moment.shape
    tiles = cols // tile

    def begin():
        def squares(index, total):
            part = moment[:, pl.ds(pl.multiple_of(index * tile, tile), tile)].astype(jnp.float32)
            return total + jnp.sum(part * part, axis=0, keepdims=True)

        total = lax.fori_loop(0, tiles, squares, jnp.zeros((1, tile), jnp.float32))
        norm = jnp.sqrt(jnp.sum(total)) + frob_eps

        @pl.loop(0, tiles)
        def _(index):
            span = pl.ds(pl.multiple_of(index * tile, tile), tile)
            iterate[:, span] = (moment[:, span].astype(jnp.float32) / norm).astype(jnp.bfloat16)

    def mirror(target, part, index):
        target[index * block : (index + 1) * block, 0 : (index + 1) * block] = part
        for other in range(index):
            target[other * block : (other + 1) * block, index * block : (index + 1) * block] = part[
                :, other * block : (other + 1) * block
            ].T

    def make_gram():
        for index in range(rows // block):
            mirror(
                gram,
                lax.dot_general(
                    iterate[index * block : (index + 1) * block, :],
                    iterate[0 : (index + 1) * block, :],
                    contract_last,
                    preferred_element_type=jnp.float32,
                ).astype(jnp.bfloat16),
                index,
            )

    def mix(gram_rows, gram_part, gram_columns):
        return (
            quintic_two * gram_part.astype(jnp.float32)
            + quintic_three * jnp.dot(gram_rows, gram_columns, preferred_element_type=jnp.float32)
        ).astype(jnp.bfloat16)

    def apply(mixer_rows, part, columns):
        return (
            quintic_one * part.astype(jnp.float32)
            + jnp.dot(mixer_rows, columns, preferred_element_type=jnp.float32)
        ).astype(jnp.bfloat16)

    def make_mixer():
        for index in range(rows // block):
            span = pl.ds(index * block, block)
            reach = (index + 1) * block
            mirror(mixer, mix(gram[span, :], gram[span, 0:reach], gram[:, 0:reach]), index)

    def advance():
        @pl.loop(0, tiles)
        def _(index):
            span = pl.ds(pl.multiple_of(index * tile, tile), tile)
            columns = iterate[:, span]
            iterate[:, span] = apply(mixer[...], columns, columns)

    def last_rows(own, row_count, out_ref):
        mixer[0:row_count, :] = mix(gram[own, :], gram[own, :], gram[...])

        @pl.loop(0, tiles)
        def _(index):
            span = pl.ds(pl.multiple_of(index * tile, tile), tile)
            out_ref[:, span] = apply(mixer[0:row_count, :], iterate[own, span], iterate[:, span])

    return begin, make_gram, make_mixer, advance, last_rows


def ortho_kernel(block, tile, row_count, base_ref, moment_ref, out_ref, iterate, gram, mixer):
    rows = moment_ref.shape[0]
    begin, make_gram, make_mixer, advance, last_rows = ortho_steps(
        moment_ref, block, tile, iterate, gram, mixer
    )
    begin()

    @pl.loop(0, NS_STEPS - 1)
    def _(step):
        make_gram()
        make_mixer()
        advance()

    make_gram()
    if row_count == rows:
        own = pl.ds(0, rows)
    else:
        own = pl.ds(pl.multiple_of(base_ref[0], row_count), row_count)
    last_rows(own, row_count, out_ref)


def tile_sizes(rows, cols):
    block = next(size for size in (256, 128, rows) if rows % size == 0)
    tile = next(size for size in (768, 512, 256, 128, cols) if cols % size == 0)
    return block, tile


def ortho_rows(moment, row_start, row_count):
    rows, cols = moment.shape
    block, tile = tile_sizes(rows, cols)
    whole = row_count % 16 != 0
    kept = rows if whole else row_count
    flops = 2 * NS_STEPS * rows * rows * (2 * cols + rows)
    rows_out = pl.pallas_call(
        functools.partial(ortho_kernel, block, tile, kept),
        out_shape=jax.ShapeDtypeStruct((kept, cols), jnp.bfloat16),
        in_specs=[
            pl.BlockSpec(memory_space=pltpu.SMEM),
            pl.BlockSpec(memory_space=pltpu.VMEM),
        ],
        out_specs=pl.BlockSpec(memory_space=pltpu.VMEM),
        scratch_shapes=[
            pltpu.VMEM((rows, cols), jnp.bfloat16),
            pltpu.VMEM((rows, rows), jnp.bfloat16),
            pltpu.VMEM((rows, rows), jnp.bfloat16),
        ],
        compiler_params=pltpu.CompilerParams(vmem_limit_bytes=40 << 20),
        cost_estimate=pl.CostEstimate(
            flops=flops, bytes_accessed=4 * rows * cols, transcendentals=0
        ),
    )(jnp.reshape(row_start, (1,)).astype(jnp.int32), moment)
    if whole:
        rows_out = lax.dynamic_slice_in_dim(rows_out, row_start, row_count, 0)
    return rows_out


MESH = pl.DeviceIdType.MESH


def at_expert(index):
    return {"expert": index}


def at_dp(index):
    return {"dp": index}


def remote(source, target, send_sem, recv_sem, device):
    return pltpu.make_async_remote_copy(
        src_ref=source,
        dst_ref=target,
        send_sem=send_sem,
        recv_sem=recv_sem,
        device_id=device,
        device_id_type=MESH,
    )


def greet(devices):
    barrier = pltpu.get_barrier_semaphore()
    for device in devices:
        pl.semaphore_signal(barrier, inc=1, device_id=device, device_id_type=MESH)
    pl.semaphore_wait(barrier, len(devices))


def neighbours(chips, planes):
    me = lax.axis_index("expert")
    core, chip = lax.rem(me, 2), lax.div(me, 2)
    plane = lax.axis_index("dp")
    ahead = [2 * lax.rem(chip + shift, chips) + core for shift in range(1, chips)]
    behind = [2 * lax.rem(chip + chips - shift, chips) + core for shift in range(1, chips)]
    above = [lax.rem(plane + shift, planes) for shift in range(1, planes)]
    return me, core, chip, plane, me + 1 - 2 * core, ahead, behind, above


def spread_start(piece, me, partner, ahead, sems, lane):
    copies = [remote(piece(me), piece(me), sems.at[0, lane, 0], sems.at[1, lane, 0], at_expert(partner))]
    for shift, peer in enumerate(ahead, 1):
        copies.append(
            remote(piece(me), piece(me), sems.at[0, lane, shift], sems.at[1, lane, shift], at_expert(peer))
        )
    for copy in copies:
        copy.start()
    return copies


def spread_relay(piece, copies, partner, behind, sems, lane):
    relays = []
    for shift, source in enumerate(behind, 1):
        copies[shift].wait_recv()
        relay = remote(
            piece(source), piece(source), sems.at[2, lane, shift], sems.at[3, lane, shift], at_expert(partner)
        )
        relay.start()
        relays.append(relay)
    return relays


def spread_finish(copies, relays):
    copies[0].wait_recv()
    for relay in relays:
        relay.wait_recv()
    for copy in copies + relays:
        copy.wait_send()


def weights_kernel(
    chips, planes, qkv_ref, out_ref, moments_ref, qkv_all, out_all, moments_all, spread_sems, moment_sems, local_sems
):
    me, core, chip, plane, partner, ahead, behind, above = neighbours(chips, planes)
    greet([at_expert(i) for i in [partner] + ahead] + [at_dp(i) for i in above])
    own_copies = [
        pltpu.make_async_copy(qkv_ref, qkv_all.at[me], local_sems.at[0]),
        pltpu.make_async_copy(out_ref, out_all.at[me], local_sems.at[1]),
    ]
    lanes = []
    for lane, (source, target) in enumerate(((qkv_ref, qkv_all), (out_ref, out_all))):
        copies = [
            remote(
                source,
                target.at[me],
                spread_sems.at[0, lane, shift],
                spread_sems.at[1, lane, shift],
                at_expert(peer),
            )
            for shift, peer in enumerate([partner] + ahead)
        ]
        for copy in copies[1:] + copies[:1]:
            copy.start()
        lanes.append((lane, target, copies))
    keepers = (planes // 2 - 1, planes // 2)
    for which, keeper in enumerate(keepers):

        @pl.when(plane != keeper)
        def _():
            remote(
                moments_ref.at[which],
                moments_all.at[plane],
                moment_sems.at[0, which],
                moment_sems.at[1, plane],
                at_dp(keeper),
            ).start()

        @pl.when(plane == keeper)
        def _():
            pltpu.make_async_copy(
                moments_ref.at[which], moments_all.at[plane], local_sems.at[2]
            ).start()

    for copy in own_copies:
        copy.start()
    relayed = [
        (copies, spread_relay(lambda i: target.at[i], copies, partner, behind, spread_sems, lane))
        for lane, target, copies in lanes
    ]
    for copies, relays in relayed:
        spread_finish(copies, relays)
    for copy in own_copies:
        copy.wait()
    for which, keeper in enumerate(keepers):

        @pl.when(plane != keeper)
        def _():
            remote(
                moments_ref.at[which],
                moments_all.at[plane],
                moment_sems.at[0, which],
                moment_sems.at[1, plane],
                at_dp(keeper),
            ).wait_send()

        @pl.when(plane == keeper)
        def _():
            pltpu.make_async_copy(
                moments_ref.at[which], moments_all.at[plane], local_sems.at[2]
            ).wait()
            for source in range(planes):
                if source != keeper:
                    remote(
                        moments_ref.at[which],
                        moments_all.at[source],
                        moment_sems.at[0, which],
                        moment_sems.at[1, source],
                        at_dp(source),
                    ).wait_recv()


def gather_weights(qkv_weight, out_weight, moments):
    members, planes = lax.axis_size("expert"), lax.axis_size("dp")
    chips = members // 2
    anywhere = pl.BlockSpec(memory_space=pl.ANY)
    return pl.pallas_call(
        functools.partial(weights_kernel, chips, planes),
        out_shape=(
            jax.ShapeDtypeStruct((members,) + qkv_weight.shape, jnp.bfloat16),
            jax.ShapeDtypeStruct((members,) + out_weight.shape, jnp.bfloat16),
            jax.ShapeDtypeStruct((planes,) + moments.shape[1:], jnp.bfloat16),
        ),
        in_specs=[anywhere] * 3,
        out_specs=[anywhere] * 3,
        scratch_shapes=[
            pltpu.SemaphoreType.DMA((4, 2, chips)),
            pltpu.SemaphoreType.DMA((2, max(2, planes))),
            pltpu.SemaphoreType.DMA((3,)),
        ],
        compiler_params=pltpu.CompilerParams(collective_id=1, has_side_effects=True),
    )(qkv_weight, out_weight, moments)


def attention_kernel(
    chips,
    planes,
    split,
    qkv_term,
    out_term,
    qkv_moment,
    out_moment,
    small_ref,
    rows_ref,
    first_weight,
    second_weight,
    expert_moment,
    grad_qkv,
    grad_out,
    new_qkv_moment,
    new_out_moment,
    small_out,
    qkv_all,
    out_all,
    expert_grads,
    iterate,
    rows_all,
    hidden,
    expert_total,
    gram,
    mixer,
    crossed,
    leaving,
    landed,
    plane_out,
    plane_in,
    plane_all,
    small_pair,
    small_chip,
    small_plane,
    cross_sems,
    chip_sems,
    plane_sems,
    share_sems,
    spread_sems,
    rows_sems,
    small_sems,
    local_sems,
):
    width = out_term.shape[2]
    lanes = qkv_term.shape[2] // width + 1
    me, core, chip, plane, partner, ahead, behind, above = neighbours(chips, planes)
    greet([at_expert(i) for i in [partner] + ahead] + [at_dp(i) for i in above])

    def cut(pair, lane):
        if lane == lanes - 1:
            return pair[1], pl.ds(0, width)
        return pair[0], pl.ds(lane * width, width)

    def term(lane, index):
        ref, columns = cut((qkv_term, out_term), lane)
        return ref[index, :, columns].astype(jnp.float32)

    order = [lanes - 1] + list(range(lanes - 1))
    crosses = {}
    for lane in order:
        for shift in range(chips):
            target = lax.rem(chip + shift, chips)
            ref, columns = cut((qkv_term, out_term), lane)
            crosses[lane, shift] = remote(
                ref.at[2 * target + 1 - core, :, columns],
                crossed.at[lane, target],
                cross_sems.at[0, lane, shift],
                cross_sems.at[1, lane, shift],
                at_expert(partner),
            )
        for shift in list(range(1, chips)) + [0]:
            crosses[lane, shift].start()
    small_copy = remote(small_ref, small_pair, small_sems.at[0, 0], small_sems.at[1, 0], at_expert(partner))
    small_copy.start()
    sends = list(crosses.values()) + [small_copy]
    rows_copies = [
        remote(rows_ref, rows_all.at[plane], rows_sems.at[0, i], rows_sems.at[1, i], at_dp(peer))
        for i, peer in enumerate(above)
    ]
    own_rows = pltpu.make_async_copy(rows_ref, rows_all.at[plane], local_sems.at[0])
    for copy in rows_copies + [own_rows]:
        copy.start()

    chip_copies = {}

    def to_chips(lane):
        for shift in range(1, chips):
            target = lax.rem(chip + shift, chips)
            crosses[lane, shift].wait_recv()
            leaving[lane, shift - 1] = (
                term(lane, 2 * target + core) + crossed[lane, target].astype(jnp.float32)
            ).astype(jnp.bfloat16)
            copy = remote(
                leaving.at[lane, shift - 1],
                landed.at[lane, shift - 1],
                chip_sems.at[0, lane, shift - 1],
                chip_sems.at[1, lane, shift - 1],
                at_expert(ahead[shift - 1]),
            )
            copy.start()
            chip_copies[lane, shift] = copy
            sends.append(copy)

    small_chip_copies = []

    def small_to_chips():
        small_copy.wait_recv()
        small_chip[chip] = small_ref[...] + small_pair[...]
        for shift, peer in enumerate(ahead, 1):
            copy = remote(
                small_chip.at[chip],
                small_chip.at[chip],
                small_sems.at[0, shift],
                small_sems.at[1, shift],
                at_expert(peer),
            )
            copy.start()
            small_chip_copies.append(copy)
            sends.append(copy)

    small_plane_copies = []

    def small_to_planes():
        for copy in small_chip_copies:
            copy.wait_recv()
        small_plane[plane] = sum(small_chip[i] for i in range(chips))
        for i, peer in enumerate(above):
            copy = remote(
                small_plane.at[plane],
                small_plane.at[plane],
                small_sems.at[0, chips + i],
                small_sems.at[1, chips + i],
                at_dp(peer),
            )
            copy.start()
            small_plane_copies.append(copy)
            sends.append(copy)

    def small_finish():
        for copy in small_plane_copies:
            copy.wait_recv()
        small_out[...] = sum(small_plane[i] for i in range(planes))

    part = plane_out.shape[2]
    plane_copies = {}

    def to_planes(lane):
        crosses[lane, 0].wait_recv()
        total = term(lane, me) + crossed[lane, chip].astype(jnp.float32)
        for shift in range(1, chips):
            chip_copies[lane, shift].wait_recv()
            total = total + landed[lane, shift - 1].astype(jnp.float32)
        if split:
            for i in range(planes):
                plane_out[lane, i] = total[i * part : (i + 1) * part].astype(jnp.bfloat16)
        else:
            plane_in[lane, plane] = total.astype(jnp.bfloat16)
        plane_copies[lane] = []
        for i, peer in enumerate(above):
            copy = remote(
                plane_out.at[lane, peer] if split else plane_in.at[lane, plane],
                plane_in.at[lane, plane],
                plane_sems.at[0, lane, i],
                plane_sems.at[1, lane, i],
                at_dp(peer),
            )
            copy.start()
            plane_copies[lane].append(copy)
            sends.append(copy)

    share_copies = {}

    def share_planes(lane):
        share_copies[lane] = []
        if not split:
            return
        for copy in plane_copies[lane]:
            copy.wait_recv()
        plane_in[lane, plane] = plane_out[lane, plane]
        total = plane_in[lane, 0].astype(jnp.float32)
        for i in range(1, planes):
            total = total + plane_in[lane, i].astype(jnp.float32)
        plane_all[lane, plane] = total.astype(jnp.bfloat16)
        for i, peer in enumerate(above):
            copy = remote(
                plane_all.at[lane, plane],
                plane_all.at[lane, plane],
                share_sems.at[0, lane, i],
                share_sems.at[1, lane, i],
                at_dp(peer),
            )
            copy.start()
            share_copies[lane].append(copy)
            sends.append(copy)

    def piece_of(lane):
        ref, columns = cut((qkv_all, out_all), lane)
        return lambda index: ref.at[index, :, columns]

    spreads, relays = {}, {}

    def make_moment(lane):
        moment, columns = cut((qkv_moment, out_moment), lane)
        grad_target, _ = cut((grad_qkv, grad_out), lane)
        moment_target, _ = cut((new_qkv_moment, new_out_moment), lane)
        whole, _ = cut((qkv_all, out_all), lane)
        if split:
            for copy in share_copies[lane]:
                copy.wait_recv()
            grad = jnp.concatenate(
                [plane_all[lane, i].astype(jnp.float32) for i in range(planes)], axis=0
            )
        else:
            for copy in plane_copies[lane]:
                copy.wait_recv()
            grad = sum(plane_in[lane, i].astype(jnp.float32) for i in range(planes))
        fresh = decay_rate * moment[:, columns] + grad
        grad_target[:, columns] = grad
        moment_target[:, columns] = fresh
        whole[me, :, columns] = fresh.astype(jnp.bfloat16)
        spreads[lane] = spread_start(piece_of(lane), me, partner, ahead, spread_sems, lane)

    def relay(lane):
        relays[lane] = spread_relay(piece_of(lane), spreads[lane], partner, behind, spread_sems, lane)

    depth = first_weight.shape[0]
    units = first_weight.shape[1]
    block, tile = tile_sizes(depth, units)
    which = jnp.where(plane == planes // 2 - 1, 0, 1)
    slots = planes * rows_ref.shape[0]

    def hidden_rows(source):
        @pl.loop(0, units // block)
        def _(index):
            span = pl.ds(pl.multiple_of(index * block, block), block)
            preact = jnp.dot(
                rows_all[source, :, 0:depth], first_weight[:, span], preferred_element_type=jnp.float32
            )
            act_grad = jnp.dot(
                rows_all[source, :, depth : 2 * depth],
                second_weight[:, span],
                preferred_element_type=jnp.float32,
            )
            share = 0.5 * (1.0 + lax.erf(preact * 0.7071067811865476))
            slope = share + preact * jnp.exp(-0.5 * preact * preact) * 0.3989422804014327
            hidden[0, source, :, span] = (act_grad * slope).astype(jnp.bfloat16)
            hidden[1, source, :, span] = (preact * share).astype(jnp.bfloat16)

    def expert_grad(matrix):
        @pl.loop(0, depth // block)
        def _(index):
            columns = pl.ds(pl.multiple_of(matrix * depth + index * block, block), block)
            left = rows_all[:, :, columns].reshape(slots, block)
            target = pl.ds(pl.multiple_of(index * block, block), block)
            for start in range(0, units, tile):
                expert_total[target, start : start + tile] = lax.dot_general(
                    left,
                    hidden[matrix, :, :, start : start + tile].reshape(slots, tile),
                    contract_first,
                    preferred_element_type=jnp.float32,
                )

        share = expert_grads.shape[1]
        own = pl.ds(pl.multiple_of(plane * share, share), share)
        expert_grads[matrix] = expert_total[own, :]

    def add_moment():
        @pl.loop(0, units // tile)
        def _(index):
            span = pl.ds(pl.multiple_of(index * tile, tile), tile)
            expert_total[:, span] = (
                decay_rate * expert_moment[:, span].astype(jnp.float32) + expert_total[:, span]
            )

    begin, make_gram, make_mixer, advance, last_rows = ortho_steps(
        expert_total, block, tile, iterate, gram, mixer
    )

    def ortho_step():
        make_gram()
        make_mixer()
        advance()

    def begin_ortho():
        add_moment()
        begin()

    def visit(number):
        rows_copies[number].wait_recv()
        hidden_rows(lax.rem(plane + planes - 1 - number, planes))

    work = [functools.partial(visit, number) for number in range(planes - 1)]
    work += [functools.partial(expert_grad, 1 - which), functools.partial(expert_grad, which)]
    work += [begin_ortho] + [ortho_step] * NS_STEPS

    for lane in order:
        to_chips(lane)
        if lane == order[0]:
            small_to_chips()
    own_rows.wait()
    hidden_rows(plane)
    stages = [to_planes, share_planes, make_moment, relay]
    for step in range(lanes + len(stages) - 1):
        for number in range(len(stages) - 1, -1, -1):
            if 0 <= step - number < lanes:
                stages[number](order[step - number])
        if step == 0:
            small_to_planes()
        if step >= lanes - 1 and work:
            work.pop(0)()
    small_finish()
    while work:
        work.pop(0)()
    for lane in order:
        spread_finish(spreads[lane], relays[lane])
    for copy in sends:
        copy.wait_send()
    for copy in rows_copies:
        copy.wait_send()


def reduce_attention(
    qkv_term, out_term, qkv_moment, out_moment, small, rows, first_weight, second_weight, expert_moment
):
    members, planes = lax.axis_size("expert"), lax.axis_size("dp")
    chips = members // 2
    share, width = out_moment.shape
    qkv_width = qkv_moment.shape[1]
    lanes = qkv_width // width + 1
    split = share % (8 * planes) == 0
    part = share // planes if split else share
    depth, units = first_weight.shape
    local = pl.BlockSpec(memory_space=pltpu.VMEM)
    dma = pltpu.SemaphoreType.DMA
    wide = jnp.bfloat16
    return pl.pallas_call(
        functools.partial(attention_kernel, chips, planes, split),
        out_shape=(
            jax.ShapeDtypeStruct(qkv_moment.shape, jnp.float32),
            jax.ShapeDtypeStruct(out_moment.shape, jnp.float32),
            jax.ShapeDtypeStruct(qkv_moment.shape, jnp.float32),
            jax.ShapeDtypeStruct(out_moment.shape, jnp.float32),
            jax.ShapeDtypeStruct(small.shape, jnp.float32),
            jax.ShapeDtypeStruct((members, share, qkv_width), wide),
            jax.ShapeDtypeStruct((members, share, width), wide),
            jax.ShapeDtypeStruct((2, depth // planes, units), jnp.float32),
            jax.ShapeDtypeStruct((depth, units), wide),
        ),
        in_specs=[local] * 9,
        out_specs=[local] * 9,
        scratch_shapes=[
            pltpu.VMEM((planes,) + rows.shape, wide),
            pltpu.VMEM((2, planes, rows.shape[0], units), wide),
            pltpu.VMEM((depth, units), jnp.float32),
            pltpu.VMEM((depth, depth), wide),
            pltpu.VMEM((depth, depth), wide),
            pltpu.VMEM((lanes, chips, share, width), wide),
            pltpu.VMEM((lanes, chips - 1, share, width), wide),
            pltpu.VMEM((lanes, chips - 1, share, width), wide),
            pltpu.VMEM((lanes, planes, part, width) if split else (1, 1, part, width), wide),
            pltpu.VMEM((lanes, planes, part, width), wide),
            pltpu.VMEM((lanes, planes, part, width) if split else (1, 1, part, width), wide),
            pltpu.VMEM(small.shape, jnp.float32),
            pltpu.VMEM((chips,) + small.shape, jnp.float32),
            pltpu.VMEM((planes,) + small.shape, jnp.float32),
            dma((2, lanes, chips)),
            dma((2, lanes, chips - 1)),
            dma((2, lanes, planes - 1)),
            dma((2, lanes, planes - 1)),
            dma((4, lanes, chips)),
            dma((2, planes - 1)),
            dma((2, chips + planes - 1)),
            dma((1,)),
        ],
        compiler_params=pltpu.CompilerParams(
            collective_id=2, has_side_effects=True, vmem_limit_bytes=60 << 20
        ),
    )(
        qkv_term,
        out_term,
        qkv_moment,
        out_moment,
        small,
        rows,
        first_weight,
        second_weight,
        expert_moment,
    )


def split_heads(qkv_rows, image_count, head_width):
    shaped = qkv_rows.reshape(image_count, SEQ, 3, HEADS, head_width)
    return (shaped[:, :, 0], shaped[:, :, 1], shaped[:, :, 2])


def attention_scores(query_rows, key_rows, score_scale):
    return (
        jnp.einsum("ishd,ithd->ihst", query_rows, key_rows, preferred_element_type=jnp.float32)
        * score_scale
    )


def body(
    tokens,
    cotangent,
    routes,
    priority,
    ln_gains,
    ln_biases,
    qkv_weight,
    out_weight,
    router,
    w_in,
    w_out,
    norm_momentum,
    router_momentum,
    qkv_momentum,
    out_momentum,
    w_in_momentum,
    w_out_momentum,
):
    token_count, model_width = tokens.shape
    experts = router.shape[1]
    hidden_units = w_in.shape[2]
    capacity = (token_count + experts - 1) // experts
    slots_all = experts * capacity
    dp_share = model_width // lax.axis_size("dp")
    image_count = token_count // SEQ
    head_width = model_width // HEADS
    score_scale = 1.0 / math.sqrt(head_width)
    first_weight = w_in[0]
    second_weight = w_out[0]
    cot_float = cotangent.astype(jnp.float32)
    dp_size = lax.axis_size("dp")
    dp_index = lax.axis_index("dp")
    members = lax.axis_size("expert")
    keep_first, keep_second = (dp_size // 2 - 1, dp_size // 2)
    full_qkv, full_out, every_moment = gather_weights(
        qkv_weight, out_weight, jnp.concatenate([w_in_momentum, w_out_momentum]).astype(jnp.bfloat16)
    )
    full_qkv = full_qkv.reshape(model_width, 3 * model_width)
    full_out = full_out.reshape(model_width, model_width)
    every_moment = every_moment.reshape(model_width, hidden_units)
    token_float = tokens.astype(jnp.float32)
    scaled_one, inverse_one, normed_one = layer_stats(token_float, ln_gains[0], ln_biases[0])
    attn_in = normed_one.astype(jnp.bfloat16)
    qkv_rows = jnp.dot(attn_in, full_qkv, preferred_element_type=jnp.float32).astype(jnp.bfloat16)
    query_rows, key_rows, value_rows = split_heads(qkv_rows, image_count, head_width)
    scores = attention_scores(query_rows, key_rows, score_scale)
    log_total = jnp.log(jnp.sum(jnp.exp(scores), axis=3, keepdims=True))
    attn_probs = jnp.exp(scores - log_total).astype(jnp.bfloat16)
    mixed_rows = (
        jnp.einsum("ihst,ithd->ishd", attn_probs, value_rows, preferred_element_type=jnp.float32)
        .astype(jnp.bfloat16)
        .reshape(token_count, model_width)
    )
    middle_rows = token_float + jnp.dot(mixed_rows, full_out, preferred_element_type=jnp.float32)
    slot_flat = slot_index(routes, priority[0], experts, capacity)
    scaled, inverse, normed = layer_stats(middle_rows, ln_gains[1], ln_biases[1])
    logits = jnp.dot(normed, router, precision=highest)
    gate_values = gates_of(logits, routes)
    position = jnp.arange(slots_all, dtype=jnp.int32)[:, None]
    pick_first = (slot_flat[:, 0][None, :] == position).astype(jnp.float32)
    pick_second = (slot_flat[:, 1][None, :] == position).astype(jnp.float32)
    placing = (pick_first + pick_second).astype(jnp.bfloat16)
    lean_first, lean_second = (pick_first.astype(jnp.bfloat16), pick_second.astype(jnp.bfloat16))
    gated = jnp.concatenate(
        [
            (gate_values[:, 0:1] * cot_float).astype(jnp.bfloat16),
            (gate_values[:, 1:2] * cot_float).astype(jnp.bfloat16),
        ],
        axis=0,
    )
    dispatch = jnp.dot(
        placing, normed.astype(jnp.bfloat16), preferred_element_type=jnp.float32
    ).astype(jnp.bfloat16)
    sent_grad = jnp.dot(
        jnp.concatenate([lean_first, lean_second], axis=1),
        gated,
        preferred_element_type=jnp.float32,
    ).astype(jnp.bfloat16)

    def to_blocks(rows_one, rows_two):
        return jnp.concatenate(
            [
                rows_one.reshape(experts, capacity, model_width),
                rows_two.reshape(experts, capacity, model_width),
            ],
            axis=2,
        )

    arrived = lax.all_to_all(
        to_blocks(dispatch, sent_grad), "expert", split_axis=0, concat_axis=0, tiled=True
    ).reshape(slots_all, 2 * model_width)
    arrived_rows = arrived[:, :model_width]
    grad_rows = arrived[:, model_width:]
    preact_first = jnp.dot(arrived_rows, first_weight, preferred_element_type=jnp.float32)
    active_first = jax.nn.gelu(preact_first, approximate=False).astype(jnp.bfloat16)
    result = lax.dot_general(
        active_first, second_weight, contract_last, preferred_element_type=jnp.float32
    ).astype(jnp.bfloat16)
    act_grad = jnp.dot(grad_rows, second_weight, preferred_element_type=jnp.float32)
    expert_pre_grad = (act_grad * gelu_slope(preact_first)).astype(jnp.bfloat16)
    row_grad = lax.dot_general(
        expert_pre_grad, first_weight, contract_last, preferred_element_type=jnp.float32
    ).astype(jnp.bfloat16)
    returned = lax.all_to_all(
        to_blocks(result, row_grad), "expert", split_axis=0, concat_axis=0, tiled=True
    ).reshape(slots_all, 2 * model_width)
    back_first = lax.dot_general(
        lean_first, returned, contract_first, preferred_element_type=jnp.float32
    )
    back_second = lax.dot_general(
        lean_second, returned, contract_first, preferred_element_type=jnp.float32
    )
    picked_first, picked_second = (back_first[:, :model_width], back_second[:, :model_width])
    block_out = middle_rows + (
        gate_values[:, 0:1] * picked_first + gate_values[:, 1:2] * picked_second
    )
    grad_gap = jnp.sum(picked_first * cot_float, axis=1) - jnp.sum(picked_second * cot_float, axis=1)
    logit_step = gate_values[:, 0] * gate_values[:, 1] * grad_gap
    columns = jnp.arange(experts, dtype=jnp.int32)[None, :]
    logit_grad = (
        (routes[:, 0:1] == columns).astype(jnp.float32)
        - (routes[:, 1:2] == columns).astype(jnp.float32)
    ) * logit_step[:, None]
    gathered = back_first[:, model_width:] + back_second[:, model_width:]
    normed_grad = gathered + lax.dot_general(
        logit_grad, router, contract_last, precision=highest
    )
    router_local = lax.dot_general(normed, logit_grad, contract_first, precision=highest)
    middle_grad = input_grad(cot_float, normed_grad, scaled, inverse, ln_gains[1])
    middle_rounded = middle_grad.astype(jnp.bfloat16)
    mixed_grad = lax.dot_general(
        middle_rounded, full_out, contract_last, preferred_element_type=jnp.float32
    ).astype(jnp.bfloat16)
    scores_again = attention_scores(query_rows, key_rows, score_scale)
    probs_again = jnp.exp(scores_again - log_total).astype(jnp.bfloat16)
    grad_heads = mixed_grad.reshape(image_count, SEQ, HEADS, head_width)
    value_grad = jnp.einsum(
        "ihst,ishd->ithd", probs_again, grad_heads, preferred_element_type=jnp.float32
    )
    prob_grad = jnp.einsum(
        "ishd,ithd->ihst", grad_heads, value_rows, preferred_element_type=jnp.float32
    )
    prob_float = probs_again.astype(jnp.float32)
    row_delta = jnp.sum(prob_float * prob_grad, axis=3, keepdims=True)
    score_grad = (prob_float * (prob_grad - row_delta) * score_scale).astype(jnp.bfloat16)
    query_grad = jnp.einsum(
        "ihst,ithd->ishd", score_grad, key_rows, preferred_element_type=jnp.float32
    )
    key_grad = jnp.einsum(
        "ihst,ishd->ithd", score_grad, query_rows, preferred_element_type=jnp.float32
    )
    qkv_grad = (
        jnp.stack([query_grad, key_grad, value_grad], axis=2)
        .astype(jnp.bfloat16)
        .reshape(token_count, 3 * model_width)
    )
    attn_in_grad = lax.dot_general(
        qkv_grad, full_qkv, contract_last, preferred_element_type=jnp.float32
    )
    grad_tokens = input_grad(middle_grad, attn_in_grad, scaled_one, inverse_one, ln_gains[0])
    qkv_term = lax.dot_general(
        attn_in, qkv_grad, contract_first, preferred_element_type=jnp.float32
    )
    out_term = lax.dot_general(
        mixed_rows, middle_rounded, contract_first, preferred_element_type=jnp.float32
    )
    norm_local = jnp.stack(
        [
            jnp.sum(attn_in_grad * scaled_one, axis=0),
            jnp.sum(normed_grad * scaled, axis=0),
            jnp.sum(attn_in_grad, axis=0),
            jnp.sum(normed_grad, axis=0),
        ]
    )
    small = jnp.concatenate([router_local.T, norm_local], axis=0)
    small_rows = experts + 4
    slot_pad = -slots_all % 16
    (
        grad_qkv,
        grad_out,
        moment_qkv,
        moment_out,
        small_total,
        whole_qkv,
        whole_out,
        expert_grads,
        iter_whole,
    ) = reduce_attention(
        qkv_term.astype(jnp.bfloat16).reshape(members, -1, 3 * model_width),
        out_term.astype(jnp.bfloat16).reshape(members, -1, model_width),
        qkv_momentum,
        out_momentum,
        jnp.pad(small, ((0, -small_rows % 8), (0, 0))),
        jnp.pad(arrived, ((0, slot_pad), (0, 0))),
        first_weight,
        second_weight,
        every_moment,
    )
    whole_qkv = whole_qkv.reshape(model_width, 3 * model_width)
    whole_out = whole_out.reshape(model_width, model_width)
    grad_router = small_total[:experts].T
    grad_norm = small_total[experts:small_rows]
    row_base = dp_index * dp_share
    grad_first, grad_second = (expert_grads[0], expert_grads[1])
    moment_first = decay_rate * w_in_momentum[0] + grad_first
    moment_second = decay_rate * w_out_momentum[0] + grad_second
    iter_slices = [
        lax.dynamic_slice_in_dim(iter_whole, ((dp_index + i) % dp_size) * dp_share, dp_share, 0)
        for i in range(dp_size)
    ]
    iter_first, iter_second = (iter_slices[0], iter_slices[0])
    for shift in range(1, dp_size):
        received = lax.ppermute(
            iter_slices[shift],
            "dp",
            [(i, (i + shift) % dp_size) for i in (keep_first, keep_second)],
        )
        iter_first = jnp.where(dp_index == (keep_first + shift) % dp_size, received, iter_first)
        iter_second = jnp.where(dp_index == (keep_second + shift) % dp_size, received, iter_second)
    expert_share = qkv_weight.shape[0]
    expert_base = lax.axis_index("expert") * expert_share
    iter_out = ortho_rows(whole_out, expert_base, expert_share)
    iter_qkv = ortho_rows(whole_qkv, expert_base, expert_share)
    new_norm_momentum = decay_rate * norm_momentum + grad_norm
    new_norm = jnp.concatenate([ln_gains, ln_biases], axis=0) - norm_rate * new_norm_momentum
    new_router_momentum = decay_rate * router_momentum + grad_router
    new_router = router - matrix_rate * ortho_tall(new_router_momentum).astype(jnp.float32)

    rows_first = lax.dynamic_slice_in_dim(first_weight, row_base, dp_share, 0).astype(jnp.float32)
    rows_second = lax.dynamic_slice_in_dim(second_weight, row_base, dp_share, 0).astype(jnp.float32)
    widen_factor = math.sqrt(max(1.0, hidden_units / model_width))
    new_first = rows_first - matrix_rate * widen_factor * iter_first.astype(jnp.float32)
    new_second = rows_second - matrix_rate * iter_second.astype(jnp.float32)
    new_qkv = qkv_weight.astype(jnp.float32) - matrix_rate * math.sqrt(3.0) * iter_qkv.astype(
        jnp.float32
    )
    new_out = out_weight.astype(jnp.float32) - matrix_rate * iter_out.astype(jnp.float32)
    return (
        block_out,
        grad_tokens,
        grad_norm,
        grad_router,
        grad_qkv,
        grad_out,
        grad_first[None],
        grad_second[None],
        new_norm,
        new_norm_momentum,
        new_router,
        new_router_momentum,
        new_qkv,
        moment_qkv,
        new_out,
        moment_out,
        new_first[None],
        moment_first[None],
        new_second[None],
        moment_second[None],
    )


def solution(mesh):
    in_specs = (
        P(("dp", "expert"), None),
        P(("dp", "expert"), None),
        P(("dp", "expert"), None),
        P(("dp", "expert"), None),
        P(),
        P(),
        P("expert", None),
        P("expert", None),
        P(),
        P("expert", None, None),
        P("expert", None, None),
        P(),
        P(),
        P("expert", None),
        P("expert", None),
        P("expert", "dp", None),
        P("expert", "dp", None),
    )
    out_specs = (
        P(("dp", "expert"), None),
        P(("dp", "expert"), None),
        P(),
        P(),
        P("expert", None),
        P("expert", None),
        P("expert", "dp", None),
        P("expert", "dp", None),
        P(),
        P(),
        P(),
        P(),
        P("expert", None),
        P("expert", None),
        P("expert", None),
        P("expert", None),
        P("expert", "dp", None),
        P("expert", "dp", None),
        P("expert", "dp", None),
        P("expert", "dp", None),
    )
    return jax.shard_map(body, mesh=mesh, in_specs=in_specs, out_specs=out_specs, check_vma=False)
```

```python
import functools
import math

import jax
import jax.numpy as jnp
from jax import lax
from jax.experimental import pallas as pl
from jax.experimental.pallas import tpu as pltpu
from jax.sharding import PartitionSpec as P

HEADS = 12
NS_STEPS = 5
SEQ = 197


quintic_one = 3.4445
quintic_two = -4.775
quintic_three = 2.0315
decay_rate = 0.9
matrix_rate = 0.2
norm_rate = 0.004
norm_eps = 1e-06
frob_eps = 1e-07
highest = lax.Precision.HIGHEST
contract_last = (((1,), (1,)), ((), ()))
contract_first = (((0,), (0,)), ((), ()))


def gelu_slope(preact):
    return (
        0.5 * (1.0 + lax.erf(preact * 0.7071067811865476))
        + preact * jnp.exp(-0.5 * preact * preact) * 0.3989422804014327
    )


def layer_stats(token_rows, gain, bias):
    centre = token_rows - jnp.mean(token_rows, axis=-1, keepdims=True)
    inverse = lax.rsqrt(jnp.mean(centre * centre, axis=-1, keepdims=True) + norm_eps)
    scaled = centre * inverse
    return (scaled, inverse, scaled * gain + bias)


def slot_index(choice_ids, order_rows, experts, capacity):
    token_count = choice_ids.shape[0]
    ranks = jnp.arange(token_count, dtype=jnp.int32)
    turn = jnp.sum(
        jnp.where(order_rows[:, None] == ranks[None, :], ranks[:, None], 0), axis=0, dtype=jnp.int32
    )
    earlier = (turn[None, :] < turn[:, None]).astype(jnp.bfloat16)
    columns = jnp.arange(experts, dtype=jnp.int32)[None, :]
    first = (choice_ids[:, 0:1] == columns).astype(jnp.bfloat16)
    second = (choice_ids[:, 1:2] == columns).astype(jnp.bfloat16)
    counts = jnp.dot(
        earlier, jnp.concatenate([first, second], axis=1), preferred_element_type=jnp.float32
    )
    first_float, second_float = first.astype(jnp.float32), second.astype(jnp.float32)
    first_slot = jnp.sum(counts[:, :experts] * first_float, axis=1)
    second_slot = jnp.sum(
        (counts[:, experts:] + jnp.sum(first_float, axis=0, keepdims=True)) * second_float, axis=1
    )
    slot_values = jnp.stack([first_slot, second_slot], axis=1).astype(jnp.int32)
    return jnp.where(
        slot_values < capacity, choice_ids * capacity + slot_values, experts * capacity
    )


def gates_of(logits, choice_ids):
    columns = jnp.arange(logits.shape[1], dtype=jnp.int32)[None, :]
    first_logit = jnp.sum(jnp.where(choice_ids[:, 0:1] == columns, logits, 0.0), axis=1)
    second_logit = jnp.sum(jnp.where(choice_ids[:, 1:2] == columns, logits, 0.0), axis=1)
    first_gate = jax.nn.sigmoid(first_logit - second_logit)
    return jnp.stack([first_gate, 1.0 - first_gate], axis=1)


def input_grad(base_grad, normed_grad, scaled, inverse, gain):
    lifted = normed_grad * gain
    centred = (
        lifted
        - jnp.mean(lifted, axis=-1, keepdims=True)
        - scaled * jnp.mean(lifted * scaled, axis=-1, keepdims=True)
    )
    return base_grad + inverse * centred


def ortho_tall(matrix):
    iterate = (matrix / (jnp.sqrt(jnp.sum(matrix * matrix)) + frob_eps)).astype(jnp.bfloat16)
    for iteration in range(NS_STEPS):
        gram_matrix = lax.dot_general(
            iterate, iterate, contract_first, preferred_element_type=jnp.float32
        ).astype(jnp.bfloat16)
        mixer_matrix = (
            quintic_two * gram_matrix.astype(jnp.float32)
            + quintic_three * jnp.dot(gram_matrix, gram_matrix, preferred_element_type=jnp.float32)
        ).astype(jnp.bfloat16)
        iterate = (
            quintic_one * iterate.astype(jnp.float32)
            + jnp.dot(iterate, mixer_matrix, preferred_element_type=jnp.float32)
        ).astype(jnp.bfloat16)
    return iterate


def ortho_steps(read, block, tile, iterate, gram, mixer):
    rows, cols = iterate.shape
    tiles = cols // tile

    def begin():
        def squares(index, total):
            part = read(pl.ds(pl.multiple_of(index * tile, tile), tile))
            return total + jnp.sum(part * part, axis=0, keepdims=True)

        total = lax.fori_loop(0, tiles, squares, jnp.zeros((1, tile), jnp.float32))
        norm = jnp.sqrt(jnp.sum(total)) + frob_eps

        @pl.loop(0, tiles)
        def _(index):
            span = pl.ds(pl.multiple_of(index * tile, tile), tile)
            iterate[:, span] = (read(span) / norm).astype(jnp.bfloat16)

    def mirror(target, part, index):
        target[index * block : (index + 1) * block, 0 : (index + 1) * block] = part
        for other in range(index):
            target[other * block : (other + 1) * block, index * block : (index + 1) * block] = part[
                :, other * block : (other + 1) * block
            ].T

    def make_gram():
        for index in range(rows // block):
            mirror(
                gram,
                lax.dot_general(
                    iterate[index * block : (index + 1) * block, :],
                    iterate[0 : (index + 1) * block, :],
                    contract_last,
                    preferred_element_type=jnp.float32,
                ).astype(jnp.bfloat16),
                index,
            )

    def mix(gram_rows, gram_part, gram_columns):
        return (
            quintic_two * gram_part.astype(jnp.float32)
            + quintic_three * jnp.dot(gram_rows, gram_columns, preferred_element_type=jnp.float32)
        ).astype(jnp.bfloat16)

    def apply(mixer_rows, part, columns):
        return (
            quintic_one * part.astype(jnp.float32)
            + jnp.dot(mixer_rows, columns, preferred_element_type=jnp.float32)
        ).astype(jnp.bfloat16)

    def make_mixer():
        for index in range(rows // block):
            span = pl.ds(index * block, block)
            reach = (index + 1) * block
            mirror(mixer, mix(gram[span, :], gram[span, 0:reach], gram[:, 0:reach]), index)

    def advance():
        @pl.loop(0, tiles)
        def _(index):
            span = pl.ds(pl.multiple_of(index * tile, tile), tile)
            columns = iterate[:, span]
            iterate[:, span] = apply(mixer[...], columns, columns)

    def last_rows(own, row_count, out_ref):
        mixer[0:row_count, :] = mix(gram[own, :], gram[own, :], gram[...])

        @pl.loop(0, tiles)
        def _(index):
            span = pl.ds(pl.multiple_of(index * tile, tile), tile)
            out_ref[:, span] = apply(mixer[0:row_count, :], iterate[own, span], iterate[:, span])

    return begin, make_gram, make_mixer, advance, last_rows


def tile_sizes(rows, cols):
    block = next(size for size in (256, 128, rows) if rows % size == 0)
    tile = next(size for size in (768, 512, 256, 128, cols) if cols % size == 0)
    return block, tile


MESH = pl.DeviceIdType.MESH


def at_expert(index):
    return {"expert": index}


def at_dp(index):
    return {"dp": index}


def remote(source, target, send_sem, recv_sem, device):
    return pltpu.make_async_remote_copy(
        src_ref=source,
        dst_ref=target,
        send_sem=send_sem,
        recv_sem=recv_sem,
        device_id=device,
        device_id_type=MESH,
    )


def greet(devices):
    barrier = pltpu.get_barrier_semaphore()
    for device in devices:
        pl.semaphore_signal(barrier, inc=1, device_id=device, device_id_type=MESH)
    pl.semaphore_wait(barrier, len(devices))


def neighbours(chips, planes):
    me = lax.axis_index("expert")
    core, chip = lax.rem(me, 2), lax.div(me, 2)
    plane = lax.axis_index("dp")
    ahead = [2 * lax.rem(chip + shift, chips) + core for shift in range(1, chips)]
    behind = [2 * lax.rem(chip + chips - shift, chips) + core for shift in range(1, chips)]
    above = [lax.rem(plane + shift, planes) for shift in range(1, planes)]
    return me, core, chip, plane, me + 1 - 2 * core, ahead, behind, above


def spread_start(piece, me, partner, ahead, sems, lane):
    copies = [remote(piece(me), piece(me), sems.at[0, lane, 0], sems.at[1, lane, 0], at_expert(partner))]
    for shift, peer in enumerate(ahead, 1):
        copies.append(
            remote(piece(me), piece(me), sems.at[0, lane, shift], sems.at[1, lane, shift], at_expert(peer))
        )
    for copy in copies:
        copy.start()
    return copies


def spread_relay(piece, copies, partner, behind, sems, lane):
    relays = []
    for shift, source in enumerate(behind, 1):
        copies[shift].wait_recv()
        relay = remote(
            piece(source), piece(source), sems.at[2, lane, shift], sems.at[3, lane, shift], at_expert(partner)
        )
        relay.start()
        relays.append(relay)
    return relays


def spread_finish(copies, relays):
    copies[0].wait_recv()
    for relay in relays:
        relay.wait_recv()
    for copy in copies + relays:
        copy.wait_send()


def weights_kernel(
    chips, planes, qkv_ref, out_ref, moments_ref, qkv_all, out_all, moments_all, spread_sems, moment_sems, local_sems
):
    me, core, chip, plane, partner, ahead, behind, above = neighbours(chips, planes)
    greet([at_expert(i) for i in [partner] + ahead] + [at_dp(i) for i in above])
    own_copies = [
        pltpu.make_async_copy(qkv_ref, qkv_all.at[me], local_sems.at[0]),
        pltpu.make_async_copy(out_ref, out_all.at[me], local_sems.at[1]),
    ]
    lanes = []
    for lane, (source, target) in enumerate(((qkv_ref, qkv_all), (out_ref, out_all))):
        copies = [
            remote(
                source,
                target.at[me],
                spread_sems.at[0, lane, shift],
                spread_sems.at[1, lane, shift],
                at_expert(peer),
            )
            for shift, peer in enumerate([partner] + ahead)
        ]
        for copy in copies[1:] + copies[:1]:
            copy.start()
        lanes.append((lane, target, copies))
    keepers = (planes // 2 - 1, planes // 2)
    for which, keeper in enumerate(keepers):

        @pl.when(plane != keeper)
        def _():
            remote(
                moments_ref.at[which],
                moments_all.at[plane],
                moment_sems.at[0, which],
                moment_sems.at[1, plane],
                at_dp(keeper),
            ).start()

        @pl.when(plane == keeper)
        def _():
            pltpu.make_async_copy(
                moments_ref.at[which], moments_all.at[plane], local_sems.at[2]
            ).start()

    for copy in own_copies:
        copy.start()
    relayed = [
        (copies, spread_relay(lambda i: target.at[i], copies, partner, behind, spread_sems, lane))
        for lane, target, copies in lanes
    ]
    for copies, relays in relayed:
        spread_finish(copies, relays)
    for copy in own_copies:
        copy.wait()
    for which, keeper in enumerate(keepers):

        @pl.when(plane != keeper)
        def _():
            remote(
                moments_ref.at[which],
                moments_all.at[plane],
                moment_sems.at[0, which],
                moment_sems.at[1, plane],
                at_dp(keeper),
            ).wait_send()

        @pl.when(plane == keeper)
        def _():
            pltpu.make_async_copy(
                moments_ref.at[which], moments_all.at[plane], local_sems.at[2]
            ).wait()
            for source in range(planes):
                if source != keeper:
                    remote(
                        moments_ref.at[which],
                        moments_all.at[source],
                        moment_sems.at[0, which],
                        moment_sems.at[1, source],
                        at_dp(source),
                    ).wait_recv()


def gather_weights(qkv_weight, out_weight, moments):
    members, planes = lax.axis_size("expert"), lax.axis_size("dp")
    chips = members // 2
    anywhere = pl.BlockSpec(memory_space=pl.ANY)
    return pl.pallas_call(
        functools.partial(weights_kernel, chips, planes),
        out_shape=(
            jax.ShapeDtypeStruct((members,) + qkv_weight.shape, jnp.bfloat16),
            jax.ShapeDtypeStruct((members,) + out_weight.shape, jnp.bfloat16),
            jax.ShapeDtypeStruct((planes,) + moments.shape[1:], jnp.bfloat16),
        ),
        in_specs=[anywhere] * 3,
        out_specs=[anywhere] * 3,
        scratch_shapes=[
            pltpu.SemaphoreType.DMA((4, 2, chips)),
            pltpu.SemaphoreType.DMA((2, max(2, planes))),
            pltpu.SemaphoreType.DMA((3,)),
        ],
        compiler_params=pltpu.CompilerParams(collective_id=1, has_side_effects=True),
    )(qkv_weight, out_weight, moments)


def attention_kernel(
    chips,
    planes,
    split,
    qkv_term,
    out_term,
    qkv_moment,
    out_moment,
    small_ref,
    rows_ref,
    first_weight,
    second_weight,
    expert_moment,
    grad_qkv,
    grad_out,
    new_qkv_moment,
    new_out_moment,
    small_out,
    iter_qkv,
    iter_out,
    expert_grads,
    iter_expert,
    qkv_all,
    out_all,
    iterate,
    wide_iterate,
    rows_all,
    hidden,
    expert_total,
    gram,
    mixer,
    crossed,
    leaving,
    landed,
    plane_out,
    plane_in,
    plane_all,
    small_pair,
    small_chip,
    small_plane,
    cross_sems,
    chip_sems,
    plane_sems,
    share_sems,
    spread_sems,
    rows_sems,
    small_sems,
    iter_sems,
    local_sems,
):
    width = out_term.shape[2]
    lanes = qkv_term.shape[2] // width + 1
    me, core, chip, plane, partner, ahead, behind, above = neighbours(chips, planes)
    greet([at_expert(i) for i in [partner] + ahead] + [at_dp(i) for i in above])

    def cut(pair, lane):
        if lane == lanes - 1:
            return pair[1], pl.ds(0, width)
        return pair[0], pl.ds(lane * width, width)

    def term(lane, index):
        ref, columns = cut((qkv_term, out_term), lane)
        return ref[index, :, columns].astype(jnp.float32)

    order = [lanes - 1] + list(range(lanes - 1))
    crosses = {}
    for lane in order:
        for shift in range(chips):
            target = lax.rem(chip + shift, chips)
            ref, columns = cut((qkv_term, out_term), lane)
            crosses[lane, shift] = remote(
                ref.at[2 * target + 1 - core, :, columns],
                crossed.at[lane, target],
                cross_sems.at[0, lane, shift],
                cross_sems.at[1, lane, shift],
                at_expert(partner),
            )
        for shift in list(range(1, chips)) + [0]:
            crosses[lane, shift].start()
    small_copy = remote(small_ref, small_pair, small_sems.at[0, 0], small_sems.at[1, 0], at_expert(partner))
    small_copy.start()
    sends = list(crosses.values()) + [small_copy]
    rows_copies = [
        remote(rows_ref, rows_all.at[plane], rows_sems.at[0, i], rows_sems.at[1, i], at_dp(peer))
        for i, peer in enumerate(above)
    ]
    own_rows = pltpu.make_async_copy(rows_ref, rows_all.at[plane], local_sems.at[0])
    moment_copy = pltpu.make_async_copy(expert_moment, iterate, local_sems.at[1])
    for copy in rows_copies + [own_rows, moment_copy]:
        copy.start()

    chip_copies = {}

    def to_chips(lane):
        for shift in range(1, chips):
            target = lax.rem(chip + shift, chips)
            crosses[lane, shift].wait_recv()
            leaving[lane, shift - 1] = (
                term(lane, 2 * target + core) + crossed[lane, target].astype(jnp.float32)
            ).astype(jnp.bfloat16)
            copy = remote(
                leaving.at[lane, shift - 1],
                landed.at[lane, shift - 1],
                chip_sems.at[0, lane, shift - 1],
                chip_sems.at[1, lane, shift - 1],
                at_expert(ahead[shift - 1]),
            )
            copy.start()
            chip_copies[lane, shift] = copy
            sends.append(copy)

    small_chip_copies = []

    def small_to_chips():
        small_copy.wait_recv()
        small_chip[chip] = small_ref[...] + small_pair[...]
        for shift, peer in enumerate(ahead, 1):
            copy = remote(
                small_chip.at[chip],
                small_chip.at[chip],
                small_sems.at[0, shift],
                small_sems.at[1, shift],
                at_expert(peer),
            )
            copy.start()
            small_chip_copies.append(copy)
            sends.append(copy)

    small_plane_copies = []

    def small_to_planes():
        for copy in small_chip_copies:
            copy.wait_recv()
        small_plane[plane] = sum(small_chip[i] for i in range(chips))
        for i, peer in enumerate(above):
            copy = remote(
                small_plane.at[plane],
                small_plane.at[plane],
                small_sems.at[0, chips + i],
                small_sems.at[1, chips + i],
                at_dp(peer),
            )
            copy.start()
            small_plane_copies.append(copy)
            sends.append(copy)

    def small_finish():
        for copy in small_plane_copies:
            copy.wait_recv()
        small_out[...] = sum(small_plane[i] for i in range(planes))

    part = plane_out.shape[2]
    plane_copies = {}

    def to_planes(lane):
        crosses[lane, 0].wait_recv()
        total = term(lane, me) + crossed[lane, chip].astype(jnp.float32)
        for shift in range(1, chips):
            chip_copies[lane, shift].wait_recv()
            total = total + landed[lane, shift - 1].astype(jnp.float32)
        if split:
            for i in range(planes):
                plane_out[lane, i] = total[i * part : (i + 1) * part].astype(jnp.bfloat16)
        else:
            plane_in[lane, plane] = total.astype(jnp.bfloat16)
        plane_copies[lane] = []
        for i, peer in enumerate(above):
            copy = remote(
                plane_out.at[lane, peer] if split else plane_in.at[lane, plane],
                plane_in.at[lane, plane],
                plane_sems.at[0, lane, i],
                plane_sems.at[1, lane, i],
                at_dp(peer),
            )
            copy.start()
            plane_copies[lane].append(copy)
            sends.append(copy)

    share_copies = {}

    def share_planes(lane):
        share_copies[lane] = []
        if not split:
            return
        for copy in plane_copies[lane]:
            copy.wait_recv()
        plane_in[lane, plane] = plane_out[lane, plane]
        total = plane_in[lane, 0].astype(jnp.float32)
        for i in range(1, planes):
            total = total + plane_in[lane, i].astype(jnp.float32)
        plane_all[lane, plane] = total.astype(jnp.bfloat16)
        for i, peer in enumerate(above):
            copy = remote(
                plane_all.at[lane, plane],
                plane_all.at[lane, plane],
                share_sems.at[0, lane, i],
                share_sems.at[1, lane, i],
                at_dp(peer),
            )
            copy.start()
            share_copies[lane].append(copy)
            sends.append(copy)

    def piece_of(lane):
        ref, columns = cut((qkv_all, out_all), lane)
        return lambda index: ref.at[index, :, columns]

    spreads, relays = {}, {}

    def make_moment(lane):
        moment, columns = cut((qkv_moment, out_moment), lane)
        grad_target, _ = cut((grad_qkv, grad_out), lane)
        moment_target, _ = cut((new_qkv_moment, new_out_moment), lane)
        whole, _ = cut((qkv_all, out_all), lane)
        if split:
            for copy in share_copies[lane]:
                copy.wait_recv()
            grad = jnp.concatenate(
                [plane_all[lane, i].astype(jnp.float32) for i in range(planes)], axis=0
            )
        else:
            for copy in plane_copies[lane]:
                copy.wait_recv()
            grad = sum(plane_in[lane, i].astype(jnp.float32) for i in range(planes))
        fresh = decay_rate * moment[:, columns] + grad
        grad_target[:, columns] = grad
        moment_target[:, columns] = fresh
        whole[me, :, columns] = fresh.astype(jnp.bfloat16)
        spreads[lane] = spread_start(piece_of(lane), me, partner, ahead, spread_sems, lane)

    def relay(lane):
        relays[lane] = spread_relay(piece_of(lane), spreads[lane], partner, behind, spread_sems, lane)

    depth = first_weight.shape[0]
    units = first_weight.shape[1]
    block, tile = tile_sizes(depth, units)
    which = jnp.where(plane == planes // 2 - 1, 0, 1)
    slots = planes * rows_ref.shape[0]

    def hidden_rows(source):
        @pl.loop(0, units // block)
        def _(index):
            span = pl.ds(pl.multiple_of(index * block, block), block)
            preact = jnp.dot(
                rows_all[source, :, 0:depth], first_weight[:, span], preferred_element_type=jnp.float32
            )
            act_grad = jnp.dot(
                rows_all[source, :, depth : 2 * depth],
                second_weight[:, span],
                preferred_element_type=jnp.float32,
            )
            share = 0.5 * (1.0 + lax.erf(preact * 0.7071067811865476))
            slope = share + preact * jnp.exp(-0.5 * preact * preact) * 0.3989422804014327
            hidden[0, source, :, span] = (act_grad * slope).astype(jnp.bfloat16)
            hidden[1, source, :, span] = (preact * share).astype(jnp.bfloat16)

    def expert_grad(matrix):
        @pl.loop(0, depth // block)
        def _(index):
            columns = pl.ds(pl.multiple_of(matrix * depth + index * block, block), block)
            left = rows_all[:, :, columns].reshape(slots, block)
            target = pl.ds(pl.multiple_of(index * block, block), block)
            for start in range(0, units, tile):
                expert_total[target, start : start + tile] = lax.dot_general(
                    left,
                    hidden[matrix, :, :, start : start + tile].reshape(slots, tile),
                    contract_first,
                    preferred_element_type=jnp.float32,
                )

        share = expert_grads.shape[1]
        own = pl.ds(pl.multiple_of(plane * share, share), share)
        expert_grads[matrix] = expert_total[own, :]

    def add_moment():
        moment_copy.wait()

        @pl.loop(0, units // tile)
        def _(index):
            span = pl.ds(pl.multiple_of(index * tile, tile), tile)
            expert_total[:, span] = (
                decay_rate * iterate[:, span].astype(jnp.float32) + expert_total[:, span]
            )

    begin, make_gram, make_mixer, advance, last_rows = ortho_steps(
        lambda span: expert_total[:, span], block, tile, iterate, gram, mixer
    )

    def ortho_step():
        make_gram()
        make_mixer()
        advance()

    def begin_ortho():
        add_moment()
        begin()

    def visit(number):
        rows_copies[number].wait_recv()
        hidden_rows(lax.rem(plane + planes - 1 - number, planes))

    work = [functools.partial(visit, number) for number in range(planes - 1)]
    work += [functools.partial(expert_grad, 1 - which), functools.partial(expert_grad, which)]
    work += [begin_ortho] + [ortho_step] * NS_STEPS

    expert_share = expert_grads.shape[1]
    keepers = (planes // 2 - 1, planes // 2)

    def iter_copy(keeper, matrix, shift, peer):
        own = pl.ds(pl.multiple_of(peer * expert_share, expert_share), expert_share)
        return remote(
            iterate.at[own, :],
            iter_expert.at[matrix],
            iter_sems.at[0, shift],
            iter_sems.at[1, matrix],
            at_dp(peer),
        )

    def send_iterates():
        for matrix, keeper in enumerate(keepers):

            @pl.when(plane == keeper)
            def _():
                for shift, peer in enumerate(above):
                    iter_copy(keeper, matrix, shift, peer).start()
                iter_expert[matrix] = iterate[keeper * expert_share : (keeper + 1) * expert_share, :]

    def await_iterates():
        for matrix, keeper in enumerate(keepers):

            @pl.when(plane == keeper)
            def _():
                for shift, peer in enumerate(above):
                    iter_copy(keeper, matrix, shift, peer).wait_send()

            @pl.when(plane != keeper)
            def _():
                iter_copy(keeper, matrix, 0, plane).wait_recv()

    def attention_ortho(whole, target):
        cols = whole.shape[2]
        chunk = tile_sizes(depth, cols)[1]
        start, build_gram, build_mixer, step_on, last = ortho_steps(
            lambda span: whole[:, :, span].astype(jnp.float32).reshape(depth, chunk),
            block,
            chunk,
            wide_iterate.at[:, 0:cols],
            gram,
            mixer,
        )
        start()

        @pl.loop(0, NS_STEPS - 1)
        def _(step):
            build_gram()
            build_mixer()
            step_on()

        build_gram()
        kept = target.shape[0]
        if kept == depth:
            own = pl.ds(0, depth)
        else:
            own = pl.ds(pl.multiple_of(me * kept, kept), kept)
        last(own, kept, target)

    work += [send_iterates]

    for lane in order:
        to_chips(lane)
        if lane == order[0]:
            small_to_chips()
    own_rows.wait()
    hidden_rows(plane)
    stages = [to_planes, share_planes, make_moment, relay]
    for step in range(lanes + len(stages) - 1):
        for number in range(len(stages) - 1, -1, -1):
            if 0 <= step - number < lanes:
                stages[number](order[step - number])
        if step == 0:
            small_to_planes()
        if step >= lanes - 1:
            work.pop(0)()
    small_finish()
    while work:
        work.pop(0)()
    spread_finish(spreads[order[0]], relays[order[0]])
    attention_ortho(out_all, iter_out)
    for lane in order[1:]:
        spread_finish(spreads[lane], relays[lane])
    attention_ortho(qkv_all, iter_qkv)
    for copy in sends:
        copy.wait_send()
    for copy in rows_copies:
        copy.wait_send()
    await_iterates()


def reduce_attention(
    qkv_term, out_term, qkv_moment, out_moment, small, rows, first_weight, second_weight, expert_moment
):
    members, planes = lax.axis_size("expert"), lax.axis_size("dp")
    chips = members // 2
    share, width = out_moment.shape
    qkv_width = qkv_moment.shape[1]
    lanes = qkv_width // width + 1
    split = share % (8 * planes) == 0
    part = share // planes if split else share
    depth, units = first_weight.shape
    kept = share if share % 16 == 0 else depth
    local = pl.BlockSpec(memory_space=pltpu.VMEM)
    dma = pltpu.SemaphoreType.DMA
    wide = jnp.bfloat16
    return pl.pallas_call(
        functools.partial(attention_kernel, chips, planes, split),
        out_shape=(
            jax.ShapeDtypeStruct(qkv_moment.shape, jnp.float32),
            jax.ShapeDtypeStruct(out_moment.shape, jnp.float32),
            jax.ShapeDtypeStruct(qkv_moment.shape, jnp.float32),
            jax.ShapeDtypeStruct(out_moment.shape, jnp.float32),
            jax.ShapeDtypeStruct(small.shape, jnp.float32),
            jax.ShapeDtypeStruct((kept, qkv_width), wide),
            jax.ShapeDtypeStruct((kept, width), wide),
            jax.ShapeDtypeStruct((2, depth // planes, units), jnp.float32),
            jax.ShapeDtypeStruct((2, depth // planes, units), wide),
        ),
        in_specs=[local] * 8 + [pl.BlockSpec(memory_space=pl.ANY)],
        out_specs=[local] * 9,
        scratch_shapes=[
            pltpu.VMEM((members, share, qkv_width), wide),
            pltpu.VMEM((members, share, width), wide),
            pltpu.VMEM((depth, units), wide),
            pltpu.VMEM((depth, qkv_width), wide),
            pltpu.VMEM((planes,) + rows.shape, wide),
            pltpu.VMEM((2, planes, rows.shape[0], units), wide),
            pltpu.VMEM((depth, units), jnp.float32),
            pltpu.VMEM((depth, depth), wide),
            pltpu.VMEM((depth, depth), wide),
            pltpu.VMEM((lanes, chips, share, width), wide),
            pltpu.VMEM((lanes, chips - 1, share, width), wide),
            pltpu.VMEM((lanes, chips - 1, share, width), wide),
            pltpu.VMEM((lanes, planes, part, width) if split else (1, 1, part, width), wide),
            pltpu.VMEM((lanes, planes, part, width), wide),
            pltpu.VMEM((lanes, planes, part, width) if split else (1, 1, part, width), wide),
            pltpu.VMEM(small.shape, jnp.float32),
            pltpu.VMEM((chips,) + small.shape, jnp.float32),
            pltpu.VMEM((planes,) + small.shape, jnp.float32),
            dma((2, lanes, chips)),
            dma((2, lanes, chips - 1)),
            dma((2, lanes, planes - 1)),
            dma((2, lanes, planes - 1)),
            dma((4, lanes, chips)),
            dma((2, planes - 1)),
            dma((2, chips + planes - 1)),
            dma((2, max(2, planes - 1))),
            dma((2,)),
        ],
        compiler_params=pltpu.CompilerParams(
            collective_id=2, has_side_effects=True, vmem_limit_bytes=63 << 20
        ),
    )(
        qkv_term,
        out_term,
        qkv_moment,
        out_moment,
        small,
        rows,
        first_weight,
        second_weight,
        expert_moment,
    )


def split_heads(qkv_rows, image_count, head_width):
    shaped = qkv_rows.reshape(image_count, SEQ, 3, HEADS, head_width)
    return (shaped[:, :, 0], shaped[:, :, 1], shaped[:, :, 2])


def attention_scores(query_rows, key_rows, score_scale):
    return (
        jnp.einsum("ishd,ithd->ihst", query_rows, key_rows, preferred_element_type=jnp.float32)
        * score_scale
    )


def body(
    tokens,
    cotangent,
    routes,
    priority,
    ln_gains,
    ln_biases,
    qkv_weight,
    out_weight,
    router,
    w_in,
    w_out,
    norm_momentum,
    router_momentum,
    qkv_momentum,
    out_momentum,
    w_in_momentum,
    w_out_momentum,
):
    token_count, model_width = tokens.shape
    experts = router.shape[1]
    hidden_units = w_in.shape[2]
    capacity = (token_count + experts - 1) // experts
    slots_all = experts * capacity
    dp_share = model_width // lax.axis_size("dp")
    image_count = token_count // SEQ
    head_width = model_width // HEADS
    score_scale = 1.0 / math.sqrt(head_width)
    first_weight = w_in[0]
    second_weight = w_out[0]
    cot_float = cotangent.astype(jnp.float32)
    dp_size = lax.axis_size("dp")
    dp_index = lax.axis_index("dp")
    members = lax.axis_size("expert")
    keep_first, keep_second = (dp_size // 2 - 1, dp_size // 2)
    full_qkv, full_out, every_moment = gather_weights(
        qkv_weight, out_weight, jnp.concatenate([w_in_momentum, w_out_momentum]).astype(jnp.bfloat16)
    )
    full_qkv = full_qkv.reshape(model_width, 3 * model_width)
    full_out = full_out.reshape(model_width, model_width)
    every_moment = every_moment.reshape(model_width, hidden_units)
    token_float = tokens.astype(jnp.float32)
    scaled_one, inverse_one, normed_one = layer_stats(token_float, ln_gains[0], ln_biases[0])
    attn_in = normed_one.astype(jnp.bfloat16)
    qkv_rows = jnp.dot(attn_in, full_qkv, preferred_element_type=jnp.float32).astype(jnp.bfloat16)
    query_rows, key_rows, value_rows = split_heads(qkv_rows, image_count, head_width)
    scores = attention_scores(query_rows, key_rows, score_scale)
    log_total = jnp.log(jnp.sum(jnp.exp(scores), axis=3, keepdims=True))
    attn_probs = jnp.exp(scores - log_total).astype(jnp.bfloat16)
    mixed_rows = (
        jnp.einsum("ihst,ithd->ishd", attn_probs, value_rows, preferred_element_type=jnp.float32)
        .astype(jnp.bfloat16)
        .reshape(token_count, model_width)
    )
    middle_rows = token_float + jnp.dot(mixed_rows, full_out, preferred_element_type=jnp.float32)
    slot_flat = slot_index(routes, priority[0], experts, capacity)
    scaled, inverse, normed = layer_stats(middle_rows, ln_gains[1], ln_biases[1])
    logits = jnp.dot(normed, router, precision=highest)
    gate_values = gates_of(logits, routes)
    position = jnp.arange(slots_all, dtype=jnp.int32)[:, None]
    pick_first = (slot_flat[:, 0][None, :] == position).astype(jnp.float32)
    pick_second = (slot_flat[:, 1][None, :] == position).astype(jnp.float32)
    placing = (pick_first + pick_second).astype(jnp.bfloat16)
    lean_first, lean_second = (pick_first.astype(jnp.bfloat16), pick_second.astype(jnp.bfloat16))
    gated = jnp.concatenate(
        [
            (gate_values[:, 0:1] * cot_float).astype(jnp.bfloat16),
            (gate_values[:, 1:2] * cot_float).astype(jnp.bfloat16),
        ],
        axis=0,
    )
    dispatch = jnp.dot(
        placing, normed.astype(jnp.bfloat16), preferred_element_type=jnp.float32
    ).astype(jnp.bfloat16)
    sent_grad = jnp.dot(
        jnp.concatenate([lean_first, lean_second], axis=1),
        gated,
        preferred_element_type=jnp.float32,
    ).astype(jnp.bfloat16)

    def to_blocks(rows_one, rows_two):
        return jnp.concatenate(
            [
                rows_one.reshape(experts, capacity, model_width),
                rows_two.reshape(experts, capacity, model_width),
            ],
            axis=2,
        )

    arrived = lax.all_to_all(
        to_blocks(dispatch, sent_grad), "expert", split_axis=0, concat_axis=0, tiled=True
    ).reshape(slots_all, 2 * model_width)
    arrived_rows = arrived[:, :model_width]
    grad_rows = arrived[:, model_width:]
    preact_first = jnp.dot(arrived_rows, first_weight, preferred_element_type=jnp.float32)
    active_first = jax.nn.gelu(preact_first, approximate=False).astype(jnp.bfloat16)
    result = lax.dot_general(
        active_first, second_weight, contract_last, preferred_element_type=jnp.float32
    ).astype(jnp.bfloat16)
    act_grad = jnp.dot(grad_rows, second_weight, preferred_element_type=jnp.float32)
    expert_pre_grad = (act_grad * gelu_slope(preact_first)).astype(jnp.bfloat16)
    row_grad = lax.dot_general(
        expert_pre_grad, first_weight, contract_last, preferred_element_type=jnp.float32
    ).astype(jnp.bfloat16)
    returned = lax.all_to_all(
        to_blocks(result, row_grad), "expert", split_axis=0, concat_axis=0, tiled=True
    ).reshape(slots_all, 2 * model_width)
    back_first = lax.dot_general(
        lean_first, returned, contract_first, preferred_element_type=jnp.float32
    )
    back_second = lax.dot_general(
        lean_second, returned, contract_first, preferred_element_type=jnp.float32
    )
    picked_first, picked_second = (back_first[:, :model_width], back_second[:, :model_width])
    block_out = middle_rows + (
        gate_values[:, 0:1] * picked_first + gate_values[:, 1:2] * picked_second
    )
    grad_gap = jnp.sum(picked_first * cot_float, axis=1) - jnp.sum(picked_second * cot_float, axis=1)
    logit_step = gate_values[:, 0] * gate_values[:, 1] * grad_gap
    columns = jnp.arange(experts, dtype=jnp.int32)[None, :]
    logit_grad = (
        (routes[:, 0:1] == columns).astype(jnp.float32)
        - (routes[:, 1:2] == columns).astype(jnp.float32)
    ) * logit_step[:, None]
    gathered = back_first[:, model_width:] + back_second[:, model_width:]
    normed_grad = gathered + lax.dot_general(
        logit_grad, router, contract_last, precision=highest
    )
    router_local = lax.dot_general(normed, logit_grad, contract_first, precision=highest)
    middle_grad = input_grad(cot_float, normed_grad, scaled, inverse, ln_gains[1])
    middle_rounded = middle_grad.astype(jnp.bfloat16)
    mixed_grad = lax.dot_general(
        middle_rounded, full_out, contract_last, preferred_element_type=jnp.float32
    ).astype(jnp.bfloat16)
    scores_again = attention_scores(query_rows, key_rows, score_scale)
    probs_again = jnp.exp(scores_again - log_total).astype(jnp.bfloat16)
    grad_heads = mixed_grad.reshape(image_count, SEQ, HEADS, head_width)
    value_grad = jnp.einsum(
        "ihst,ishd->ithd", probs_again, grad_heads, preferred_element_type=jnp.float32
    )
    prob_grad = jnp.einsum(
        "ishd,ithd->ihst", grad_heads, value_rows, preferred_element_type=jnp.float32
    )
    prob_float = probs_again.astype(jnp.float32)
    row_delta = jnp.sum(prob_float * prob_grad, axis=3, keepdims=True)
    score_grad = (prob_float * (prob_grad - row_delta) * score_scale).astype(jnp.bfloat16)
    query_grad = jnp.einsum(
        "ihst,ithd->ishd", score_grad, key_rows, preferred_element_type=jnp.float32
    )
    key_grad = jnp.einsum(
        "ihst,ishd->ithd", score_grad, query_rows, preferred_element_type=jnp.float32
    )
    qkv_grad = (
        jnp.stack([query_grad, key_grad, value_grad], axis=2)
        .astype(jnp.bfloat16)
        .reshape(token_count, 3 * model_width)
    )
    attn_in_grad = lax.dot_general(
        qkv_grad, full_qkv, contract_last, preferred_element_type=jnp.float32
    )
    grad_tokens = input_grad(middle_grad, attn_in_grad, scaled_one, inverse_one, ln_gains[0])
    qkv_term = lax.dot_general(
        attn_in, qkv_grad, contract_first, preferred_element_type=jnp.float32
    )
    out_term = lax.dot_general(
        mixed_rows, middle_rounded, contract_first, preferred_element_type=jnp.float32
    )
    norm_local = jnp.stack(
        [
            jnp.sum(attn_in_grad * scaled_one, axis=0),
            jnp.sum(normed_grad * scaled, axis=0),
            jnp.sum(attn_in_grad, axis=0),
            jnp.sum(normed_grad, axis=0),
        ]
    )
    small = jnp.concatenate([router_local.T, norm_local], axis=0)
    small_rows = experts + 4
    slot_pad = -slots_all % 16
    (
        grad_qkv,
        grad_out,
        moment_qkv,
        moment_out,
        small_total,
        iter_qkv,
        iter_out,
        expert_grads,
        iter_expert,
    ) = reduce_attention(
        qkv_term.astype(jnp.bfloat16).reshape(members, -1, 3 * model_width),
        out_term.astype(jnp.bfloat16).reshape(members, -1, model_width),
        qkv_momentum,
        out_momentum,
        jnp.pad(small, ((0, -small_rows % 8), (0, 0))),
        jnp.pad(arrived, ((0, slot_pad), (0, 0))),
        first_weight,
        second_weight,
        every_moment,
    )
    grad_router = small_total[:experts].T
    grad_norm = small_total[experts:small_rows]
    row_base = dp_index * dp_share
    grad_first, grad_second = (expert_grads[0], expert_grads[1])
    moment_first = decay_rate * w_in_momentum[0] + grad_first
    moment_second = decay_rate * w_out_momentum[0] + grad_second
    iter_first, iter_second = (iter_expert[0], iter_expert[1])
    expert_share = qkv_weight.shape[0]
    if iter_out.shape[0] != expert_share:
        expert_base = lax.axis_index("expert") * expert_share
        iter_out = lax.dynamic_slice_in_dim(iter_out, expert_base, expert_share, 0)
        iter_qkv = lax.dynamic_slice_in_dim(iter_qkv, expert_base, expert_share, 0)
    new_norm_momentum = decay_rate * norm_momentum + grad_norm
    new_norm = jnp.concatenate([ln_gains, ln_biases], axis=0) - norm_rate * new_norm_momentum
    new_router_momentum = decay_rate * router_momentum + grad_router
    new_router = router - matrix_rate * ortho_tall(new_router_momentum).astype(jnp.float32)

    rows_first = lax.dynamic_slice_in_dim(first_weight, row_base, dp_share, 0).astype(jnp.float32)
    rows_second = lax.dynamic_slice_in_dim(second_weight, row_base, dp_share, 0).astype(jnp.float32)
    widen_factor = math.sqrt(max(1.0, hidden_units / model_width))
    new_first = rows_first - matrix_rate * widen_factor * iter_first.astype(jnp.float32)
    new_second = rows_second - matrix_rate * iter_second.astype(jnp.float32)
    new_qkv = qkv_weight.astype(jnp.float32) - matrix_rate * math.sqrt(3.0) * iter_qkv.astype(
        jnp.float32
    )
    new_out = out_weight.astype(jnp.float32) - matrix_rate * iter_out.astype(jnp.float32)
    return (
        block_out,
        grad_tokens,
        grad_norm,
        grad_router,
        grad_qkv,
        grad_out,
        grad_first[None],
        grad_second[None],
        new_norm,
        new_norm_momentum,
        new_router,
        new_router_momentum,
        new_qkv,
        moment_qkv,
        new_out,
        moment_out,
        new_first[None],
        moment_first[None],
        new_second[None],
        moment_second[None],
    )


def solution(mesh):
    in_specs = (
        P(("dp", "expert"), None),
        P(("dp", "expert"), None),
        P(("dp", "expert"), None),
        P(("dp", "expert"), None),
        P(),
        P(),
        P("expert", None),
        P("expert", None),
        P(),
        P("expert", None, None),
        P("expert", None, None),
        P(),
        P(),
        P("expert", None),
        P("expert", None),
        P("expert", "dp", None),
        P("expert", "dp", None),
    )
    out_specs = (
        P(("dp", "expert"), None),
        P(("dp", "expert"), None),
        P(),
        P(),
        P("expert", None),
        P("expert", None),
        P("expert", "dp", None),
        P("expert", "dp", None),
        P(),
        P(),
        P(),
        P(),
        P("expert", None),
        P("expert", None),
        P("expert", None),
        P("expert", None),
        P("expert", "dp", None),
        P("expert", "dp", None),
        P("expert", "dp", None),
        P("expert", "dp", None),
    )
    return jax.shard_map(body, mesh=mesh, in_specs=in_specs, out_specs=out_specs, check_vma=False)
```

```python
import functools
import math

import jax
import jax.numpy as jnp
from jax import lax
from jax.experimental import pallas as pl
from jax.experimental.pallas import tpu as pltpu
from jax.sharding import PartitionSpec as P

HEADS = 12
NS_STEPS = 5
SEQ = 197


quintic_one = 3.4445
quintic_two = -4.775
quintic_three = 2.0315
decay_rate = 0.9
matrix_rate = 0.2
norm_rate = 0.004
norm_eps = 1e-06
frob_eps = 1e-07
highest = lax.Precision.HIGHEST
contract_last = (((1,), (1,)), ((), ()))
contract_first = (((0,), (0,)), ((), ()))


def gelu_slope(preact):
    return (
        0.5 * (1.0 + lax.erf(preact * 0.7071067811865476))
        + preact * jnp.exp(-0.5 * preact * preact) * 0.3989422804014327
    )


def layer_stats(token_rows, gain, bias):
    centre = token_rows - jnp.mean(token_rows, axis=-1, keepdims=True)
    inverse = lax.rsqrt(jnp.mean(centre * centre, axis=-1, keepdims=True) + norm_eps)
    scaled = centre * inverse
    return (scaled, inverse, scaled * gain + bias)


def slot_index(choice_ids, order_rows, experts, capacity, stride):
    token_count = choice_ids.shape[0]
    ranks = jnp.arange(token_count, dtype=jnp.int32)
    turn = jnp.sum(
        jnp.where(order_rows[:, None] == ranks[None, :], ranks[:, None], 0), axis=0, dtype=jnp.int32
    )
    earlier = (turn[None, :] < turn[:, None]).astype(jnp.bfloat16)
    columns = jnp.arange(experts, dtype=jnp.int32)[None, :]
    first = (choice_ids[:, 0:1] == columns).astype(jnp.bfloat16)
    second = (choice_ids[:, 1:2] == columns).astype(jnp.bfloat16)
    counts = jnp.dot(
        earlier, jnp.concatenate([first, second], axis=1), preferred_element_type=jnp.float32
    )
    first_float, second_float = first.astype(jnp.float32), second.astype(jnp.float32)
    first_slot = jnp.sum(counts[:, :experts] * first_float, axis=1)
    second_slot = jnp.sum(
        (counts[:, experts:] + jnp.sum(first_float, axis=0, keepdims=True)) * second_float, axis=1
    )
    slot_values = jnp.stack([first_slot, second_slot], axis=1).astype(jnp.int32)
    return jnp.where(
        slot_values < capacity, choice_ids * stride + slot_values, experts * stride
    )


def gates_of(logits, choice_ids):
    columns = jnp.arange(logits.shape[1], dtype=jnp.int32)[None, :]
    first_logit = jnp.sum(jnp.where(choice_ids[:, 0:1] == columns, logits, 0.0), axis=1)
    second_logit = jnp.sum(jnp.where(choice_ids[:, 1:2] == columns, logits, 0.0), axis=1)
    first_gate = jax.nn.sigmoid(first_logit - second_logit)
    return jnp.stack([first_gate, 1.0 - first_gate], axis=1)


def input_grad(base_grad, normed_grad, scaled, inverse, gain):
    lifted = normed_grad * gain
    centred = (
        lifted
        - jnp.mean(lifted, axis=-1, keepdims=True)
        - scaled * jnp.mean(lifted * scaled, axis=-1, keepdims=True)
    )
    return base_grad + inverse * centred


def ortho_tall(matrix):
    iterate = (matrix / (jnp.sqrt(jnp.sum(matrix * matrix)) + frob_eps)).astype(jnp.bfloat16)
    for iteration in range(NS_STEPS):
        gram_matrix = lax.dot_general(
            iterate, iterate, contract_first, preferred_element_type=jnp.float32
        ).astype(jnp.bfloat16)
        mixer_matrix = (
            quintic_two * gram_matrix.astype(jnp.float32)
            + quintic_three * jnp.dot(gram_matrix, gram_matrix, preferred_element_type=jnp.float32)
        ).astype(jnp.bfloat16)
        iterate = (
            quintic_one * iterate.astype(jnp.float32)
            + jnp.dot(iterate, mixer_matrix, preferred_element_type=jnp.float32)
        ).astype(jnp.bfloat16)
    return iterate


def ortho_steps(read, block, tile, iterate, gram, mixer):
    rows, cols = iterate.shape
    tiles = cols // tile

    def begin():
        def squares(index, total):
            part = read(pl.ds(pl.multiple_of(index * tile, tile), tile))
            return total + jnp.sum(part * part, axis=0, keepdims=True)

        total = lax.fori_loop(0, tiles, squares, jnp.zeros((1, tile), jnp.float32))
        norm = jnp.sqrt(jnp.sum(total)) + frob_eps

        @pl.loop(0, tiles)
        def _(index):
            span = pl.ds(pl.multiple_of(index * tile, tile), tile)
            iterate[:, span] = (read(span) / norm).astype(jnp.bfloat16)

    def mirror(target, part, index):
        target[index * block : (index + 1) * block, 0 : (index + 1) * block] = part
        for other in range(index):
            target[other * block : (other + 1) * block, index * block : (index + 1) * block] = part[
                :, other * block : (other + 1) * block
            ].T

    def make_gram():
        for index in range(rows // block):
            mirror(
                gram,
                lax.dot_general(
                    iterate[index * block : (index + 1) * block, :],
                    iterate[0 : (index + 1) * block, :],
                    contract_last,
                    preferred_element_type=jnp.float32,
                ).astype(jnp.bfloat16),
                index,
            )

    def mix(gram_rows, gram_part, gram_columns):
        return (
            quintic_two * gram_part.astype(jnp.float32)
            + quintic_three * jnp.dot(gram_rows, gram_columns, preferred_element_type=jnp.float32)
        ).astype(jnp.bfloat16)

    def apply(mixer_rows, part, columns):
        return (
            quintic_one * part.astype(jnp.float32)
            + jnp.dot(mixer_rows, columns, preferred_element_type=jnp.float32)
        ).astype(jnp.bfloat16)

    def make_mixer():
        for index in range(rows // block):
            span = pl.ds(index * block, block)
            reach = (index + 1) * block
            mirror(mixer, mix(gram[span, :], gram[span, 0:reach], gram[:, 0:reach]), index)

    def advance():
        @pl.loop(0, tiles)
        def _(index):
            span = pl.ds(pl.multiple_of(index * tile, tile), tile)
            columns = iterate[:, span]
            iterate[:, span] = apply(mixer[...], columns, columns)

    def last_rows(own, row_count, out_ref):
        mixer[0:row_count, :] = mix(gram[own, :], gram[own, :], gram[...])

        @pl.loop(0, tiles)
        def _(index):
            span = pl.ds(pl.multiple_of(index * tile, tile), tile)
            out_ref[:, span] = apply(mixer[0:row_count, :], iterate[own, span], iterate[:, span])

    return begin, make_gram, make_mixer, advance, last_rows


def tile_sizes(rows, cols):
    block = next(size for size in (256, 128, rows) if rows % size == 0)
    tile = next(size for size in (768, 512, 256, 128, cols) if cols % size == 0)
    return block, tile


MESH = pl.DeviceIdType.MESH


def at_expert(index):
    return {"expert": index}


def at_dp(index):
    return {"dp": index}


def remote(source, target, send_sem, recv_sem, device):
    return pltpu.make_async_remote_copy(
        src_ref=source,
        dst_ref=target,
        send_sem=send_sem,
        recv_sem=recv_sem,
        device_id=device,
        device_id_type=MESH,
    )


def greet(devices):
    barrier = pltpu.get_barrier_semaphore()
    for device in devices:
        pl.semaphore_signal(barrier, inc=1, device_id=device, device_id_type=MESH)
    pl.semaphore_wait(barrier, len(devices))


def neighbours(chips, planes):
    me = lax.axis_index("expert")
    core, chip = lax.rem(me, 2), lax.div(me, 2)
    plane = lax.axis_index("dp")
    ahead = [2 * lax.rem(chip + shift, chips) + core for shift in range(1, chips)]
    behind = [2 * lax.rem(chip + chips - shift, chips) + core for shift in range(1, chips)]
    above = [lax.rem(plane + shift, planes) for shift in range(1, planes)]
    return me, core, chip, plane, me + 1 - 2 * core, ahead, behind, above


def spread_start(piece, me, partner, ahead, sems, lane):
    copies = [remote(piece(me), piece(me), sems.at[0, lane, 0], sems.at[1, lane, 0], at_expert(partner))]
    for shift, peer in enumerate(ahead, 1):
        copies.append(
            remote(piece(me), piece(me), sems.at[0, lane, shift], sems.at[1, lane, shift], at_expert(peer))
        )
    for copy in copies:
        copy.start()
    return copies


def spread_relay(piece, copies, partner, behind, sems, lane):
    relays = []
    for shift, source in enumerate(behind, 1):
        copies[shift].wait_recv()
        relay = remote(
            piece(source), piece(source), sems.at[2, lane, shift], sems.at[3, lane, shift], at_expert(partner)
        )
        relay.start()
        relays.append(relay)
    return relays


def spread_finish(copies, relays):
    copies[0].wait_recv()
    for relay in relays:
        relay.wait_recv()
    for copy in copies + relays:
        copy.wait_send()


def weights_kernel(
    chips, planes, qkv_ref, out_ref, moments_ref, qkv_all, out_all, moments_all, spread_sems, moment_sems, local_sems
):
    me, core, chip, plane, partner, ahead, behind, above = neighbours(chips, planes)
    greet([at_expert(i) for i in [partner] + ahead] + [at_dp(i) for i in above])
    own_copies = [
        pltpu.make_async_copy(qkv_ref, qkv_all.at[me], local_sems.at[0]),
        pltpu.make_async_copy(out_ref, out_all.at[me], local_sems.at[1]),
    ]
    lanes = []
    for lane, (source, target) in enumerate(((qkv_ref, qkv_all), (out_ref, out_all))):
        copies = [
            remote(
                source,
                target.at[me],
                spread_sems.at[0, lane, shift],
                spread_sems.at[1, lane, shift],
                at_expert(peer),
            )
            for shift, peer in enumerate([partner] + ahead)
        ]
        for copy in copies[1:] + copies[:1]:
            copy.start()
        lanes.append((lane, target, copies))
    keepers = (planes // 2 - 1, planes // 2)
    for which, keeper in enumerate(keepers):

        @pl.when(plane != keeper)
        def _():
            remote(
                moments_ref.at[which],
                moments_all.at[plane],
                moment_sems.at[0, which],
                moment_sems.at[1, plane],
                at_dp(keeper),
            ).start()

        @pl.when(plane == keeper)
        def _():
            pltpu.make_async_copy(
                moments_ref.at[which], moments_all.at[plane], local_sems.at[2]
            ).start()

    for copy in own_copies:
        copy.start()
    relayed = [
        (copies, spread_relay(lambda i: target.at[i], copies, partner, behind, spread_sems, lane))
        for lane, target, copies in lanes
    ]
    for copies, relays in relayed:
        spread_finish(copies, relays)
    for copy in own_copies:
        copy.wait()
    for which, keeper in enumerate(keepers):

        @pl.when(plane != keeper)
        def _():
            remote(
                moments_ref.at[which],
                moments_all.at[plane],
                moment_sems.at[0, which],
                moment_sems.at[1, plane],
                at_dp(keeper),
            ).wait_send()

        @pl.when(plane == keeper)
        def _():
            pltpu.make_async_copy(
                moments_ref.at[which], moments_all.at[plane], local_sems.at[2]
            ).wait()
            for source in range(planes):
                if source != keeper:
                    remote(
                        moments_ref.at[which],
                        moments_all.at[source],
                        moment_sems.at[0, which],
                        moment_sems.at[1, source],
                        at_dp(source),
                    ).wait_recv()


def gather_weights(qkv_weight, out_weight, moments):
    members, planes = lax.axis_size("expert"), lax.axis_size("dp")
    chips = members // 2
    anywhere = pl.BlockSpec(memory_space=pl.ANY)
    return pl.pallas_call(
        functools.partial(weights_kernel, chips, planes),
        out_shape=(
            jax.ShapeDtypeStruct((members,) + qkv_weight.shape, jnp.bfloat16),
            jax.ShapeDtypeStruct((members,) + out_weight.shape, jnp.bfloat16),
            jax.ShapeDtypeStruct((planes,) + moments.shape[1:], jnp.bfloat16),
        ),
        in_specs=[anywhere] * 3,
        out_specs=[anywhere] * 3,
        scratch_shapes=[
            pltpu.SemaphoreType.DMA((4, 2, chips)),
            pltpu.SemaphoreType.DMA((2, max(2, planes))),
            pltpu.SemaphoreType.DMA((3,)),
        ],
        compiler_params=pltpu.CompilerParams(collective_id=1, has_side_effects=True),
    )(qkv_weight, out_weight, moments)


def expert_kernel(
    members,
    planes,
    blocks_ref,
    packing_ref,
    first_weight,
    second_weight,
    back_ref,
    rows_all,
    arrived,
    leaving,
    active,
    pre_grad,
    outcome,
    go_sems,
    back_sems,
    rows_sems,
):
    me, plane = lax.axis_index("expert"), lax.axis_index("dp")
    others = [lax.rem(me + shift, members) for shift in range(1, members)]
    above = [lax.rem(plane + shift, planes) for shift in range(1, planes)]
    greet([at_expert(i) for i in others] + [at_dp(i) for i in above])

    def exchange(source, target, sems):
        copies = [
            remote(source.at[peer], target.at[me], sems.at[0, i], sems.at[1, i], at_expert(peer))
            for i, peer in enumerate(others)
        ]
        for copy in copies:
            copy.start()
        target[me] = source[me]
        return copies

    slots, depth = outcome.shape[0], first_weight.shape[0]
    units = first_weight.shape[1]
    stride = blocks_ref.shape[1]
    gone = exchange(blocks_ref, arrived, go_sems)
    for copy in gone:
        copy.wait_recv()
    rows = jnp.dot(
        packing_ref[...],
        arrived[...].reshape(members * stride, 2 * depth),
        preferred_element_type=jnp.float32,
    ).astype(jnp.bfloat16)
    rows_all[plane] = rows
    rows_copies = [
        remote(rows_all.at[plane], rows_all.at[plane], rows_sems.at[0, i], rows_sems.at[1, i], at_dp(peer))
        for i, peer in enumerate(above)
    ]
    for copy in rows_copies:
        copy.start()
    block = tile_sizes(depth, units)[0]

    @pl.loop(0, units // block)
    def _(index):
        span = pl.ds(pl.multiple_of(index * block, block), block)
        preact = jnp.dot(
            rows_all[plane, :, 0:depth], first_weight[:, span], preferred_element_type=jnp.float32
        )
        act_grad = jnp.dot(
            rows_all[plane, :, depth : 2 * depth],
            second_weight[:, span],
            preferred_element_type=jnp.float32,
        )
        share = 0.5 * (1.0 + lax.erf(preact * 0.7071067811865476))
        slope = share + preact * jnp.exp(-0.5 * preact * preact) * 0.3989422804014327
        active[:, span] = (preact * share).astype(jnp.bfloat16)
        pre_grad[:, span] = (act_grad * slope).astype(jnp.bfloat16)

    for part, (left, weight) in enumerate(((active, second_weight), (pre_grad, first_weight))):
        for start in range(0, depth, block):
            outcome[:, part * depth + start : part * depth + start + block] = lax.dot_general(
                left[...],
                weight[start : start + block, :],
                contract_last,
                preferred_element_type=jnp.float32,
            ).astype(jnp.bfloat16)
    leaving[...] = (
        lax.dot_general(
            packing_ref[...], outcome[...], contract_first, preferred_element_type=jnp.float32
        )
        .astype(jnp.bfloat16)
        .reshape(members, stride, 2 * depth)
    )
    returned = exchange(leaving, back_ref, back_sems)
    for copy in returned:
        copy.wait_recv()
    for copy in gone + returned:
        copy.wait_send()
    for copy in rows_copies:
        copy.wait()


def run_experts(blocks, packing, first_weight, second_weight):
    members, planes = lax.axis_size("expert"), lax.axis_size("dp")
    slots = packing.shape[0]
    depth, units = first_weight.shape
    local = pl.BlockSpec(memory_space=pltpu.VMEM)
    dma = pltpu.SemaphoreType.DMA
    wide = jnp.bfloat16
    return pl.pallas_call(
        functools.partial(expert_kernel, members, planes),
        out_shape=(
            jax.ShapeDtypeStruct(blocks.shape, wide),
            jax.ShapeDtypeStruct((planes, slots, 2 * depth), wide),
        ),
        in_specs=[local] * 4,
        out_specs=[local] * 2,
        scratch_shapes=[
            pltpu.VMEM(blocks.shape, wide),
            pltpu.VMEM(blocks.shape, wide),
            pltpu.VMEM((slots, units), wide),
            pltpu.VMEM((slots, units), wide),
            pltpu.VMEM((slots, 2 * depth), wide),
            dma((2, members - 1)),
            dma((2, members - 1)),
            dma((2, planes - 1)),
        ],
        compiler_params=pltpu.CompilerParams(
            collective_id=3, has_side_effects=True, vmem_limit_bytes=48 << 20
        ),
    )(blocks, packing, first_weight, second_weight)


def attention_kernel(
    chips,
    planes,
    split,
    qkv_term,
    out_term,
    qkv_moment,
    out_moment,
    small_ref,
    rows_all,
    first_weight,
    second_weight,
    expert_moment,
    grad_qkv,
    grad_out,
    new_qkv_moment,
    new_out_moment,
    small_out,
    iter_qkv,
    iter_out,
    expert_grads,
    iter_expert,
    qkv_all,
    out_all,
    iterate,
    wide_iterate,
    hidden,
    expert_total,
    gram,
    mixer,
    crossed,
    leaving,
    landed,
    plane_out,
    plane_in,
    plane_all,
    small_pair,
    small_chip,
    small_plane,
    cross_sems,
    chip_sems,
    plane_sems,
    share_sems,
    spread_sems,
    small_sems,
    iter_sems,
    local_sems,
):
    width = out_term.shape[2]
    lanes = qkv_term.shape[2] // width + 1
    me, core, chip, plane, partner, ahead, behind, above = neighbours(chips, planes)
    greet([at_expert(i) for i in [partner] + ahead] + [at_dp(i) for i in above])

    def cut(pair, lane):
        if lane == lanes - 1:
            return pair[1], pl.ds(0, width)
        return pair[0], pl.ds(lane * width, width)

    def term(lane, index):
        ref, columns = cut((qkv_term, out_term), lane)
        return ref[index, :, columns].astype(jnp.float32)

    order = [lanes - 1] + list(range(lanes - 1))
    crosses = {}
    for lane in order:
        for shift in range(chips):
            target = lax.rem(chip + shift, chips)
            ref, columns = cut((qkv_term, out_term), lane)
            crosses[lane, shift] = remote(
                ref.at[2 * target + 1 - core, :, columns],
                crossed.at[lane, target],
                cross_sems.at[0, lane, shift],
                cross_sems.at[1, lane, shift],
                at_expert(partner),
            )
        for shift in list(range(1, chips)) + [0]:
            crosses[lane, shift].start()
    small_copy = remote(small_ref, small_pair, small_sems.at[0, 0], small_sems.at[1, 0], at_expert(partner))
    small_copy.start()
    sends = list(crosses.values()) + [small_copy]
    moment_copy = pltpu.make_async_copy(expert_moment, iterate, local_sems.at[0])
    moment_copy.start()

    chip_copies = {}

    def to_chips(lane):
        for shift in range(1, chips):
            target = lax.rem(chip + shift, chips)
            crosses[lane, shift].wait_recv()
            leaving[lane, shift - 1] = (
                term(lane, 2 * target + core) + crossed[lane, target].astype(jnp.float32)
            ).astype(jnp.bfloat16)
            copy = remote(
                leaving.at[lane, shift - 1],
                landed.at[lane, shift - 1],
                chip_sems.at[0, lane, shift - 1],
                chip_sems.at[1, lane, shift - 1],
                at_expert(ahead[shift - 1]),
            )
            copy.start()
            chip_copies[lane, shift] = copy
            sends.append(copy)

    small_chip_copies = []

    def small_to_chips():
        small_copy.wait_recv()
        small_chip[chip] = small_ref[...] + small_pair[...]
        for shift, peer in enumerate(ahead, 1):
            copy = remote(
                small_chip.at[chip],
                small_chip.at[chip],
                small_sems.at[0, shift],
                small_sems.at[1, shift],
                at_expert(peer),
            )
            copy.start()
            small_chip_copies.append(copy)
            sends.append(copy)

    small_plane_copies = []

    def small_to_planes():
        for copy in small_chip_copies:
            copy.wait_recv()
        small_plane[plane] = sum(small_chip[i] for i in range(chips))
        for i, peer in enumerate(above):
            copy = remote(
                small_plane.at[plane],
                small_plane.at[plane],
                small_sems.at[0, chips + i],
                small_sems.at[1, chips + i],
                at_dp(peer),
            )
            copy.start()
            small_plane_copies.append(copy)
            sends.append(copy)

    def small_finish():
        for copy in small_plane_copies:
            copy.wait_recv()
        small_out[...] = sum(small_plane[i] for i in range(planes))

    part = plane_out.shape[2]
    plane_copies = {}

    def to_planes(lane):
        crosses[lane, 0].wait_recv()
        total = term(lane, me) + crossed[lane, chip].astype(jnp.float32)
        for shift in range(1, chips):
            chip_copies[lane, shift].wait_recv()
            total = total + landed[lane, shift - 1].astype(jnp.float32)
        if split:
            for i in range(planes):
                plane_out[lane, i] = total[i * part : (i + 1) * part].astype(jnp.bfloat16)
        else:
            plane_in[lane, plane] = total.astype(jnp.bfloat16)
        plane_copies[lane] = []
        for i, peer in enumerate(above):
            copy = remote(
                plane_out.at[lane, peer] if split else plane_in.at[lane, plane],
                plane_in.at[lane, plane],
                plane_sems.at[0, lane, i],
                plane_sems.at[1, lane, i],
                at_dp(peer),
            )
            copy.start()
            plane_copies[lane].append(copy)
            sends.append(copy)

    share_copies = {}

    def share_planes(lane):
        share_copies[lane] = []
        if not split:
            return
        for copy in plane_copies[lane]:
            copy.wait_recv()
        plane_in[lane, plane] = plane_out[lane, plane]
        total = plane_in[lane, 0].astype(jnp.float32)
        for i in range(1, planes):
            total = total + plane_in[lane, i].astype(jnp.float32)
        plane_all[lane, plane] = total.astype(jnp.bfloat16)
        for i, peer in enumerate(above):
            copy = remote(
                plane_all.at[lane, plane],
                plane_all.at[lane, plane],
                share_sems.at[0, lane, i],
                share_sems.at[1, lane, i],
                at_dp(peer),
            )
            copy.start()
            share_copies[lane].append(copy)
            sends.append(copy)

    def piece_of(lane):
        ref, columns = cut((qkv_all, out_all), lane)
        return lambda index: ref.at[index, :, columns]

    spreads, relays = {}, {}

    def make_moment(lane):
        moment, columns = cut((qkv_moment, out_moment), lane)
        grad_target, _ = cut((grad_qkv, grad_out), lane)
        moment_target, _ = cut((new_qkv_moment, new_out_moment), lane)
        whole, _ = cut((qkv_all, out_all), lane)
        if split:
            for copy in share_copies[lane]:
                copy.wait_recv()
            grad = jnp.concatenate(
                [plane_all[lane, i].astype(jnp.float32) for i in range(planes)], axis=0
            )
        else:
            for copy in plane_copies[lane]:
                copy.wait_recv()
            grad = sum(plane_in[lane, i].astype(jnp.float32) for i in range(planes))
        fresh = decay_rate * moment[:, columns] + grad
        grad_target[:, columns] = grad
        moment_target[:, columns] = fresh
        whole[me, :, columns] = fresh.astype(jnp.bfloat16)
        spreads[lane] = spread_start(piece_of(lane), me, partner, ahead, spread_sems, lane)

    def relay(lane):
        relays[lane] = spread_relay(piece_of(lane), spreads[lane], partner, behind, spread_sems, lane)

    depth = first_weight.shape[0]
    units = first_weight.shape[1]
    block, tile = tile_sizes(depth, units)
    which = jnp.where(plane == planes // 2 - 1, 0, 1)
    slots = planes * rows_all.shape[1]

    def hidden_rows(source):
        @pl.loop(0, units // block)
        def _(index):
            span = pl.ds(pl.multiple_of(index * block, block), block)
            preact = jnp.dot(
                rows_all[source, :, 0:depth], first_weight[:, span], preferred_element_type=jnp.float32
            )
            act_grad = jnp.dot(
                rows_all[source, :, depth : 2 * depth],
                second_weight[:, span],
                preferred_element_type=jnp.float32,
            )
            share = 0.5 * (1.0 + lax.erf(preact * 0.7071067811865476))
            slope = share + preact * jnp.exp(-0.5 * preact * preact) * 0.3989422804014327
            hidden[0, source, :, span] = (act_grad * slope).astype(jnp.bfloat16)
            hidden[1, source, :, span] = (preact * share).astype(jnp.bfloat16)

    def expert_grad(matrix):
        @pl.loop(0, depth // block)
        def _(index):
            columns = pl.ds(pl.multiple_of(matrix * depth + index * block, block), block)
            left = rows_all[:, :, columns].reshape(slots, block)
            target = pl.ds(pl.multiple_of(index * block, block), block)
            for start in range(0, units, tile):
                expert_total[target, start : start + tile] = lax.dot_general(
                    left,
                    hidden[matrix, :, :, start : start + tile].reshape(slots, tile),
                    contract_first,
                    preferred_element_type=jnp.float32,
                )

        share = expert_grads.shape[1]
        own = pl.ds(pl.multiple_of(plane * share, share), share)
        expert_grads[matrix] = expert_total[own, :]

    def add_moment():
        moment_copy.wait()

        @pl.loop(0, units // tile)
        def _(index):
            span = pl.ds(pl.multiple_of(index * tile, tile), tile)
            expert_total[:, span] = (
                decay_rate * iterate[:, span].astype(jnp.float32) + expert_total[:, span]
            )

    begin, make_gram, make_mixer, advance, last_rows = ortho_steps(
        lambda span: expert_total[:, span], block, tile, iterate, gram, mixer
    )

    def ortho_step():
        make_gram()
        make_mixer()
        advance()

    def begin_ortho():
        add_moment()
        begin()

    work = [functools.partial(hidden_rows, source) for source in range(planes)]
    work += [functools.partial(expert_grad, 1 - which), functools.partial(expert_grad, which)]
    work += [begin_ortho] + [ortho_step] * NS_STEPS

    expert_share = expert_grads.shape[1]
    keepers = (planes // 2 - 1, planes // 2)

    def iter_copy(keeper, matrix, shift, peer):
        own = pl.ds(pl.multiple_of(peer * expert_share, expert_share), expert_share)
        return remote(
            iterate.at[own, :],
            iter_expert.at[matrix],
            iter_sems.at[0, shift],
            iter_sems.at[1, matrix],
            at_dp(peer),
        )

    def send_iterates():
        for matrix, keeper in enumerate(keepers):

            @pl.when(plane == keeper)
            def _():
                for shift, peer in enumerate(above):
                    iter_copy(keeper, matrix, shift, peer).start()
                iter_expert[matrix] = iterate[keeper * expert_share : (keeper + 1) * expert_share, :]

    def await_iterates():
        for matrix, keeper in enumerate(keepers):

            @pl.when(plane == keeper)
            def _():
                for shift, peer in enumerate(above):
                    iter_copy(keeper, matrix, shift, peer).wait_send()

            @pl.when(plane != keeper)
            def _():
                iter_copy(keeper, matrix, 0, plane).wait_recv()

    def attention_ortho(whole, target):
        cols = whole.shape[2]
        chunk = tile_sizes(depth, cols)[1]
        start, build_gram, build_mixer, step_on, last = ortho_steps(
            lambda span: whole[:, :, span].astype(jnp.float32).reshape(depth, chunk),
            block,
            chunk,
            wide_iterate.at[:, 0:cols],
            gram,
            mixer,
        )
        start()

        @pl.loop(0, NS_STEPS - 1)
        def _(step):
            build_gram()
            build_mixer()
            step_on()

        build_gram()
        kept = target.shape[0]
        if kept == depth:
            own = pl.ds(0, depth)
        else:
            own = pl.ds(pl.multiple_of(me * kept, kept), kept)
        last(own, kept, target)

    work += [send_iterates]

    for lane in order:
        to_chips(lane)
        if lane == order[0]:
            small_to_chips()
    stages = [to_planes, share_planes, make_moment, relay]
    for step in range(lanes + len(stages) - 1):
        for number in range(len(stages) - 1, -1, -1):
            if 0 <= step - number < lanes:
                stages[number](order[step - number])
        if step == 0:
            small_to_planes()
        for _ in range(1 if step >= lanes else 2):
            if work:
                work.pop(0)()
    small_finish()
    while work:
        work.pop(0)()
    spread_finish(spreads[order[0]], relays[order[0]])
    attention_ortho(out_all, iter_out)
    for lane in order[1:]:
        spread_finish(spreads[lane], relays[lane])
    attention_ortho(qkv_all, iter_qkv)
    for copy in sends:
        copy.wait_send()
    await_iterates()


def reduce_attention(
    qkv_term, out_term, qkv_moment, out_moment, small, rows, first_weight, second_weight, expert_moment
):
    members, planes = lax.axis_size("expert"), lax.axis_size("dp")
    chips = members // 2
    share, width = out_moment.shape
    qkv_width = qkv_moment.shape[1]
    lanes = qkv_width // width + 1
    split = share % (8 * planes) == 0
    part = share // planes if split else share
    depth, units = first_weight.shape
    kept = share if share % 16 == 0 else depth
    local = pl.BlockSpec(memory_space=pltpu.VMEM)
    dma = pltpu.SemaphoreType.DMA
    wide = jnp.bfloat16
    return pl.pallas_call(
        functools.partial(attention_kernel, chips, planes, split),
        out_shape=(
            jax.ShapeDtypeStruct(qkv_moment.shape, jnp.float32),
            jax.ShapeDtypeStruct(out_moment.shape, jnp.float32),
            jax.ShapeDtypeStruct(qkv_moment.shape, jnp.float32),
            jax.ShapeDtypeStruct(out_moment.shape, jnp.float32),
            jax.ShapeDtypeStruct(small.shape, jnp.float32),
            jax.ShapeDtypeStruct((kept, qkv_width), wide),
            jax.ShapeDtypeStruct((kept, width), wide),
            jax.ShapeDtypeStruct((2, depth // planes, units), jnp.float32),
            jax.ShapeDtypeStruct((2, depth // planes, units), wide),
        ),
        in_specs=[local] * 8 + [pl.BlockSpec(memory_space=pl.ANY)],
        out_specs=[local] * 9,
        scratch_shapes=[
            pltpu.VMEM((members, share, qkv_width), wide),
            pltpu.VMEM((members, share, width), wide),
            pltpu.VMEM((depth, units), wide),
            pltpu.VMEM((depth, qkv_width), wide),
            pltpu.VMEM((2,) + rows.shape[:2] + (units,), wide),
            pltpu.VMEM((depth, units), jnp.float32),
            pltpu.VMEM((depth, depth), wide),
            pltpu.VMEM((depth, depth), wide),
            pltpu.VMEM((lanes, chips, share, width), wide),
            pltpu.VMEM((lanes, chips - 1, share, width), wide),
            pltpu.VMEM((lanes, chips - 1, share, width), wide),
            pltpu.VMEM((lanes, planes, part, width) if split else (1, 1, part, width), wide),
            pltpu.VMEM((lanes, planes, part, width), wide),
            pltpu.VMEM((lanes, planes, part, width) if split else (1, 1, part, width), wide),
            pltpu.VMEM(small.shape, jnp.float32),
            pltpu.VMEM((chips,) + small.shape, jnp.float32),
            pltpu.VMEM((planes,) + small.shape, jnp.float32),
            dma((2, lanes, chips)),
            dma((2, lanes, chips - 1)),
            dma((2, lanes, planes - 1)),
            dma((2, lanes, planes - 1)),
            dma((4, lanes, chips)),
            dma((2, chips + planes - 1)),
            dma((2, max(2, planes - 1))),
            dma((1,)),
        ],
        compiler_params=pltpu.CompilerParams(
            collective_id=2, has_side_effects=True, vmem_limit_bytes=63 << 20
        ),
    )(
        qkv_term,
        out_term,
        qkv_moment,
        out_moment,
        small,
        rows,
        first_weight,
        second_weight,
        expert_moment,
    )


def split_heads(qkv_rows, image_count, head_width):
    shaped = qkv_rows.reshape(image_count, SEQ, 3, HEADS, head_width)
    return (shaped[:, :, 0], shaped[:, :, 1], shaped[:, :, 2])


def attention_scores(query_rows, key_rows, score_scale):
    return (
        jnp.einsum("ishd,ithd->ihst", query_rows, key_rows, preferred_element_type=jnp.float32)
        * score_scale
    )


def body(
    tokens,
    cotangent,
    routes,
    priority,
    ln_gains,
    ln_biases,
    qkv_weight,
    out_weight,
    router,
    w_in,
    w_out,
    norm_momentum,
    router_momentum,
    qkv_momentum,
    out_momentum,
    w_in_momentum,
    w_out_momentum,
):
    token_count, model_width = tokens.shape
    experts = router.shape[1]
    hidden_units = w_in.shape[2]
    capacity = (token_count + experts - 1) // experts
    slots_all = experts * capacity
    dp_share = model_width // lax.axis_size("dp")
    image_count = token_count // SEQ
    head_width = model_width // HEADS
    score_scale = 1.0 / math.sqrt(head_width)
    first_weight = w_in[0]
    second_weight = w_out[0]
    cot_float = cotangent.astype(jnp.float32)
    dp_size = lax.axis_size("dp")
    dp_index = lax.axis_index("dp")
    members = lax.axis_size("expert")
    keep_first, keep_second = (dp_size // 2 - 1, dp_size // 2)
    full_qkv, full_out, every_moment = gather_weights(
        qkv_weight, out_weight, jnp.concatenate([w_in_momentum, w_out_momentum]).astype(jnp.bfloat16)
    )
    full_qkv = full_qkv.reshape(model_width, 3 * model_width)
    full_out = full_out.reshape(model_width, model_width)
    every_moment = every_moment.reshape(model_width, hidden_units)
    token_float = tokens.astype(jnp.float32)
    scaled_one, inverse_one, normed_one = layer_stats(token_float, ln_gains[0], ln_biases[0])
    attn_in = normed_one.astype(jnp.bfloat16)
    qkv_rows = jnp.dot(attn_in, full_qkv, preferred_element_type=jnp.float32).astype(jnp.bfloat16)
    query_rows, key_rows, value_rows = split_heads(qkv_rows, image_count, head_width)
    scores = attention_scores(query_rows, key_rows, score_scale)
    log_total = jnp.log(jnp.sum(jnp.exp(scores), axis=3, keepdims=True))
    attn_probs = jnp.exp(scores - log_total).astype(jnp.bfloat16)
    mixed_rows = (
        jnp.einsum("ihst,ithd->ishd", attn_probs, value_rows, preferred_element_type=jnp.float32)
        .astype(jnp.bfloat16)
        .reshape(token_count, model_width)
    )
    middle_rows = token_float + jnp.dot(mixed_rows, full_out, preferred_element_type=jnp.float32)
    stride = capacity + -capacity % 16
    slot_flat = slot_index(routes, priority[0], experts, capacity, stride)
    scaled, inverse, normed = layer_stats(middle_rows, ln_gains[1], ln_biases[1])
    logits = jnp.dot(normed, router, precision=highest)
    gate_values = gates_of(logits, routes)
    position = jnp.arange(experts * stride, dtype=jnp.int32)[:, None]
    pick_first = (slot_flat[:, 0][None, :] == position).astype(jnp.float32)
    pick_second = (slot_flat[:, 1][None, :] == position).astype(jnp.float32)
    placing = (pick_first + pick_second).astype(jnp.bfloat16)
    lean_first, lean_second = (pick_first.astype(jnp.bfloat16), pick_second.astype(jnp.bfloat16))
    gated = jnp.concatenate(
        [
            (gate_values[:, 0:1] * cot_float).astype(jnp.bfloat16),
            (gate_values[:, 1:2] * cot_float).astype(jnp.bfloat16),
        ],
        axis=0,
    )
    dispatch = jnp.dot(
        placing, normed.astype(jnp.bfloat16), preferred_element_type=jnp.float32
    ).astype(jnp.bfloat16)
    sent_grad = jnp.dot(
        jnp.concatenate([lean_first, lean_second], axis=1),
        gated,
        preferred_element_type=jnp.float32,
    ).astype(jnp.bfloat16)

    slot_rows = slots_all + -slots_all % 16
    packed = jnp.arange(slot_rows, dtype=jnp.int32)[:, None]
    packing = (
        (position[:, 0][None, :] == packed // capacity * stride + packed % capacity)
        & (packed < slots_all)
    ).astype(jnp.bfloat16)
    returned, every_rows = run_experts(
        jnp.concatenate([dispatch, sent_grad], axis=1).reshape(experts, stride, 2 * model_width),
        packing,
        first_weight,
        second_weight,
    )
    returned = returned.reshape(experts * stride, 2 * model_width)
    back_first = lax.dot_general(
        lean_first, returned, contract_first, preferred_element_type=jnp.float32
    )
    back_second = lax.dot_general(
        lean_second, returned, contract_first, preferred_element_type=jnp.float32
    )
    picked_first, picked_second = (back_first[:, :model_width], back_second[:, :model_width])
    block_out = middle_rows + (
        gate_values[:, 0:1] * picked_first + gate_values[:, 1:2] * picked_second
    )
    grad_gap = jnp.sum(picked_first * cot_float, axis=1) - jnp.sum(picked_second * cot_float, axis=1)
    logit_step = gate_values[:, 0] * gate_values[:, 1] * grad_gap
    columns = jnp.arange(experts, dtype=jnp.int32)[None, :]
    logit_grad = (
        (routes[:, 0:1] == columns).astype(jnp.float32)
        - (routes[:, 1:2] == columns).astype(jnp.float32)
    ) * logit_step[:, None]
    gathered = back_first[:, model_width:] + back_second[:, model_width:]
    normed_grad = gathered + lax.dot_general(
        logit_grad, router, contract_last, precision=highest
    )
    router_local = lax.dot_general(normed, logit_grad, contract_first, precision=highest)
    middle_grad = input_grad(cot_float, normed_grad, scaled, inverse, ln_gains[1])
    middle_rounded = middle_grad.astype(jnp.bfloat16)
    mixed_grad = lax.dot_general(
        middle_rounded, full_out, contract_last, preferred_element_type=jnp.float32
    ).astype(jnp.bfloat16)
    scores_again = attention_scores(query_rows, key_rows, score_scale)
    probs_again = jnp.exp(scores_again - log_total).astype(jnp.bfloat16)
    grad_heads = mixed_grad.reshape(image_count, SEQ, HEADS, head_width)
    value_grad = jnp.einsum(
        "ihst,ishd->ithd", probs_again, grad_heads, preferred_element_type=jnp.float32
    )
    prob_grad = jnp.einsum(
        "ishd,ithd->ihst", grad_heads, value_rows, preferred_element_type=jnp.float32
    )
    prob_float = probs_again.astype(jnp.float32)
    row_delta = jnp.sum(prob_float * prob_grad, axis=3, keepdims=True)
    score_grad = (prob_float * (prob_grad - row_delta) * score_scale).astype(jnp.bfloat16)
    query_grad = jnp.einsum(
        "ihst,ithd->ishd", score_grad, key_rows, preferred_element_type=jnp.float32
    )
    key_grad = jnp.einsum(
        "ihst,ishd->ithd", score_grad, query_rows, preferred_element_type=jnp.float32
    )
    qkv_grad = (
        jnp.stack([query_grad, key_grad, value_grad], axis=2)
        .astype(jnp.bfloat16)
        .reshape(token_count, 3 * model_width)
    )
    attn_in_grad = lax.dot_general(
        qkv_grad, full_qkv, contract_last, preferred_element_type=jnp.float32
    )
    grad_tokens = input_grad(middle_grad, attn_in_grad, scaled_one, inverse_one, ln_gains[0])
    qkv_term = lax.dot_general(
        attn_in, qkv_grad, contract_first, preferred_element_type=jnp.float32
    )
    out_term = lax.dot_general(
        mixed_rows, middle_rounded, contract_first, preferred_element_type=jnp.float32
    )
    norm_local = jnp.stack(
        [
            jnp.sum(attn_in_grad * scaled_one, axis=0),
            jnp.sum(normed_grad * scaled, axis=0),
            jnp.sum(attn_in_grad, axis=0),
            jnp.sum(normed_grad, axis=0),
        ]
    )
    small = jnp.concatenate([router_local.T, norm_local], axis=0)
    small_rows = experts + 4
    (
        grad_qkv,
        grad_out,
        moment_qkv,
        moment_out,
        small_total,
        iter_qkv,
        iter_out,
        expert_grads,
        iter_expert,
    ) = reduce_attention(
        qkv_term.astype(jnp.bfloat16).reshape(members, -1, 3 * model_width),
        out_term.astype(jnp.bfloat16).reshape(members, -1, model_width),
        qkv_momentum,
        out_momentum,
        jnp.pad(small, ((0, -small_rows % 8), (0, 0))),
        every_rows,
        first_weight,
        second_weight,
        every_moment,
    )
    grad_router = small_total[:experts].T
    grad_norm = small_total[experts:small_rows]
    row_base = dp_index * dp_share
    grad_first, grad_second = (expert_grads[0], expert_grads[1])
    moment_first = decay_rate * w_in_momentum[0] + grad_first
    moment_second = decay_rate * w_out_momentum[0] + grad_second
    iter_first, iter_second = (iter_expert[0], iter_expert[1])
    expert_share = qkv_weight.shape[0]
    if iter_out.shape[0] != expert_share:
        expert_base = lax.axis_index("expert") * expert_share
        iter_out = lax.dynamic_slice_in_dim(iter_out, expert_base, expert_share, 0)
        iter_qkv = lax.dynamic_slice_in_dim(iter_qkv, expert_base, expert_share, 0)
    new_norm_momentum = decay_rate * norm_momentum + grad_norm
    new_norm = jnp.concatenate([ln_gains, ln_biases], axis=0) - norm_rate * new_norm_momentum
    new_router_momentum = decay_rate * router_momentum + grad_router
    new_router = router - matrix_rate * ortho_tall(new_router_momentum).astype(jnp.float32)

    rows_first = lax.dynamic_slice_in_dim(first_weight, row_base, dp_share, 0).astype(jnp.float32)
    rows_second = lax.dynamic_slice_in_dim(second_weight, row_base, dp_share, 0).astype(jnp.float32)
    widen_factor = math.sqrt(max(1.0, hidden_units / model_width))
    new_first = rows_first - matrix_rate * widen_factor * iter_first.astype(jnp.float32)
    new_second = rows_second - matrix_rate * iter_second.astype(jnp.float32)
    new_qkv = qkv_weight.astype(jnp.float32) - matrix_rate * math.sqrt(3.0) * iter_qkv.astype(
        jnp.float32
    )
    new_out = out_weight.astype(jnp.float32) - matrix_rate * iter_out.astype(jnp.float32)
    return (
        block_out,
        grad_tokens,
        grad_norm,
        grad_router,
        grad_qkv,
        grad_out,
        grad_first[None],
        grad_second[None],
        new_norm,
        new_norm_momentum,
        new_router,
        new_router_momentum,
        new_qkv,
        moment_qkv,
        new_out,
        moment_out,
        new_first[None],
        moment_first[None],
        new_second[None],
        moment_second[None],
    )


def solution(mesh):
    in_specs = (
        P(("dp", "expert"), None),
        P(("dp", "expert"), None),
        P(("dp", "expert"), None),
        P(("dp", "expert"), None),
        P(),
        P(),
        P("expert", None),
        P("expert", None),
        P(),
        P("expert", None, None),
        P("expert", None, None),
        P(),
        P(),
        P("expert", None),
        P("expert", None),
        P("expert", "dp", None),
        P("expert", "dp", None),
    )
    out_specs = (
        P(("dp", "expert"), None),
        P(("dp", "expert"), None),
        P(),
        P(),
        P("expert", None),
        P("expert", None),
        P("expert", "dp", None),
        P("expert", "dp", None),
        P(),
        P(),
        P(),
        P(),
        P("expert", None),
        P("expert", None),
        P("expert", None),
        P("expert", None),
        P("expert", "dp", None),
        P("expert", "dp", None),
        P("expert", "dp", None),
        P("expert", "dp", None),
    )
    return jax.shard_map(body, mesh=mesh, in_specs=in_specs, out_specs=out_specs, check_vma=False)
```

```python
import functools
import math

import jax
import jax.numpy as jnp
from jax import lax
from jax.experimental import pallas as pl
from jax.experimental.pallas import tpu as pltpu
from jax.sharding import PartitionSpec as P

HEADS = 12
NS_STEPS = 5
SEQ = 197


quintic_one = 3.4445
quintic_two = -4.775
quintic_three = 2.0315
decay_rate = 0.9
matrix_rate = 0.2
norm_rate = 0.004
norm_eps = 1e-06
frob_eps = 1e-07
highest = lax.Precision.HIGHEST
contract_last = (((1,), (1,)), ((), ()))
contract_first = (((0,), (0,)), ((), ()))


def gelu_slope(preact):
    return (
        0.5 * (1.0 + lax.erf(preact * 0.7071067811865476))
        + preact * jnp.exp(-0.5 * preact * preact) * 0.3989422804014327
    )


def layer_stats(token_rows, gain, bias):
    centre = token_rows - jnp.mean(token_rows, axis=-1, keepdims=True)
    inverse = lax.rsqrt(jnp.mean(centre * centre, axis=-1, keepdims=True) + norm_eps)
    scaled = centre * inverse
    return (scaled, inverse, scaled * gain + bias)


def slot_index(choice_ids, order_rows, experts, capacity, stride):
    token_count = choice_ids.shape[0]
    ranks = jnp.arange(token_count, dtype=jnp.int32)
    turn = jnp.sum(
        jnp.where(order_rows[:, None] == ranks[None, :], ranks[:, None], 0), axis=0, dtype=jnp.int32
    )
    earlier = (turn[None, :] < turn[:, None]).astype(jnp.bfloat16)
    columns = jnp.arange(experts, dtype=jnp.int32)[None, :]
    first = (choice_ids[:, 0:1] == columns).astype(jnp.bfloat16)
    second = (choice_ids[:, 1:2] == columns).astype(jnp.bfloat16)
    counts = jnp.dot(
        earlier, jnp.concatenate([first, second], axis=1), preferred_element_type=jnp.float32
    )
    first_float, second_float = first.astype(jnp.float32), second.astype(jnp.float32)
    first_slot = jnp.sum(counts[:, :experts] * first_float, axis=1)
    second_slot = jnp.sum(
        (counts[:, experts:] + jnp.sum(first_float, axis=0, keepdims=True)) * second_float, axis=1
    )
    slot_values = jnp.stack([first_slot, second_slot], axis=1).astype(jnp.int32)
    return jnp.where(
        slot_values < capacity, choice_ids * stride + slot_values, experts * stride
    )


def gates_of(logits, choice_ids):
    columns = jnp.arange(logits.shape[1], dtype=jnp.int32)[None, :]
    first_logit = jnp.sum(jnp.where(choice_ids[:, 0:1] == columns, logits, 0.0), axis=1)
    second_logit = jnp.sum(jnp.where(choice_ids[:, 1:2] == columns, logits, 0.0), axis=1)
    first_gate = jax.nn.sigmoid(first_logit - second_logit)
    return jnp.stack([first_gate, 1.0 - first_gate], axis=1)


def input_grad(base_grad, normed_grad, scaled, inverse, gain):
    lifted = normed_grad * gain
    centred = (
        lifted
        - jnp.mean(lifted, axis=-1, keepdims=True)
        - scaled * jnp.mean(lifted * scaled, axis=-1, keepdims=True)
    )
    return base_grad + inverse * centred


def ortho_steps(read, block, tile, iterate, gram, mixer):
    rows, cols = iterate.shape
    tiles = cols // tile

    def begin():
        def squares(index, total):
            part = read(pl.ds(pl.multiple_of(index * tile, tile), tile))
            return total + jnp.sum(part * part, axis=0, keepdims=True)

        total = lax.fori_loop(0, tiles, squares, jnp.zeros((1, tile), jnp.float32))
        norm = jnp.sqrt(jnp.sum(total)) + frob_eps

        @pl.loop(0, tiles)
        def _(index):
            span = pl.ds(pl.multiple_of(index * tile, tile), tile)
            iterate[:, span] = (read(span) / norm).astype(jnp.bfloat16)

    def mirror(target, part, index):
        target[index * block : (index + 1) * block, 0 : (index + 1) * block] = part
        for other in range(index):
            target[other * block : (other + 1) * block, index * block : (index + 1) * block] = part[
                :, other * block : (other + 1) * block
            ].T

    def make_gram():
        for index in range(rows // block):
            mirror(
                gram,
                lax.dot_general(
                    iterate[index * block : (index + 1) * block, :],
                    iterate[0 : (index + 1) * block, :],
                    contract_last,
                    preferred_element_type=jnp.float32,
                ).astype(jnp.bfloat16),
                index,
            )

    def mix(gram_rows, gram_part, gram_columns):
        return (
            quintic_two * gram_part.astype(jnp.float32)
            + quintic_three * jnp.dot(gram_rows, gram_columns, preferred_element_type=jnp.float32)
        ).astype(jnp.bfloat16)

    def apply(mixer_rows, part, columns):
        return (
            quintic_one * part.astype(jnp.float32)
            + jnp.dot(mixer_rows, columns, preferred_element_type=jnp.float32)
        ).astype(jnp.bfloat16)

    def make_mixer():
        for index in range(rows // block):
            span = pl.ds(index * block, block)
            reach = (index + 1) * block
            mirror(mixer, mix(gram[span, :], gram[span, 0:reach], gram[:, 0:reach]), index)

    def advance():
        @pl.loop(0, tiles)
        def _(index):
            span = pl.ds(pl.multiple_of(index * tile, tile), tile)
            columns = iterate[:, span]
            iterate[:, span] = apply(mixer[...], columns, columns)

    def last_rows(own, row_count, out_ref):
        mixer[0:row_count, :] = mix(gram[own, :], gram[own, :], gram[...])

        @pl.loop(0, tiles)
        def _(index):
            span = pl.ds(pl.multiple_of(index * tile, tile), tile)
            out_ref[:, span] = apply(mixer[0:row_count, :], iterate[own, span], iterate[:, span])

    return begin, make_gram, make_mixer, advance, last_rows


def tile_sizes(rows, cols):
    block = next(size for size in (256, 128, rows) if rows % size == 0)
    tile = next(size for size in (768, 512, 256, 128, cols) if cols % size == 0)
    return block, tile


MESH = pl.DeviceIdType.MESH


def at_expert(index):
    return {"expert": index}


def at_dp(index):
    return {"dp": index}


def remote(source, target, send_sem, recv_sem, device):
    return pltpu.make_async_remote_copy(
        src_ref=source,
        dst_ref=target,
        send_sem=send_sem,
        recv_sem=recv_sem,
        device_id=device,
        device_id_type=MESH,
    )


def greet(devices):
    barrier = pltpu.get_barrier_semaphore()
    for device in devices:
        pl.semaphore_signal(barrier, inc=1, device_id=device, device_id_type=MESH)
    pl.semaphore_wait(barrier, len(devices))


def neighbours(chips, planes):
    me = lax.axis_index("expert")
    core, chip = lax.rem(me, 2), lax.div(me, 2)
    plane = lax.axis_index("dp")
    ahead = [2 * lax.rem(chip + shift, chips) + core for shift in range(1, chips)]
    behind = [2 * lax.rem(chip + chips - shift, chips) + core for shift in range(1, chips)]
    above = [lax.rem(plane + shift, planes) for shift in range(1, planes)]
    return me, core, chip, plane, me + 1 - 2 * core, ahead, behind, above


def spread_start(piece, me, partner, ahead, sems, lane):
    copies = [remote(piece(me), piece(me), sems.at[0, lane, 0], sems.at[1, lane, 0], at_expert(partner))]
    for shift, peer in enumerate(ahead, 1):
        copies.append(
            remote(piece(me), piece(me), sems.at[0, lane, shift], sems.at[1, lane, shift], at_expert(peer))
        )
    for copy in copies:
        copy.start()
    return copies


def spread_relay(piece, copies, partner, behind, sems, lane):
    relays = []
    for shift, source in enumerate(behind, 1):
        copies[shift].wait_recv()
        relay = remote(
            piece(source), piece(source), sems.at[2, lane, shift], sems.at[3, lane, shift], at_expert(partner)
        )
        relay.start()
        relays.append(relay)
    return relays


def spread_finish(copies, relays):
    copies[0].wait_recv()
    for relay in relays:
        relay.wait_recv()
    for copy in copies + relays:
        copy.wait_send()


def weights_kernel(
    chips, planes, qkv_ref, out_ref, moments_ref, qkv_all, out_all, moments_all, spread_sems, moment_sems, local_sems
):
    me, core, chip, plane, partner, ahead, behind, above = neighbours(chips, planes)
    greet([at_expert(i) for i in [partner] + ahead] + [at_dp(i) for i in above])
    own_copies = [
        pltpu.make_async_copy(qkv_ref, qkv_all.at[me], local_sems.at[0]),
        pltpu.make_async_copy(out_ref, out_all.at[me], local_sems.at[1]),
    ]
    lanes = []
    for lane, (source, target) in enumerate(((qkv_ref, qkv_all), (out_ref, out_all))):
        copies = [
            remote(
                source,
                target.at[me],
                spread_sems.at[0, lane, shift],
                spread_sems.at[1, lane, shift],
                at_expert(peer),
            )
            for shift, peer in enumerate([partner] + ahead)
        ]
        for copy in copies[1:] + copies[:1]:
            copy.start()
        lanes.append((lane, target, copies))
    keepers = (planes // 2 - 1, planes // 2)
    for which, keeper in enumerate(keepers):

        @pl.when(plane != keeper)
        def _():
            remote(
                moments_ref.at[which],
                moments_all.at[plane],
                moment_sems.at[0, which],
                moment_sems.at[1, plane],
                at_dp(keeper),
            ).start()

        @pl.when(plane == keeper)
        def _():
            pltpu.make_async_copy(
                moments_ref.at[which], moments_all.at[plane], local_sems.at[2]
            ).start()

    for copy in own_copies:
        copy.start()
    relayed = [
        (copies, spread_relay(lambda i: target.at[i], copies, partner, behind, spread_sems, lane))
        for lane, target, copies in lanes
    ]
    for copies, relays in relayed:
        spread_finish(copies, relays)
    for copy in own_copies:
        copy.wait()
    for which, keeper in enumerate(keepers):

        @pl.when(plane != keeper)
        def _():
            remote(
                moments_ref.at[which],
                moments_all.at[plane],
                moment_sems.at[0, which],
                moment_sems.at[1, plane],
                at_dp(keeper),
            ).wait_send()

        @pl.when(plane == keeper)
        def _():
            pltpu.make_async_copy(
                moments_ref.at[which], moments_all.at[plane], local_sems.at[2]
            ).wait()
            for source in range(planes):
                if source != keeper:
                    remote(
                        moments_ref.at[which],
                        moments_all.at[source],
                        moment_sems.at[0, which],
                        moment_sems.at[1, source],
                        at_dp(source),
                    ).wait_recv()


def gather_weights(qkv_weight, out_weight, moments):
    members, planes = lax.axis_size("expert"), lax.axis_size("dp")
    chips = members // 2
    anywhere = pl.BlockSpec(memory_space=pl.ANY)
    return pl.pallas_call(
        functools.partial(weights_kernel, chips, planes),
        out_shape=(
            jax.ShapeDtypeStruct((members,) + qkv_weight.shape, jnp.bfloat16),
            jax.ShapeDtypeStruct((members,) + out_weight.shape, jnp.bfloat16),
            jax.ShapeDtypeStruct((planes,) + moments.shape[1:], jnp.bfloat16),
        ),
        in_specs=[anywhere] * 3,
        out_specs=[anywhere] * 3,
        scratch_shapes=[
            pltpu.SemaphoreType.DMA((4, 2, chips)),
            pltpu.SemaphoreType.DMA((2, max(2, planes))),
            pltpu.SemaphoreType.DMA((3,)),
        ],
        compiler_params=pltpu.CompilerParams(collective_id=1, has_side_effects=True),
    )(qkv_weight, out_weight, moments)


def expert_kernel(
    members,
    planes,
    blocks_ref,
    packing_ref,
    first_weight,
    second_weight,
    back_ref,
    rows_all,
    hidden,
    arrived,
    leaving,
    outcome,
    go_sems,
    back_sems,
    rows_sems,
):
    me, plane = lax.axis_index("expert"), lax.axis_index("dp")
    others = [lax.rem(me + shift, members) for shift in range(1, members)]
    above = [lax.rem(plane + shift, planes) for shift in range(1, planes)]
    greet([at_expert(i) for i in others] + [at_dp(i) for i in above])

    def exchange(source, target, sems):
        copies = [
            remote(source.at[peer], target.at[me], sems.at[0, i], sems.at[1, i], at_expert(peer))
            for i, peer in enumerate(others)
        ]
        for copy in copies:
            copy.start()
        target[me] = source[me]
        return copies

    depth, units = first_weight.shape
    stride = blocks_ref.shape[1]
    gone = exchange(blocks_ref, arrived, go_sems)
    for copy in gone:
        copy.wait_recv()
    rows_all[plane] = jnp.dot(
        packing_ref[...],
        arrived[...].reshape(members * stride, 2 * depth),
        preferred_element_type=jnp.float32,
    ).astype(jnp.bfloat16)
    last = planes - 1

    def hop(way, number, block):
        return remote(
            rows_all.at[block],
            rows_all.at[block],
            rows_sems.at[0, way, number],
            rows_sems.at[1, way, number],
            at_dp(lax.rem(plane + planes + 1 - 2 * way, planes)),
        )

    def can_send(way, number):
        if way == 0:
            return (plane < last) & (plane >= number)
        return (plane > 0) & (plane + number <= last)

    def block_of(way, number):
        return plane - number if way == 0 else plane + number

    for way in range(2):

        @pl.when(can_send(way, 0))
        def _():
            hop(way, 0, plane).start()

    block = tile_sizes(depth, units)[0]

    def hidden_rows(source):
        @pl.loop(0, units // block)
        def _(index):
            span = pl.ds(pl.multiple_of(index * block, block), block)
            preact = jnp.dot(
                rows_all[source, :, 0:depth], first_weight[:, span], preferred_element_type=jnp.float32
            )
            act_grad = jnp.dot(
                rows_all[source, :, depth : 2 * depth],
                second_weight[:, span],
                preferred_element_type=jnp.float32,
            )
            share = 0.5 * (1.0 + lax.erf(preact * 0.7071067811865476))
            slope = share + preact * jnp.exp(-0.5 * preact * preact) * 0.3989422804014327
            hidden[0, source, :, span] = (act_grad * slope).astype(jnp.bfloat16)
            hidden[1, source, :, span] = (preact * share).astype(jnp.bfloat16)

    hidden_rows(plane)
    for part, weight in enumerate((second_weight, first_weight)):
        for start in range(0, depth, block):
            outcome[:, part * depth + start : part * depth + start + block] = lax.dot_general(
                hidden[1 - part, plane],
                weight[start : start + block, :],
                contract_last,
                preferred_element_type=jnp.float32,
            ).astype(jnp.bfloat16)
    leaving[...] = (
        lax.dot_general(
            packing_ref[...], outcome[...], contract_first, preferred_element_type=jnp.float32
        )
        .astype(jnp.bfloat16)
        .reshape(members, stride, 2 * depth)
    )
    returned = exchange(leaving, back_ref, back_sems)
    for number in range(1, planes):
        arrives = (plane >= number, plane + number <= last)
        for way in range(2):

            @pl.when(arrives[way])
            def _():
                source = block_of(way, number)
                hop(way, number - 1, source).wait_recv()

            if number < last:

                @pl.when(can_send(way, number))
                def _():
                    hop(way, number, block_of(way, number)).start()

        for way in range(2):

            @pl.when(arrives[way])
            def _():
                hidden_rows(block_of(way, number))

    for copy in returned:
        copy.wait_recv()
    for copy in gone + returned:
        copy.wait_send()
    for number in range(last):
        for way in range(2):

            @pl.when(can_send(way, number))
            def _():
                hop(way, number, block_of(way, number)).wait_send()


def run_experts(blocks, packing, first_weight, second_weight):
    members, planes = lax.axis_size("expert"), lax.axis_size("dp")
    slots = packing.shape[0]
    depth, units = first_weight.shape
    local = pl.BlockSpec(memory_space=pltpu.VMEM)
    dma = pltpu.SemaphoreType.DMA
    wide = jnp.bfloat16
    return pl.pallas_call(
        functools.partial(expert_kernel, members, planes),
        out_shape=(
            jax.ShapeDtypeStruct(blocks.shape, wide),
            jax.ShapeDtypeStruct((planes, slots, 2 * depth), wide),
            jax.ShapeDtypeStruct((2, planes, slots, units), wide),
        ),
        in_specs=[local] * 4,
        out_specs=[local] * 3,
        scratch_shapes=[
            pltpu.VMEM(blocks.shape, wide),
            pltpu.VMEM(blocks.shape, wide),
            pltpu.VMEM((slots, 2 * depth), wide),
            dma((2, members - 1)),
            dma((2, members - 1)),
            dma((2, 2, planes - 1)),
        ],
        compiler_params=pltpu.CompilerParams(
            collective_id=3, has_side_effects=True, vmem_limit_bytes=48 << 20
        ),
    )(blocks, packing, first_weight, second_weight)


def attention_kernel(
    chips,
    planes,
    split,
    qkv_term,
    out_term,
    qkv_moment,
    out_moment,
    small_ref,
    rows_all,
    hidden,
    expert_moment,
    router_moment,
    grad_qkv,
    grad_out,
    new_qkv_moment,
    new_out_moment,
    small_out,
    iter_qkv,
    iter_out,
    expert_grads,
    iter_expert,
    iter_router,
    qkv_all,
    out_all,
    iterate,
    wide_iterate,
    expert_total,
    gram,
    mixer,
    crossed,
    leaving,
    landed,
    plane_out,
    plane_in,
    plane_all,
    small_pair,
    small_chip,
    small_plane,
    cross_sems,
    chip_sems,
    plane_sems,
    share_sems,
    spread_sems,
    small_sems,
    iter_sems,
    local_sems,
):
    width = out_term.shape[2]
    lanes = qkv_term.shape[2] // width + 1
    me, core, chip, plane, partner, ahead, behind, above = neighbours(chips, planes)
    greet([at_expert(i) for i in [partner] + ahead] + [at_dp(i) for i in above])

    def cut(pair, lane):
        if lane == lanes - 1:
            return pair[1], pl.ds(0, width)
        return pair[0], pl.ds(lane * width, width)

    def term(lane, index):
        ref, columns = cut((qkv_term, out_term), lane)
        return ref[index, :, columns].astype(jnp.float32)

    order = [lanes - 1] + list(range(lanes - 1))
    crosses = {}
    for lane in order:
        for shift in range(chips):
            target = lax.rem(chip + shift, chips)
            ref, columns = cut((qkv_term, out_term), lane)
            crosses[lane, shift] = remote(
                ref.at[2 * target + 1 - core, :, columns],
                crossed.at[lane, target],
                cross_sems.at[0, lane, shift],
                cross_sems.at[1, lane, shift],
                at_expert(partner),
            )
        for shift in list(range(1, chips)) + [0]:
            crosses[lane, shift].start()
    small_copy = remote(small_ref, small_pair, small_sems.at[0, 0], small_sems.at[1, 0], at_expert(partner))
    small_copy.start()
    sends = list(crosses.values()) + [small_copy]
    moment_copy = pltpu.make_async_copy(expert_moment, iterate, local_sems.at[0])
    moment_copy.start()

    chip_copies = {}

    def to_chips(lane):
        for shift in range(1, chips):
            target = lax.rem(chip + shift, chips)
            crosses[lane, shift].wait_recv()
            leaving[lane, shift - 1] = (
                term(lane, 2 * target + core) + crossed[lane, target].astype(jnp.float32)
            ).astype(jnp.bfloat16)
            copy = remote(
                leaving.at[lane, shift - 1],
                landed.at[lane, shift - 1],
                chip_sems.at[0, lane, shift - 1],
                chip_sems.at[1, lane, shift - 1],
                at_expert(ahead[shift - 1]),
            )
            copy.start()
            chip_copies[lane, shift] = copy
            sends.append(copy)

    small_chip_copies = []

    def small_to_chips():
        small_copy.wait_recv()
        small_chip[chip] = small_ref[...] + small_pair[...]
        for shift, peer in enumerate(ahead, 1):
            copy = remote(
                small_chip.at[chip],
                small_chip.at[chip],
                small_sems.at[0, shift],
                small_sems.at[1, shift],
                at_expert(peer),
            )
            copy.start()
            small_chip_copies.append(copy)
            sends.append(copy)

    small_plane_copies = []

    def small_to_planes():
        for copy in small_chip_copies:
            copy.wait_recv()
        small_plane[plane] = sum(small_chip[i] for i in range(chips))
        for i, peer in enumerate(above):
            copy = remote(
                small_plane.at[plane],
                small_plane.at[plane],
                small_sems.at[0, chips + i],
                small_sems.at[1, chips + i],
                at_dp(peer),
            )
            copy.start()
            small_plane_copies.append(copy)
            sends.append(copy)

    def small_finish():
        for copy in small_plane_copies:
            copy.wait_recv()
        small_out[...] = sum(small_plane[i] for i in range(planes))
        count = router_moment.shape[0]
        fresh = decay_rate * router_moment[...] + small_out[0:count, :]
        norm = jnp.sqrt(jnp.sum(fresh * fresh)) + frob_eps

        def rounded(values):
            return values.astype(jnp.bfloat16).astype(jnp.float32)

        turned = rounded(fresh / norm)
        for _ in range(NS_STEPS):
            product = rounded(
                lax.dot_general(turned, turned, contract_last, preferred_element_type=jnp.float32)
            )
            blend = rounded(
                quintic_two * product
                + quintic_three * jnp.dot(product, product, preferred_element_type=jnp.float32)
            )
            turned = rounded(
                quintic_one * turned + jnp.dot(blend, turned, preferred_element_type=jnp.float32)
            )
        iter_router[...] = turned

    part = plane_out.shape[2]
    plane_copies = {}

    def to_planes(lane):
        crosses[lane, 0].wait_recv()
        total = term(lane, me) + crossed[lane, chip].astype(jnp.float32)
        for shift in range(1, chips):
            chip_copies[lane, shift].wait_recv()
            total = total + landed[lane, shift - 1].astype(jnp.float32)
        if split:
            for i in range(planes):
                plane_out[lane, i] = total[i * part : (i + 1) * part].astype(jnp.bfloat16)
        else:
            plane_in[lane, plane] = total.astype(jnp.bfloat16)
        plane_copies[lane] = []
        for i, peer in enumerate(above):
            copy = remote(
                plane_out.at[lane, peer] if split else plane_in.at[lane, plane],
                plane_in.at[lane, plane],
                plane_sems.at[0, lane, i],
                plane_sems.at[1, lane, i],
                at_dp(peer),
            )
            copy.start()
            plane_copies[lane].append(copy)
            sends.append(copy)

    share_copies = {}

    def share_planes(lane):
        share_copies[lane] = []
        if not split:
            return
        for copy in plane_copies[lane]:
            copy.wait_recv()
        plane_in[lane, plane] = plane_out[lane, plane]
        total = plane_in[lane, 0].astype(jnp.float32)
        for i in range(1, planes):
            total = total + plane_in[lane, i].astype(jnp.float32)
        plane_all[lane, plane] = total.astype(jnp.bfloat16)
        for i, peer in enumerate(above):
            copy = remote(
                plane_all.at[lane, plane],
                plane_all.at[lane, plane],
                share_sems.at[0, lane, i],
                share_sems.at[1, lane, i],
                at_dp(peer),
            )
            copy.start()
            share_copies[lane].append(copy)
            sends.append(copy)

    def piece_of(lane):
        ref, columns = cut((qkv_all, out_all), lane)
        return lambda index: ref.at[index, :, columns]

    spreads, relays = {}, {}

    def make_moment(lane):
        moment, columns = cut((qkv_moment, out_moment), lane)
        grad_target, _ = cut((grad_qkv, grad_out), lane)
        moment_target, _ = cut((new_qkv_moment, new_out_moment), lane)
        whole, _ = cut((qkv_all, out_all), lane)
        if split:
            for copy in share_copies[lane]:
                copy.wait_recv()
            grad = jnp.concatenate(
                [plane_all[lane, i].astype(jnp.float32) for i in range(planes)], axis=0
            )
        else:
            for copy in plane_copies[lane]:
                copy.wait_recv()
            grad = sum(plane_in[lane, i].astype(jnp.float32) for i in range(planes))
        fresh = decay_rate * moment[:, columns] + grad
        grad_target[:, columns] = grad
        moment_target[:, columns] = fresh
        whole[me, :, columns] = fresh.astype(jnp.bfloat16)
        spreads[lane] = spread_start(piece_of(lane), me, partner, ahead, spread_sems, lane)

    def relay(lane):
        relays[lane] = spread_relay(piece_of(lane), spreads[lane], partner, behind, spread_sems, lane)

    depth, units = iterate.shape
    block, tile = tile_sizes(depth, units)
    which = jnp.where(plane == planes // 2 - 1, 0, 1)
    slots = planes * rows_all.shape[1]

    def expert_grad(matrix):
        @pl.loop(0, depth // block)
        def _(index):
            columns = pl.ds(pl.multiple_of(matrix * depth + index * block, block), block)
            left = rows_all[:, :, columns].reshape(slots, block)
            target = pl.ds(pl.multiple_of(index * block, block), block)
            for start in range(0, units, tile):
                expert_total[target, start : start + tile] = lax.dot_general(
                    left,
                    hidden[matrix, :, :, start : start + tile].reshape(slots, tile),
                    contract_first,
                    preferred_element_type=jnp.float32,
                )

        share = expert_grads.shape[1]
        own = pl.ds(pl.multiple_of(plane * share, share), share)
        expert_grads[matrix] = expert_total[own, :]

    def add_moment():
        moment_copy.wait()

        @pl.loop(0, units // tile)
        def _(index):
            span = pl.ds(pl.multiple_of(index * tile, tile), tile)
            expert_total[:, span] = (
                decay_rate * iterate[:, span].astype(jnp.float32) + expert_total[:, span]
            )

    begin, make_gram, make_mixer, advance, last_rows = ortho_steps(
        lambda span: expert_total[:, span], block, tile, iterate, gram, mixer
    )

    def ortho_step():
        make_gram()
        make_mixer()
        advance()

    def begin_ortho():
        add_moment()
        begin()

    work = [functools.partial(expert_grad, 1 - which), functools.partial(expert_grad, which)]
    work += [begin_ortho] + [ortho_step] * NS_STEPS

    expert_share = expert_grads.shape[1]
    keepers = (planes // 2 - 1, planes // 2)

    def iter_copy(keeper, matrix, shift, peer):
        own = pl.ds(pl.multiple_of(peer * expert_share, expert_share), expert_share)
        return remote(
            iterate.at[own, :],
            iter_expert.at[matrix],
            iter_sems.at[0, shift],
            iter_sems.at[1, matrix],
            at_dp(peer),
        )

    def send_iterates():
        for matrix, keeper in enumerate(keepers):

            @pl.when(plane == keeper)
            def _():
                for shift, peer in enumerate(above):
                    iter_copy(keeper, matrix, shift, peer).start()
                iter_expert[matrix] = iterate[keeper * expert_share : (keeper + 1) * expert_share, :]

    def await_iterates():
        for matrix, keeper in enumerate(keepers):

            @pl.when(plane == keeper)
            def _():
                for shift, peer in enumerate(above):
                    iter_copy(keeper, matrix, shift, peer).wait_send()

            @pl.when(plane != keeper)
            def _():
                iter_copy(keeper, matrix, 0, plane).wait_recv()

    def attention_ortho(whole, target):
        cols = whole.shape[2]
        chunk = tile_sizes(depth, cols)[1]
        start, build_gram, build_mixer, step_on, last = ortho_steps(
            lambda span: whole[:, :, span].astype(jnp.float32).reshape(depth, chunk),
            block,
            chunk,
            wide_iterate.at[:, 0:cols],
            gram,
            mixer,
        )
        start()

        @pl.loop(0, NS_STEPS - 1)
        def _(step):
            build_gram()
            build_mixer()
            step_on()

        build_gram()
        kept = target.shape[0]
        if kept == depth:
            own = pl.ds(0, depth)
        else:
            own = pl.ds(pl.multiple_of(me * kept, kept), kept)
        last(own, kept, target)

    work += [send_iterates]

    for lane in order:
        to_chips(lane)
        if lane == order[0]:
            small_to_chips()
    stages = [to_planes, share_planes, make_moment, relay]
    for step in range(lanes + len(stages) - 1):
        for number in range(len(stages) - 1, -1, -1):
            if 0 <= step - number < lanes:
                stages[number](order[step - number])
        if step == 0:
            small_to_planes()
        if work:
            work.pop(0)()
        if step == lanes - 1:
            small_finish()
    while work:
        work.pop(0)()
    spread_finish(spreads[order[0]], relays[order[0]])
    attention_ortho(out_all, iter_out)
    for lane in order[1:]:
        spread_finish(spreads[lane], relays[lane])
    attention_ortho(qkv_all, iter_qkv)
    for copy in sends:
        copy.wait_send()
    await_iterates()


def reduce_attention(
    qkv_term,
    out_term,
    qkv_moment,
    out_moment,
    small,
    rows,
    hidden,
    expert_moment,
    router_moment,
):
    members, planes = lax.axis_size("expert"), lax.axis_size("dp")
    chips = members // 2
    share, width = out_moment.shape
    qkv_width = qkv_moment.shape[1]
    lanes = qkv_width // width + 1
    split = share % (8 * planes) == 0
    part = share // planes if split else share
    depth, units = expert_moment.shape
    kept = share if share % 16 == 0 else depth
    local = pl.BlockSpec(memory_space=pltpu.VMEM)
    dma = pltpu.SemaphoreType.DMA
    wide = jnp.bfloat16
    return pl.pallas_call(
        functools.partial(attention_kernel, chips, planes, split),
        out_shape=(
            jax.ShapeDtypeStruct(qkv_moment.shape, jnp.float32),
            jax.ShapeDtypeStruct(out_moment.shape, jnp.float32),
            jax.ShapeDtypeStruct(qkv_moment.shape, jnp.float32),
            jax.ShapeDtypeStruct(out_moment.shape, jnp.float32),
            jax.ShapeDtypeStruct(small.shape, jnp.float32),
            jax.ShapeDtypeStruct((kept, qkv_width), wide),
            jax.ShapeDtypeStruct((kept, width), wide),
            jax.ShapeDtypeStruct((2, depth // planes, units), jnp.float32),
            jax.ShapeDtypeStruct((2, depth // planes, units), wide),
            jax.ShapeDtypeStruct(router_moment.shape, jnp.float32),
        ),
        in_specs=[local] * 7 + [pl.BlockSpec(memory_space=pl.ANY), local],
        out_specs=[local] * 10,
        scratch_shapes=[
            pltpu.VMEM((members, share, qkv_width), wide),
            pltpu.VMEM((members, share, width), wide),
            pltpu.VMEM((depth, units), wide),
            pltpu.VMEM((depth, qkv_width), wide),
            pltpu.VMEM((depth, units), jnp.float32),
            pltpu.VMEM((depth, depth), wide),
            pltpu.VMEM((depth, depth), wide),
            pltpu.VMEM((lanes, chips, share, width), wide),
            pltpu.VMEM((lanes, chips - 1, share, width), wide),
            pltpu.VMEM((lanes, chips - 1, share, width), wide),
            pltpu.VMEM((lanes, planes, part, width) if split else (1, 1, part, width), wide),
            pltpu.VMEM((lanes, planes, part, width), wide),
            pltpu.VMEM((lanes, planes, part, width) if split else (1, 1, part, width), wide),
            pltpu.VMEM(small.shape, jnp.float32),
            pltpu.VMEM((chips,) + small.shape, jnp.float32),
            pltpu.VMEM((planes,) + small.shape, jnp.float32),
            dma((2, lanes, chips)),
            dma((2, lanes, chips - 1)),
            dma((2, lanes, planes - 1)),
            dma((2, lanes, planes - 1)),
            dma((4, lanes, chips)),
            dma((2, chips + planes - 1)),
            dma((2, max(2, planes - 1))),
            dma((1,)),
        ],
        compiler_params=pltpu.CompilerParams(
            collective_id=2, has_side_effects=True, vmem_limit_bytes=63 << 20
        ),
    )(
        qkv_term,
        out_term,
        qkv_moment,
        out_moment,
        small,
        rows,
        hidden,
        expert_moment,
        router_moment,
    )


def split_heads(qkv_rows, image_count, head_width):
    shaped = qkv_rows.reshape(image_count, SEQ, 3, HEADS, head_width)
    return (shaped[:, :, 0], shaped[:, :, 1], shaped[:, :, 2])


def attention_scores(query_rows, key_rows, score_scale):
    return (
        jnp.einsum("ishd,ithd->ihst", query_rows, key_rows, preferred_element_type=jnp.float32)
        * score_scale
    )


def body(
    tokens,
    cotangent,
    routes,
    priority,
    ln_gains,
    ln_biases,
    qkv_weight,
    out_weight,
    router,
    w_in,
    w_out,
    norm_momentum,
    router_momentum,
    qkv_momentum,
    out_momentum,
    w_in_momentum,
    w_out_momentum,
):
    token_count, model_width = tokens.shape
    experts = router.shape[1]
    hidden_units = w_in.shape[2]
    capacity = (token_count + experts - 1) // experts
    slots_all = experts * capacity
    dp_share = model_width // lax.axis_size("dp")
    image_count = token_count // SEQ
    head_width = model_width // HEADS
    score_scale = 1.0 / math.sqrt(head_width)
    first_weight = w_in[0]
    second_weight = w_out[0]
    cot_float = cotangent.astype(jnp.float32)
    dp_size = lax.axis_size("dp")
    dp_index = lax.axis_index("dp")
    members = lax.axis_size("expert")
    keep_first, keep_second = (dp_size // 2 - 1, dp_size // 2)
    full_qkv, full_out, every_moment = gather_weights(
        qkv_weight, out_weight, jnp.concatenate([w_in_momentum, w_out_momentum]).astype(jnp.bfloat16)
    )
    full_qkv = full_qkv.reshape(model_width, 3 * model_width)
    full_out = full_out.reshape(model_width, model_width)
    every_moment = every_moment.reshape(model_width, hidden_units)
    token_float = tokens.astype(jnp.float32)
    scaled_one, inverse_one, normed_one = layer_stats(token_float, ln_gains[0], ln_biases[0])
    attn_in = normed_one.astype(jnp.bfloat16)
    qkv_rows = jnp.dot(attn_in, full_qkv, preferred_element_type=jnp.float32).astype(jnp.bfloat16)
    query_rows, key_rows, value_rows = split_heads(qkv_rows, image_count, head_width)
    scores = attention_scores(query_rows, key_rows, score_scale)
    log_total = jnp.log(jnp.sum(jnp.exp(scores), axis=3, keepdims=True))
    attn_probs = jnp.exp(scores - log_total).astype(jnp.bfloat16)
    mixed_rows = (
        jnp.einsum("ihst,ithd->ishd", attn_probs, value_rows, preferred_element_type=jnp.float32)
        .astype(jnp.bfloat16)
        .reshape(token_count, model_width)
    )
    middle_rows = token_float + jnp.dot(mixed_rows, full_out, preferred_element_type=jnp.float32)
    stride = capacity + -capacity % 16
    slot_flat = slot_index(routes, priority[0], experts, capacity, stride)
    scaled, inverse, normed = layer_stats(middle_rows, ln_gains[1], ln_biases[1])
    logits = jnp.dot(normed, router, precision=highest)
    gate_values = gates_of(logits, routes)
    position = jnp.arange(experts * stride, dtype=jnp.int32)[:, None]
    pick_first = (slot_flat[:, 0][None, :] == position).astype(jnp.float32)
    pick_second = (slot_flat[:, 1][None, :] == position).astype(jnp.float32)
    placing = (pick_first + pick_second).astype(jnp.bfloat16)
    lean_first, lean_second = (pick_first.astype(jnp.bfloat16), pick_second.astype(jnp.bfloat16))
    gated = jnp.concatenate(
        [
            (gate_values[:, 0:1] * cot_float).astype(jnp.bfloat16),
            (gate_values[:, 1:2] * cot_float).astype(jnp.bfloat16),
        ],
        axis=0,
    )
    dispatch = jnp.dot(
        placing, normed.astype(jnp.bfloat16), preferred_element_type=jnp.float32
    ).astype(jnp.bfloat16)
    sent_grad = jnp.dot(
        jnp.concatenate([lean_first, lean_second], axis=1),
        gated,
        preferred_element_type=jnp.float32,
    ).astype(jnp.bfloat16)

    slot_rows = slots_all + -slots_all % 16
    packed = jnp.arange(slot_rows, dtype=jnp.int32)[:, None]
    packing = (
        (position[:, 0][None, :] == packed // capacity * stride + packed % capacity)
        & (packed < slots_all)
    ).astype(jnp.bfloat16)
    returned, every_rows, every_hidden = run_experts(
        jnp.concatenate([dispatch, sent_grad], axis=1).reshape(experts, stride, 2 * model_width),
        packing,
        first_weight,
        second_weight,
    )
    returned = returned.reshape(experts * stride, 2 * model_width)
    back_first = lax.dot_general(
        lean_first, returned, contract_first, preferred_element_type=jnp.float32
    )
    back_second = lax.dot_general(
        lean_second, returned, contract_first, preferred_element_type=jnp.float32
    )
    picked_first, picked_second = (back_first[:, :model_width], back_second[:, :model_width])
    block_out = middle_rows + (
        gate_values[:, 0:1] * picked_first + gate_values[:, 1:2] * picked_second
    )
    grad_gap = jnp.sum(picked_first * cot_float, axis=1) - jnp.sum(picked_second * cot_float, axis=1)
    logit_step = gate_values[:, 0] * gate_values[:, 1] * grad_gap
    columns = jnp.arange(experts, dtype=jnp.int32)[None, :]
    logit_grad = (
        (routes[:, 0:1] == columns).astype(jnp.float32)
        - (routes[:, 1:2] == columns).astype(jnp.float32)
    ) * logit_step[:, None]
    gathered = back_first[:, model_width:] + back_second[:, model_width:]
    normed_grad = gathered + lax.dot_general(
        logit_grad, router, contract_last, precision=highest
    )
    router_local = lax.dot_general(normed, logit_grad, contract_first, precision=highest)
    middle_grad = input_grad(cot_float, normed_grad, scaled, inverse, ln_gains[1])
    middle_rounded = middle_grad.astype(jnp.bfloat16)
    mixed_grad = lax.dot_general(
        middle_rounded, full_out, contract_last, preferred_element_type=jnp.float32
    ).astype(jnp.bfloat16)
    scores_again = attention_scores(query_rows, key_rows, score_scale)
    probs_again = jnp.exp(scores_again - log_total).astype(jnp.bfloat16)
    grad_heads = mixed_grad.reshape(image_count, SEQ, HEADS, head_width)
    value_grad = jnp.einsum(
        "ihst,ishd->ithd", probs_again, grad_heads, preferred_element_type=jnp.float32
    )
    prob_grad = jnp.einsum(
        "ishd,ithd->ihst", grad_heads, value_rows, preferred_element_type=jnp.float32
    )
    prob_float = probs_again.astype(jnp.float32)
    row_delta = jnp.sum(prob_float * prob_grad, axis=3, keepdims=True)
    score_grad = (prob_float * (prob_grad - row_delta) * score_scale).astype(jnp.bfloat16)
    query_grad = jnp.einsum(
        "ihst,ithd->ishd", score_grad, key_rows, preferred_element_type=jnp.float32
    )
    key_grad = jnp.einsum(
        "ihst,ishd->ithd", score_grad, query_rows, preferred_element_type=jnp.float32
    )
    qkv_grad = (
        jnp.stack([query_grad, key_grad, value_grad], axis=2)
        .astype(jnp.bfloat16)
        .reshape(token_count, 3 * model_width)
    )
    attn_in_grad = lax.dot_general(
        qkv_grad, full_qkv, contract_last, preferred_element_type=jnp.float32
    )
    grad_tokens = input_grad(middle_grad, attn_in_grad, scaled_one, inverse_one, ln_gains[0])
    qkv_term = lax.dot_general(
        attn_in, qkv_grad, contract_first, preferred_element_type=jnp.float32
    )
    out_term = lax.dot_general(
        mixed_rows, middle_rounded, contract_first, preferred_element_type=jnp.float32
    )
    norm_local = jnp.stack(
        [
            jnp.sum(attn_in_grad * scaled_one, axis=0),
            jnp.sum(normed_grad * scaled, axis=0),
            jnp.sum(attn_in_grad, axis=0),
            jnp.sum(normed_grad, axis=0),
        ]
    )
    small = jnp.concatenate([router_local.T, norm_local], axis=0)
    small_rows = experts + 4
    (
        grad_qkv,
        grad_out,
        moment_qkv,
        moment_out,
        small_total,
        iter_qkv,
        iter_out,
        expert_grads,
        iter_expert,
        iter_router,
    ) = reduce_attention(
        qkv_term.astype(jnp.bfloat16).reshape(members, -1, 3 * model_width),
        out_term.astype(jnp.bfloat16).reshape(members, -1, model_width),
        qkv_momentum,
        out_momentum,
        jnp.pad(small, ((0, -small_rows % 8), (0, 0))),
        every_rows,
        every_hidden,
        every_moment,
        router_momentum.T,
    )
    grad_router = small_total[:experts].T
    grad_norm = small_total[experts:small_rows]
    row_base = dp_index * dp_share
    grad_first, grad_second = (expert_grads[0], expert_grads[1])
    moment_first = decay_rate * w_in_momentum[0] + grad_first
    moment_second = decay_rate * w_out_momentum[0] + grad_second
    iter_first, iter_second = (iter_expert[0], iter_expert[1])
    expert_share = qkv_weight.shape[0]
    if iter_out.shape[0] != expert_share:
        expert_base = lax.axis_index("expert") * expert_share
        iter_out = lax.dynamic_slice_in_dim(iter_out, expert_base, expert_share, 0)
        iter_qkv = lax.dynamic_slice_in_dim(iter_qkv, expert_base, expert_share, 0)
    new_norm_momentum = decay_rate * norm_momentum + grad_norm
    new_norm = jnp.concatenate([ln_gains, ln_biases], axis=0) - norm_rate * new_norm_momentum
    new_router_momentum = decay_rate * router_momentum + grad_router
    new_router = router - matrix_rate * iter_router.T

    rows_first = lax.dynamic_slice_in_dim(first_weight, row_base, dp_share, 0).astype(jnp.float32)
    rows_second = lax.dynamic_slice_in_dim(second_weight, row_base, dp_share, 0).astype(jnp.float32)
    widen_factor = math.sqrt(max(1.0, hidden_units / model_width))
    new_first = rows_first - matrix_rate * widen_factor * iter_first.astype(jnp.float32)
    new_second = rows_second - matrix_rate * iter_second.astype(jnp.float32)
    new_qkv = qkv_weight.astype(jnp.float32) - matrix_rate * math.sqrt(3.0) * iter_qkv.astype(
        jnp.float32
    )
    new_out = out_weight.astype(jnp.float32) - matrix_rate * iter_out.astype(jnp.float32)
    return (
        block_out,
        grad_tokens,
        grad_norm,
        grad_router,
        grad_qkv,
        grad_out,
        grad_first[None],
        grad_second[None],
        new_norm,
        new_norm_momentum,
        new_router,
        new_router_momentum,
        new_qkv,
        moment_qkv,
        new_out,
        moment_out,
        new_first[None],
        moment_first[None],
        new_second[None],
        moment_second[None],
    )


def solution(mesh):
    in_specs = (
        P(("dp", "expert"), None),
        P(("dp", "expert"), None),
        P(("dp", "expert"), None),
        P(("dp", "expert"), None),
        P(),
        P(),
        P("expert", None),
        P("expert", None),
        P(),
        P("expert", None, None),
        P("expert", None, None),
        P(),
        P(),
        P("expert", None),
        P("expert", None),
        P("expert", "dp", None),
        P("expert", "dp", None),
    )
    out_specs = (
        P(("dp", "expert"), None),
        P(("dp", "expert"), None),
        P(),
        P(),
        P("expert", None),
        P("expert", None),
        P("expert", "dp", None),
        P("expert", "dp", None),
        P(),
        P(),
        P(),
        P(),
        P("expert", None),
        P("expert", None),
        P("expert", None),
        P("expert", None),
        P("expert", "dp", None),
        P("expert", "dp", None),
        P("expert", "dp", None),
        P("expert", "dp", None),
    )
    return jax.shard_map(body, mesh=mesh, in_specs=in_specs, out_specs=out_specs, check_vma=False)
```

```python
import functools
import math

import jax
import jax.numpy as jnp
from jax import lax
from jax.experimental import pallas as pl
from jax.experimental.pallas import tpu as pltpu
from jax.sharding import PartitionSpec as P

HEADS = 12
NS_STEPS = 5
SEQ = 197


quintic_one = 3.4445
quintic_two = -4.775
quintic_three = 2.0315
decay_rate = 0.9
matrix_rate = 0.2
norm_rate = 0.004
norm_eps = 1e-06
frob_eps = 1e-07
highest = lax.Precision.HIGHEST
contract_last = (((1,), (1,)), ((), ()))
contract_first = (((0,), (0,)), ((), ()))


def gelu_slope(preact):
    return (
        0.5 * (1.0 + lax.erf(preact * 0.7071067811865476))
        + preact * jnp.exp(-0.5 * preact * preact) * 0.3989422804014327
    )


def layer_stats(token_rows, gain, bias):
    centre = token_rows - jnp.mean(token_rows, axis=-1, keepdims=True)
    inverse = lax.rsqrt(jnp.mean(centre * centre, axis=-1, keepdims=True) + norm_eps)
    scaled = centre * inverse
    return (scaled, inverse, scaled * gain + bias)


def slot_index(choice_ids, order_rows, experts, capacity, stride):
    token_count = choice_ids.shape[0]
    ranks = jnp.arange(token_count, dtype=jnp.int32)
    turn = jnp.sum(
        jnp.where(order_rows[:, None] == ranks[None, :], ranks[:, None], 0), axis=0, dtype=jnp.int32
    )
    earlier = (turn[None, :] < turn[:, None]).astype(jnp.bfloat16)
    columns = jnp.arange(experts, dtype=jnp.int32)[None, :]
    first = (choice_ids[:, 0:1] == columns).astype(jnp.bfloat16)
    second = (choice_ids[:, 1:2] == columns).astype(jnp.bfloat16)
    counts = jnp.dot(
        earlier, jnp.concatenate([first, second], axis=1), preferred_element_type=jnp.float32
    )
    first_float, second_float = first.astype(jnp.float32), second.astype(jnp.float32)
    first_slot = jnp.sum(counts[:, :experts] * first_float, axis=1)
    second_slot = jnp.sum(
        (counts[:, experts:] + jnp.sum(first_float, axis=0, keepdims=True)) * second_float, axis=1
    )
    slot_values = jnp.stack([first_slot, second_slot], axis=1).astype(jnp.int32)
    return jnp.where(
        slot_values < capacity, choice_ids * stride + slot_values, experts * stride
    )


def gates_of(logits, choice_ids):
    columns = jnp.arange(logits.shape[1], dtype=jnp.int32)[None, :]
    first_logit = jnp.sum(jnp.where(choice_ids[:, 0:1] == columns, logits, 0.0), axis=1)
    second_logit = jnp.sum(jnp.where(choice_ids[:, 1:2] == columns, logits, 0.0), axis=1)
    first_gate = jax.nn.sigmoid(first_logit - second_logit)
    return jnp.stack([first_gate, 1.0 - first_gate], axis=1)


def input_grad(base_grad, normed_grad, scaled, inverse, gain):
    lifted = normed_grad * gain
    centred = (
        lifted
        - jnp.mean(lifted, axis=-1, keepdims=True)
        - scaled * jnp.mean(lifted * scaled, axis=-1, keepdims=True)
    )
    return base_grad + inverse * centred


def ortho_steps(read, block, tile, iterate, gram, mixer):
    rows, cols = iterate.shape
    tiles = cols // tile

    def begin():
        def squares(index, total):
            part = read(pl.ds(pl.multiple_of(index * tile, tile), tile))
            return total + jnp.sum(part * part, axis=0, keepdims=True)

        total = lax.fori_loop(0, tiles, squares, jnp.zeros((1, tile), jnp.float32))
        norm = jnp.sqrt(jnp.sum(total)) + frob_eps

        @pl.loop(0, tiles)
        def _(index):
            span = pl.ds(pl.multiple_of(index * tile, tile), tile)
            iterate[:, span] = (read(span) / norm).astype(jnp.bfloat16)

    def mirror(target, part, index):
        target[index * block : (index + 1) * block, 0 : (index + 1) * block] = part
        for other in range(index):
            target[other * block : (other + 1) * block, index * block : (index + 1) * block] = part[
                :, other * block : (other + 1) * block
            ].T

    def make_gram():
        for index in range(rows // block):
            mirror(
                gram,
                lax.dot_general(
                    iterate[index * block : (index + 1) * block, :],
                    iterate[0 : (index + 1) * block, :],
                    contract_last,
                    preferred_element_type=jnp.float32,
                ).astype(jnp.bfloat16),
                index,
            )

    def mix(gram_rows, gram_part, gram_columns):
        return (
            quintic_two * gram_part.astype(jnp.float32)
            + quintic_three * jnp.dot(gram_rows, gram_columns, preferred_element_type=jnp.float32)
        ).astype(jnp.bfloat16)

    def apply(mixer_rows, part, columns):
        return (
            quintic_one * part.astype(jnp.float32)
            + jnp.dot(mixer_rows, columns, preferred_element_type=jnp.float32)
        ).astype(jnp.bfloat16)

    def make_mixer():
        for index in range(rows // block):
            span = pl.ds(index * block, block)
            reach = (index + 1) * block
            mirror(mixer, mix(gram[span, :], gram[span, 0:reach], gram[:, 0:reach]), index)

    def advance():
        @pl.loop(0, tiles)
        def _(index):
            span = pl.ds(pl.multiple_of(index * tile, tile), tile)
            columns = iterate[:, span]
            iterate[:, span] = apply(mixer[...], columns, columns)

    def last_rows(own, row_count, out_ref):
        mixer[0:row_count, :] = mix(gram[own, :], gram[own, :], gram[...])

        @pl.loop(0, tiles)
        def _(index):
            span = pl.ds(pl.multiple_of(index * tile, tile), tile)
            out_ref[:, span] = apply(mixer[0:row_count, :], iterate[own, span], iterate[:, span])

    return begin, make_gram, make_mixer, advance, last_rows


def tile_sizes(rows, cols):
    block = next(size for size in (256, 128, rows) if rows % size == 0)
    tile = next(size for size in (768, 512, 256, 128, cols) if cols % size == 0)
    return block, tile


MESH = pl.DeviceIdType.MESH


def at_expert(index):
    return {"expert": index}


def at_dp(index):
    return {"dp": index}


def remote(source, target, send_sem, recv_sem, device):
    return pltpu.make_async_remote_copy(
        src_ref=source,
        dst_ref=target,
        send_sem=send_sem,
        recv_sem=recv_sem,
        device_id=device,
        device_id_type=MESH,
    )


def greet(devices):
    barrier = pltpu.get_barrier_semaphore()
    for device in devices:
        pl.semaphore_signal(barrier, inc=1, device_id=device, device_id_type=MESH)
    pl.semaphore_wait(barrier, len(devices))


def neighbours(chips, planes):
    me = lax.axis_index("expert")
    core, chip = lax.rem(me, 2), lax.div(me, 2)
    plane = lax.axis_index("dp")
    ahead = [2 * lax.rem(chip + shift, chips) + core for shift in range(1, chips)]
    behind = [2 * lax.rem(chip + chips - shift, chips) + core for shift in range(1, chips)]
    above = [lax.rem(plane + shift, planes) for shift in range(1, planes)]
    return me, core, chip, plane, me + 1 - 2 * core, ahead, behind, above


def spread_start(piece, me, partner, ahead, sems, lane):
    copies = [remote(piece(me), piece(me), sems.at[0, lane, 0], sems.at[1, lane, 0], at_expert(partner))]
    for shift, peer in enumerate(ahead, 1):
        copies.append(
            remote(piece(me), piece(me), sems.at[0, lane, shift], sems.at[1, lane, shift], at_expert(peer))
        )
    for copy in copies:
        copy.start()
    return copies


def spread_relay(piece, copies, partner, behind, sems, lane):
    relays = []
    for shift, source in enumerate(behind, 1):
        copies[shift].wait_recv()
        relay = remote(
            piece(source), piece(source), sems.at[2, lane, shift], sems.at[3, lane, shift], at_expert(partner)
        )
        relay.start()
        relays.append(relay)
    return relays


def spread_finish(copies, relays):
    copies[0].wait_recv()
    for relay in relays:
        relay.wait_recv()
    for copy in copies + relays:
        copy.wait_send()


def weights_kernel(
    chips, planes, qkv_ref, out_ref, moments_ref, qkv_all, out_all, moments_all, spread_sems, moment_sems, local_sems
):
    me, core, chip, plane, partner, ahead, behind, above = neighbours(chips, planes)
    greet([at_expert(i) for i in [partner] + ahead] + [at_dp(i) for i in above])
    own_copies = [
        pltpu.make_async_copy(qkv_ref, qkv_all.at[me], local_sems.at[0]),
        pltpu.make_async_copy(out_ref, out_all.at[me], local_sems.at[1]),
    ]
    lanes = []
    for lane, (source, target) in enumerate(((qkv_ref, qkv_all), (out_ref, out_all))):
        copies = [
            remote(
                source,
                target.at[me],
                spread_sems.at[0, lane, shift],
                spread_sems.at[1, lane, shift],
                at_expert(peer),
            )
            for shift, peer in enumerate([partner] + ahead)
        ]
        for copy in copies[1:] + copies[:1]:
            copy.start()
        lanes.append((lane, target, copies))
    keepers = (planes // 2 - 1, planes // 2)
    for which, keeper in enumerate(keepers):

        @pl.when(plane != keeper)
        def _():
            remote(
                moments_ref.at[which],
                moments_all.at[plane],
                moment_sems.at[0, which],
                moment_sems.at[1, plane],
                at_dp(keeper),
            ).start()

        @pl.when(plane == keeper)
        def _():
            pltpu.make_async_copy(
                moments_ref.at[which], moments_all.at[plane], local_sems.at[2]
            ).start()

    for copy in own_copies:
        copy.start()
    relayed = [
        (copies, spread_relay(lambda i: target.at[i], copies, partner, behind, spread_sems, lane))
        for lane, target, copies in lanes
    ]
    for copies, relays in relayed:
        spread_finish(copies, relays)
    for copy in own_copies:
        copy.wait()
    for which, keeper in enumerate(keepers):

        @pl.when(plane != keeper)
        def _():
            remote(
                moments_ref.at[which],
                moments_all.at[plane],
                moment_sems.at[0, which],
                moment_sems.at[1, plane],
                at_dp(keeper),
            ).wait_send()

        @pl.when(plane == keeper)
        def _():
            pltpu.make_async_copy(
                moments_ref.at[which], moments_all.at[plane], local_sems.at[2]
            ).wait()
            for source in range(planes):
                if source != keeper:
                    remote(
                        moments_ref.at[which],
                        moments_all.at[source],
                        moment_sems.at[0, which],
                        moment_sems.at[1, source],
                        at_dp(source),
                    ).wait_recv()


def gather_weights(qkv_weight, out_weight, moments):
    members, planes = lax.axis_size("expert"), lax.axis_size("dp")
    chips = members // 2
    anywhere = pl.BlockSpec(memory_space=pl.ANY)
    return pl.pallas_call(
        functools.partial(weights_kernel, chips, planes),
        out_shape=(
            jax.ShapeDtypeStruct((members,) + qkv_weight.shape, jnp.bfloat16),
            jax.ShapeDtypeStruct((members,) + out_weight.shape, jnp.bfloat16),
            jax.ShapeDtypeStruct((planes,) + moments.shape[1:], jnp.bfloat16),
        ),
        in_specs=[anywhere] * 3,
        out_specs=[anywhere] * 3,
        scratch_shapes=[
            pltpu.SemaphoreType.DMA((4, 2, chips)),
            pltpu.SemaphoreType.DMA((2, max(2, planes))),
            pltpu.SemaphoreType.DMA((3,)),
        ],
        compiler_params=pltpu.CompilerParams(collective_id=1, has_side_effects=True),
    )(qkv_weight, out_weight, moments)


def expert_kernel(
    members,
    planes,
    blocks_ref,
    packing_ref,
    first_weight,
    second_weight,
    back_ref,
    rows_all,
    hidden,
    arrived,
    leaving,
    outcome,
    go_sems,
    back_sems,
    rows_sems,
):
    me, plane = lax.axis_index("expert"), lax.axis_index("dp")
    others = [lax.rem(me + shift, members) for shift in range(1, members)]
    above = [lax.rem(plane + shift, planes) for shift in range(1, planes)]
    greet([at_expert(i) for i in others] + [at_dp(i) for i in above])

    def exchange(source, target, sems):
        copies = [
            remote(source.at[peer], target.at[me], sems.at[0, i], sems.at[1, i], at_expert(peer))
            for i, peer in enumerate(others)
        ]
        for copy in copies:
            copy.start()
        target[me] = source[me]
        return copies

    depth, units = first_weight.shape
    stride = blocks_ref.shape[1]
    gone = exchange(blocks_ref, arrived, go_sems)
    for copy in gone:
        copy.wait_recv()
    rows_all[plane] = jnp.dot(
        packing_ref[...],
        arrived[...].reshape(members * stride, 2 * depth),
        preferred_element_type=jnp.float32,
    ).astype(jnp.bfloat16)
    last = planes - 1

    def hop(way, number, block):
        return remote(
            rows_all.at[block],
            rows_all.at[block],
            rows_sems.at[0, way, number],
            rows_sems.at[1, way, number],
            at_dp(lax.rem(plane + planes + 1 - 2 * way, planes)),
        )

    def can_send(way, number):
        if way == 0:
            return (plane < last) & (plane >= number)
        return (plane > 0) & (plane + number <= last)

    def block_of(way, number):
        return plane - number if way == 0 else plane + number

    for way in range(2):

        @pl.when(can_send(way, 0))
        def _():
            hop(way, 0, plane).start()

    block = tile_sizes(depth, units)[0]

    def hidden_rows(source):
        @pl.loop(0, units // block)
        def _(index):
            span = pl.ds(pl.multiple_of(index * block, block), block)
            preact = jnp.dot(
                rows_all[source, :, 0:depth], first_weight[:, span], preferred_element_type=jnp.float32
            )
            act_grad = jnp.dot(
                rows_all[source, :, depth : 2 * depth],
                second_weight[:, span],
                preferred_element_type=jnp.float32,
            )
            share = 0.5 * (1.0 + lax.erf(preact * 0.7071067811865476))
            slope = share + preact * jnp.exp(-0.5 * preact * preact) * 0.3989422804014327
            hidden[0, source, :, span] = (act_grad * slope).astype(jnp.bfloat16)
            hidden[1, source, :, span] = (preact * share).astype(jnp.bfloat16)

    hidden_rows(plane)
    for part, weight in enumerate((second_weight, first_weight)):
        for start in range(0, depth, block):
            outcome[:, part * depth + start : part * depth + start + block] = lax.dot_general(
                hidden[1 - part, plane],
                weight[start : start + block, :],
                contract_last,
                preferred_element_type=jnp.float32,
            ).astype(jnp.bfloat16)
    leaving[...] = (
        lax.dot_general(
            packing_ref[...], outcome[...], contract_first, preferred_element_type=jnp.float32
        )
        .astype(jnp.bfloat16)
        .reshape(members, stride, 2 * depth)
    )
    returned = exchange(leaving, back_ref, back_sems)
    for number in range(1, planes):
        arrives = (plane >= number, plane + number <= last)
        for way in range(2):

            @pl.when(arrives[way])
            def _():
                source = block_of(way, number)
                hop(way, number - 1, source).wait_recv()

            if number < last:

                @pl.when(can_send(way, number))
                def _():
                    hop(way, number, block_of(way, number)).start()

        for way in range(2):

            @pl.when(arrives[way])
            def _():
                hidden_rows(block_of(way, number))

    for copy in returned:
        copy.wait_recv()
    for copy in gone + returned:
        copy.wait_send()
    for number in range(last):
        for way in range(2):

            @pl.when(can_send(way, number))
            def _():
                hop(way, number, block_of(way, number)).wait_send()


def run_experts(blocks, packing, first_weight, second_weight):
    members, planes = lax.axis_size("expert"), lax.axis_size("dp")
    slots = packing.shape[0]
    depth, units = first_weight.shape
    local = pl.BlockSpec(memory_space=pltpu.VMEM)
    dma = pltpu.SemaphoreType.DMA
    wide = jnp.bfloat16
    return pl.pallas_call(
        functools.partial(expert_kernel, members, planes),
        out_shape=(
            jax.ShapeDtypeStruct(blocks.shape, wide),
            jax.ShapeDtypeStruct((planes, slots, 2 * depth), wide),
            jax.ShapeDtypeStruct((2, planes, slots, units), wide),
        ),
        in_specs=[local] * 4,
        out_specs=[local] * 3,
        scratch_shapes=[
            pltpu.VMEM(blocks.shape, wide),
            pltpu.VMEM(blocks.shape, wide),
            pltpu.VMEM((slots, 2 * depth), wide),
            dma((2, members - 1)),
            dma((2, members - 1)),
            dma((2, 2, planes - 1)),
        ],
        compiler_params=pltpu.CompilerParams(
            collective_id=3, has_side_effects=True, vmem_limit_bytes=48 << 20
        ),
    )(blocks, packing, first_weight, second_weight)


def attention_kernel(
    chips,
    planes,
    split,
    qkv_term,
    out_term,
    qkv_moment,
    out_moment,
    small_ref,
    rows_all,
    hidden,
    expert_moment,
    router_moment,
    grad_qkv,
    grad_out,
    new_qkv_moment,
    new_out_moment,
    small_out,
    iter_qkv,
    iter_out,
    expert_grads,
    iter_expert,
    iter_router,
    qkv_all,
    out_all,
    iterate,
    wide_iterate,
    expert_total,
    gram,
    mixer,
    crossed,
    leaving,
    landed,
    plane_out,
    plane_in,
    plane_all,
    small_pair,
    small_chip,
    small_plane,
    cross_sems,
    chip_sems,
    plane_sems,
    share_sems,
    spread_sems,
    small_sems,
    iter_sems,
    local_sems,
):
    width = out_term.shape[2]
    lanes = qkv_term.shape[2] // width + 1
    me, core, chip, plane, partner, ahead, behind, above = neighbours(chips, planes)
    greet([at_expert(i) for i in [partner] + ahead] + [at_dp(i) for i in above])

    def cut(pair, lane):
        if lane == lanes - 1:
            return pair[1], pl.ds(0, width)
        return pair[0], pl.ds(lane * width, width)

    def term(lane, index):
        ref, columns = cut((qkv_term, out_term), lane)
        return ref[index, :, columns].astype(jnp.float32)

    order = [lanes - 1] + list(range(lanes - 1))
    crosses = {}
    for lane in order:
        for shift in range(chips):
            target = lax.rem(chip + shift, chips)
            ref, columns = cut((qkv_term, out_term), lane)
            crosses[lane, shift] = remote(
                ref.at[2 * target + 1 - core, :, columns],
                crossed.at[lane, target],
                cross_sems.at[0, lane, shift],
                cross_sems.at[1, lane, shift],
                at_expert(partner),
            )
        for shift in list(range(1, chips)) + [0]:
            crosses[lane, shift].start()
    small_copy = remote(small_ref, small_pair, small_sems.at[0, 0], small_sems.at[1, 0], at_expert(partner))
    small_copy.start()
    sends = list(crosses.values()) + [small_copy]
    moment_copy = pltpu.make_async_copy(expert_moment, iterate, local_sems.at[0])
    moment_copy.start()

    chip_copies = {}

    def to_chips(lane):
        for shift in range(1, chips):
            target = lax.rem(chip + shift, chips)
            crosses[lane, shift].wait_recv()
            leaving[lane, shift - 1] = (
                term(lane, 2 * target + core) + crossed[lane, target].astype(jnp.float32)
            ).astype(jnp.bfloat16)
            copy = remote(
                leaving.at[lane, shift - 1],
                landed.at[lane, shift - 1],
                chip_sems.at[0, lane, shift - 1],
                chip_sems.at[1, lane, shift - 1],
                at_expert(ahead[shift - 1]),
            )
            copy.start()
            chip_copies[lane, shift] = copy
            sends.append(copy)

    small_chip_copies = []

    def small_to_chips():
        small_copy.wait_recv()
        small_chip[chip] = small_ref[...] + small_pair[...]
        for shift, peer in enumerate(ahead, 1):
            copy = remote(
                small_chip.at[chip],
                small_chip.at[chip],
                small_sems.at[0, shift],
                small_sems.at[1, shift],
                at_expert(peer),
            )
            copy.start()
            small_chip_copies.append(copy)
            sends.append(copy)

    small_plane_copies = []

    def small_to_planes():
        for copy in small_chip_copies:
            copy.wait_recv()
        small_plane[plane] = sum(small_chip[i] for i in range(chips))
        for i, peer in enumerate(above):
            copy = remote(
                small_plane.at[plane],
                small_plane.at[plane],
                small_sems.at[0, chips + i],
                small_sems.at[1, chips + i],
                at_dp(peer),
            )
            copy.start()
            small_plane_copies.append(copy)
            sends.append(copy)

    def small_finish():
        for copy in small_plane_copies:
            copy.wait_recv()
        small_out[...] = sum(small_plane[i] for i in range(planes))
        count = router_moment.shape[0]
        fresh = decay_rate * router_moment[...] + small_out[0:count, :]
        norm = jnp.sqrt(jnp.sum(fresh * fresh)) + frob_eps

        def rounded(values):
            return values.astype(jnp.bfloat16).astype(jnp.float32)

        turned = rounded(fresh / norm)
        for _ in range(NS_STEPS):
            product = rounded(
                lax.dot_general(turned, turned, contract_last, preferred_element_type=jnp.float32)
            )
            blend = rounded(
                quintic_two * product
                + quintic_three * jnp.dot(product, product, preferred_element_type=jnp.float32)
            )
            turned = rounded(
                quintic_one * turned + jnp.dot(blend, turned, preferred_element_type=jnp.float32)
            )
        iter_router[...] = turned

    part = plane_out.shape[2]
    plane_copies = {}

    def to_planes(lane):
        crosses[lane, 0].wait_recv()
        total = term(lane, me) + crossed[lane, chip].astype(jnp.float32)
        for shift in range(1, chips):
            chip_copies[lane, shift].wait_recv()
            total = total + landed[lane, shift - 1].astype(jnp.float32)
        if split:
            for i in range(planes):
                plane_out[lane, i] = total[i * part : (i + 1) * part].astype(jnp.bfloat16)
        else:
            plane_in[lane, plane] = total.astype(jnp.bfloat16)
        plane_copies[lane] = []
        for i, peer in enumerate(above):
            copy = remote(
                plane_out.at[lane, peer] if split else plane_in.at[lane, plane],
                plane_in.at[lane, plane],
                plane_sems.at[0, lane, i],
                plane_sems.at[1, lane, i],
                at_dp(peer),
            )
            copy.start()
            plane_copies[lane].append(copy)
            sends.append(copy)

    share_copies = {}

    def share_planes(lane):
        share_copies[lane] = []
        if not split:
            return
        for copy in plane_copies[lane]:
            copy.wait_recv()
        plane_in[lane, plane] = plane_out[lane, plane]
        total = plane_in[lane, 0].astype(jnp.float32)
        for i in range(1, planes):
            total = total + plane_in[lane, i].astype(jnp.float32)
        plane_all[lane, plane] = total.astype(jnp.bfloat16)
        for i, peer in enumerate(above):
            copy = remote(
                plane_all.at[lane, plane],
                plane_all.at[lane, plane],
                share_sems.at[0, lane, i],
                share_sems.at[1, lane, i],
                at_dp(peer),
            )
            copy.start()
            share_copies[lane].append(copy)
            sends.append(copy)

    def piece_of(lane):
        ref, columns = cut((qkv_all, out_all), lane)
        return lambda index: ref.at[index, :, columns]

    spreads, relays = {}, {}

    def make_moment(lane):
        moment, columns = cut((qkv_moment, out_moment), lane)
        grad_target, _ = cut((grad_qkv, grad_out), lane)
        moment_target, _ = cut((new_qkv_moment, new_out_moment), lane)
        whole, _ = cut((qkv_all, out_all), lane)
        if split:
            for copy in share_copies[lane]:
                copy.wait_recv()
            grad = jnp.concatenate(
                [plane_all[lane, i].astype(jnp.float32) for i in range(planes)], axis=0
            )
        else:
            for copy in plane_copies[lane]:
                copy.wait_recv()
            grad = sum(plane_in[lane, i].astype(jnp.float32) for i in range(planes))
        fresh = decay_rate * moment[:, columns] + grad
        grad_target[:, columns] = grad
        moment_target[:, columns] = fresh
        whole[me, :, columns] = fresh.astype(jnp.bfloat16)
        spreads[lane] = spread_start(piece_of(lane), me, partner, ahead, spread_sems, lane)

    def relay(lane):
        relays[lane] = spread_relay(piece_of(lane), spreads[lane], partner, behind, spread_sems, lane)

    depth, units = iterate.shape
    block, tile = tile_sizes(depth, units)
    which = jnp.where(plane == planes // 2 - 1, 0, 1)
    slots = planes * rows_all.shape[1]

    def expert_grad(matrix):
        @pl.loop(0, depth // block)
        def _(index):
            columns = pl.ds(pl.multiple_of(matrix * depth + index * block, block), block)
            left = rows_all[:, :, columns].reshape(slots, block)
            target = pl.ds(pl.multiple_of(index * block, block), block)
            for start in range(0, units, tile):
                expert_total[target, start : start + tile] = lax.dot_general(
                    left,
                    hidden[matrix, :, :, start : start + tile].reshape(slots, tile),
                    contract_first,
                    preferred_element_type=jnp.float32,
                )

        share = expert_grads.shape[1]
        own = pl.ds(pl.multiple_of(plane * share, share), share)
        expert_grads[matrix] = expert_total[own, :]

    def add_moment():
        moment_copy.wait()

        @pl.loop(0, units // tile)
        def _(index):
            span = pl.ds(pl.multiple_of(index * tile, tile), tile)
            expert_total[:, span] = (
                decay_rate * iterate[:, span].astype(jnp.float32) + expert_total[:, span]
            )

    begin, make_gram, make_mixer, advance, last_rows = ortho_steps(
        lambda span: expert_total[:, span], block, tile, iterate, gram, mixer
    )

    def ortho_step():
        make_gram()
        make_mixer()
        advance()

    def begin_ortho():
        add_moment()
        begin()

    work = [functools.partial(expert_grad, 1 - which), functools.partial(expert_grad, which)]
    work += [begin_ortho] + [ortho_step] * NS_STEPS

    expert_share = expert_grads.shape[1]
    keepers = (planes // 2 - 1, planes // 2)

    def iter_copy(keeper, matrix, shift, peer):
        own = pl.ds(pl.multiple_of(peer * expert_share, expert_share), expert_share)
        return remote(
            iterate.at[own, :],
            iter_expert.at[matrix],
            iter_sems.at[0, shift],
            iter_sems.at[1, matrix],
            at_dp(peer),
        )

    def send_iterates():
        for matrix, keeper in enumerate(keepers):

            @pl.when(plane == keeper)
            def _():
                for shift, peer in enumerate(above):
                    iter_copy(keeper, matrix, shift, peer).start()
                iter_expert[matrix] = iterate[keeper * expert_share : (keeper + 1) * expert_share, :]

    def await_iterates():
        for matrix, keeper in enumerate(keepers):

            @pl.when(plane == keeper)
            def _():
                for shift, peer in enumerate(above):
                    iter_copy(keeper, matrix, shift, peer).wait_send()

            @pl.when(plane != keeper)
            def _():
                iter_copy(keeper, matrix, 0, plane).wait_recv()

    def attention_ortho(whole, target):
        cols = whole.shape[2]
        chunk = tile_sizes(depth, cols)[1]
        start, build_gram, build_mixer, step_on, last = ortho_steps(
            lambda span: whole[:, :, span].astype(jnp.float32).reshape(depth, chunk),
            block,
            chunk,
            wide_iterate.at[:, 0:cols],
            gram,
            mixer,
        )
        kept = target.shape[0]

        def advance_once():
            build_gram()
            build_mixer()
            step_on()

        def complete():
            build_gram()
            if kept == depth:
                own = pl.ds(0, depth)
            else:
                own = pl.ds(pl.multiple_of(me * kept, kept), kept)
            last(own, kept, target)

        return start, advance_once, complete

    def begin_out():
        spread_finish(spreads[order[0]], relays[order[0]])
        out_start()

    out_start, out_advance, out_complete = attention_ortho(out_all, iter_out)
    early = work
    turns = {0: early[:3], 1: early[3:5], 2: early[5:7], 3: early[7:]}
    late = max(4, lanes)
    turns[late] = [begin_out, out_advance, out_advance]
    turns[late + 1] = [send_iterates, out_advance, out_advance]
    turns[late + 2] = [out_complete]

    for lane in order:
        to_chips(lane)
        if lane == order[0]:
            small_to_chips()
    stages = [to_planes, share_planes, make_moment, relay]
    for step in range(lanes + len(stages) - 1):
        for number in range(len(stages) - 1, -1, -1):
            if 0 <= step - number < lanes:
                stages[number](order[step - number])
        if step == 0:
            small_to_planes()
        for turn in turns.pop(step, []):
            turn()
        if step == lanes - 1:
            small_finish()
    for step in sorted(turns):
        for turn in turns[step]:
            turn()
    for lane in order[1:]:
        spread_finish(spreads[lane], relays[lane])
    qkv_start, qkv_advance, qkv_complete = attention_ortho(qkv_all, iter_qkv)
    qkv_start()

    @pl.loop(0, NS_STEPS - 1)
    def _(step):
        qkv_advance()

    qkv_complete()
    for copy in sends:
        copy.wait_send()
    await_iterates()


def reduce_attention(
    qkv_term,
    out_term,
    qkv_moment,
    out_moment,
    small,
    rows,
    hidden,
    expert_moment,
    router_moment,
):
    members, planes = lax.axis_size("expert"), lax.axis_size("dp")
    chips = members // 2
    share, width = out_moment.shape
    qkv_width = qkv_moment.shape[1]
    lanes = qkv_width // width + 1
    split = share % (8 * planes) == 0
    part = share // planes if split else share
    depth, units = expert_moment.shape
    kept = share if share % 16 == 0 else depth
    local = pl.BlockSpec(memory_space=pltpu.VMEM)
    dma = pltpu.SemaphoreType.DMA
    wide = jnp.bfloat16
    return pl.pallas_call(
        functools.partial(attention_kernel, chips, planes, split),
        out_shape=(
            jax.ShapeDtypeStruct(qkv_moment.shape, jnp.float32),
            jax.ShapeDtypeStruct(out_moment.shape, jnp.float32),
            jax.ShapeDtypeStruct(qkv_moment.shape, jnp.float32),
            jax.ShapeDtypeStruct(out_moment.shape, jnp.float32),
            jax.ShapeDtypeStruct(small.shape, jnp.float32),
            jax.ShapeDtypeStruct((kept, qkv_width), wide),
            jax.ShapeDtypeStruct((kept, width), wide),
            jax.ShapeDtypeStruct((2, depth // planes, units), jnp.float32),
            jax.ShapeDtypeStruct((2, depth // planes, units), wide),
            jax.ShapeDtypeStruct(router_moment.shape, jnp.float32),
        ),
        in_specs=[local] * 7 + [pl.BlockSpec(memory_space=pl.ANY), local],
        out_specs=[local] * 10,
        scratch_shapes=[
            pltpu.VMEM((members, share, qkv_width), wide),
            pltpu.VMEM((members, share, width), wide),
            pltpu.VMEM((depth, units), wide),
            pltpu.VMEM((depth, qkv_width), wide),
            pltpu.VMEM((depth, units), jnp.float32),
            pltpu.VMEM((depth, depth), wide),
            pltpu.VMEM((depth, depth), wide),
            pltpu.VMEM((lanes, chips, share, width), wide),
            pltpu.VMEM((lanes, chips - 1, share, width), wide),
            pltpu.VMEM((lanes, chips - 1, share, width), wide),
            pltpu.VMEM((lanes, planes, part, width) if split else (1, 1, part, width), wide),
            pltpu.VMEM((lanes, planes, part, width), wide),
            pltpu.VMEM((lanes, planes, part, width) if split else (1, 1, part, width), wide),
            pltpu.VMEM(small.shape, jnp.float32),
            pltpu.VMEM((chips,) + small.shape, jnp.float32),
            pltpu.VMEM((planes,) + small.shape, jnp.float32),
            dma((2, lanes, chips)),
            dma((2, lanes, chips - 1)),
            dma((2, lanes, planes - 1)),
            dma((2, lanes, planes - 1)),
            dma((4, lanes, chips)),
            dma((2, chips + planes - 1)),
            dma((2, max(2, planes - 1))),
            dma((1,)),
        ],
        compiler_params=pltpu.CompilerParams(
            collective_id=2, has_side_effects=True, vmem_limit_bytes=63 << 20
        ),
    )(
        qkv_term,
        out_term,
        qkv_moment,
        out_moment,
        small,
        rows,
        hidden,
        expert_moment,
        router_moment,
    )


def split_heads(qkv_rows, image_count, head_width):
    shaped = qkv_rows.reshape(image_count, SEQ, 3, HEADS, head_width)
    return (shaped[:, :, 0], shaped[:, :, 1], shaped[:, :, 2])


def attention_scores(query_rows, key_rows, score_scale):
    return (
        jnp.einsum("ishd,ithd->ihst", query_rows, key_rows, preferred_element_type=jnp.float32)
        * score_scale
    )


def body(
    tokens,
    cotangent,
    routes,
    priority,
    ln_gains,
    ln_biases,
    qkv_weight,
    out_weight,
    router,
    w_in,
    w_out,
    norm_momentum,
    router_momentum,
    qkv_momentum,
    out_momentum,
    w_in_momentum,
    w_out_momentum,
):
    token_count, model_width = tokens.shape
    experts = router.shape[1]
    hidden_units = w_in.shape[2]
    capacity = (token_count + experts - 1) // experts
    slots_all = experts * capacity
    dp_share = model_width // lax.axis_size("dp")
    image_count = token_count // SEQ
    head_width = model_width // HEADS
    score_scale = 1.0 / math.sqrt(head_width)
    first_weight = w_in[0]
    second_weight = w_out[0]
    cot_float = cotangent.astype(jnp.float32)
    dp_size = lax.axis_size("dp")
    dp_index = lax.axis_index("dp")
    members = lax.axis_size("expert")
    keep_first, keep_second = (dp_size // 2 - 1, dp_size // 2)
    full_qkv, full_out, every_moment = gather_weights(
        qkv_weight, out_weight, jnp.concatenate([w_in_momentum, w_out_momentum]).astype(jnp.bfloat16)
    )
    full_qkv = full_qkv.reshape(model_width, 3 * model_width)
    full_out = full_out.reshape(model_width, model_width)
    every_moment = every_moment.reshape(model_width, hidden_units)
    token_float = tokens.astype(jnp.float32)
    scaled_one, inverse_one, normed_one = layer_stats(token_float, ln_gains[0], ln_biases[0])
    attn_in = normed_one.astype(jnp.bfloat16)
    qkv_rows = jnp.dot(attn_in, full_qkv, preferred_element_type=jnp.float32).astype(jnp.bfloat16)
    query_rows, key_rows, value_rows = split_heads(qkv_rows, image_count, head_width)
    scores = attention_scores(query_rows, key_rows, score_scale)
    log_total = jnp.log(jnp.sum(jnp.exp(scores), axis=3, keepdims=True))
    attn_probs = jnp.exp(scores - log_total).astype(jnp.bfloat16)
    mixed_rows = (
        jnp.einsum("ihst,ithd->ishd", attn_probs, value_rows, preferred_element_type=jnp.float32)
        .astype(jnp.bfloat16)
        .reshape(token_count, model_width)
    )
    middle_rows = token_float + jnp.dot(mixed_rows, full_out, preferred_element_type=jnp.float32)
    stride = capacity + -capacity % 16
    slot_flat = slot_index(routes, priority[0], experts, capacity, stride)
    scaled, inverse, normed = layer_stats(middle_rows, ln_gains[1], ln_biases[1])
    logits = jnp.dot(normed, router, precision=highest)
    gate_values = gates_of(logits, routes)
    position = jnp.arange(experts * stride, dtype=jnp.int32)[:, None]
    pick_first = (slot_flat[:, 0][None, :] == position).astype(jnp.float32)
    pick_second = (slot_flat[:, 1][None, :] == position).astype(jnp.float32)
    placing = (pick_first + pick_second).astype(jnp.bfloat16)
    lean_first, lean_second = (pick_first.astype(jnp.bfloat16), pick_second.astype(jnp.bfloat16))
    gated = jnp.concatenate(
        [
            (gate_values[:, 0:1] * cot_float).astype(jnp.bfloat16),
            (gate_values[:, 1:2] * cot_float).astype(jnp.bfloat16),
        ],
        axis=0,
    )
    dispatch = jnp.dot(
        placing, normed.astype(jnp.bfloat16), preferred_element_type=jnp.float32
    ).astype(jnp.bfloat16)
    sent_grad = jnp.dot(
        jnp.concatenate([lean_first, lean_second], axis=1),
        gated,
        preferred_element_type=jnp.float32,
    ).astype(jnp.bfloat16)

    slot_rows = slots_all + -slots_all % 16
    packed = jnp.arange(slot_rows, dtype=jnp.int32)[:, None]
    packing = (
        (position[:, 0][None, :] == packed // capacity * stride + packed % capacity)
        & (packed < slots_all)
    ).astype(jnp.bfloat16)
    returned, every_rows, every_hidden = run_experts(
        jnp.concatenate([dispatch, sent_grad], axis=1).reshape(experts, stride, 2 * model_width),
        packing,
        first_weight,
        second_weight,
    )
    returned = returned.reshape(experts * stride, 2 * model_width)
    back_first = lax.dot_general(
        lean_first, returned, contract_first, preferred_element_type=jnp.float32
    )
    back_second = lax.dot_general(
        lean_second, returned, contract_first, preferred_element_type=jnp.float32
    )
    picked_first, picked_second = (back_first[:, :model_width], back_second[:, :model_width])
    block_out = middle_rows + (
        gate_values[:, 0:1] * picked_first + gate_values[:, 1:2] * picked_second
    )
    grad_gap = jnp.sum(picked_first * cot_float, axis=1) - jnp.sum(picked_second * cot_float, axis=1)
    logit_step = gate_values[:, 0] * gate_values[:, 1] * grad_gap
    columns = jnp.arange(experts, dtype=jnp.int32)[None, :]
    logit_grad = (
        (routes[:, 0:1] == columns).astype(jnp.float32)
        - (routes[:, 1:2] == columns).astype(jnp.float32)
    ) * logit_step[:, None]
    gathered = back_first[:, model_width:] + back_second[:, model_width:]
    normed_grad = gathered + lax.dot_general(
        logit_grad, router, contract_last, precision=highest
    )
    router_local = lax.dot_general(normed, logit_grad, contract_first, precision=highest)
    middle_grad = input_grad(cot_float, normed_grad, scaled, inverse, ln_gains[1])
    middle_rounded = middle_grad.astype(jnp.bfloat16)
    mixed_grad = lax.dot_general(
        middle_rounded, full_out, contract_last, preferred_element_type=jnp.float32
    ).astype(jnp.bfloat16)
    scores_again = attention_scores(query_rows, key_rows, score_scale)
    probs_again = jnp.exp(scores_again - log_total).astype(jnp.bfloat16)
    grad_heads = mixed_grad.reshape(image_count, SEQ, HEADS, head_width)
    value_grad = jnp.einsum(
        "ihst,ishd->ithd", probs_again, grad_heads, preferred_element_type=jnp.float32
    )
    prob_grad = jnp.einsum(
        "ishd,ithd->ihst", grad_heads, value_rows, preferred_element_type=jnp.float32
    )
    prob_float = probs_again.astype(jnp.float32)
    row_delta = jnp.sum(prob_float * prob_grad, axis=3, keepdims=True)
    score_grad = (prob_float * (prob_grad - row_delta) * score_scale).astype(jnp.bfloat16)
    query_grad = jnp.einsum(
        "ihst,ithd->ishd", score_grad, key_rows, preferred_element_type=jnp.float32
    )
    key_grad = jnp.einsum(
        "ihst,ishd->ithd", score_grad, query_rows, preferred_element_type=jnp.float32
    )
    qkv_grad = (
        jnp.stack([query_grad, key_grad, value_grad], axis=2)
        .astype(jnp.bfloat16)
        .reshape(token_count, 3 * model_width)
    )
    attn_in_grad = lax.dot_general(
        qkv_grad, full_qkv, contract_last, preferred_element_type=jnp.float32
    )
    grad_tokens = input_grad(middle_grad, attn_in_grad, scaled_one, inverse_one, ln_gains[0])
    qkv_term = lax.dot_general(
        attn_in, qkv_grad, contract_first, preferred_element_type=jnp.float32
    )
    out_term = lax.dot_general(
        mixed_rows, middle_rounded, contract_first, preferred_element_type=jnp.float32
    )
    norm_local = jnp.stack(
        [
            jnp.sum(attn_in_grad * scaled_one, axis=0),
            jnp.sum(normed_grad * scaled, axis=0),
            jnp.sum(attn_in_grad, axis=0),
            jnp.sum(normed_grad, axis=0),
        ]
    )
    small = jnp.concatenate([router_local.T, norm_local], axis=0)
    small_rows = experts + 4
    (
        grad_qkv,
        grad_out,
        moment_qkv,
        moment_out,
        small_total,
        iter_qkv,
        iter_out,
        expert_grads,
        iter_expert,
        iter_router,
    ) = reduce_attention(
        qkv_term.astype(jnp.bfloat16).reshape(members, -1, 3 * model_width),
        out_term.astype(jnp.bfloat16).reshape(members, -1, model_width),
        qkv_momentum,
        out_momentum,
        jnp.pad(small, ((0, -small_rows % 8), (0, 0))),
        every_rows,
        every_hidden,
        every_moment,
        router_momentum.T,
    )
    grad_router = small_total[:experts].T
    grad_norm = small_total[experts:small_rows]
    row_base = dp_index * dp_share
    grad_first, grad_second = (expert_grads[0], expert_grads[1])
    moment_first = decay_rate * w_in_momentum[0] + grad_first
    moment_second = decay_rate * w_out_momentum[0] + grad_second
    iter_first, iter_second = (iter_expert[0], iter_expert[1])
    expert_share = qkv_weight.shape[0]
    if iter_out.shape[0] != expert_share:
        expert_base = lax.axis_index("expert") * expert_share
        iter_out = lax.dynamic_slice_in_dim(iter_out, expert_base, expert_share, 0)
        iter_qkv = lax.dynamic_slice_in_dim(iter_qkv, expert_base, expert_share, 0)
    new_norm_momentum = decay_rate * norm_momentum + grad_norm
    new_norm = jnp.concatenate([ln_gains, ln_biases], axis=0) - norm_rate * new_norm_momentum
    new_router_momentum = decay_rate * router_momentum + grad_router
    new_router = router - matrix_rate * iter_router.T

    rows_first = lax.dynamic_slice_in_dim(first_weight, row_base, dp_share, 0).astype(jnp.float32)
    rows_second = lax.dynamic_slice_in_dim(second_weight, row_base, dp_share, 0).astype(jnp.float32)
    widen_factor = math.sqrt(max(1.0, hidden_units / model_width))
    new_first = rows_first - matrix_rate * widen_factor * iter_first.astype(jnp.float32)
    new_second = rows_second - matrix_rate * iter_second.astype(jnp.float32)
    new_qkv = qkv_weight.astype(jnp.float32) - matrix_rate * math.sqrt(3.0) * iter_qkv.astype(
        jnp.float32
    )
    new_out = out_weight.astype(jnp.float32) - matrix_rate * iter_out.astype(jnp.float32)
    return (
        block_out,
        grad_tokens,
        grad_norm,
        grad_router,
        grad_qkv,
        grad_out,
        grad_first[None],
        grad_second[None],
        new_norm,
        new_norm_momentum,
        new_router,
        new_router_momentum,
        new_qkv,
        moment_qkv,
        new_out,
        moment_out,
        new_first[None],
        moment_first[None],
        new_second[None],
        moment_second[None],
    )


def solution(mesh):
    in_specs = (
        P(("dp", "expert"), None),
        P(("dp", "expert"), None),
        P(("dp", "expert"), None),
        P(("dp", "expert"), None),
        P(),
        P(),
        P("expert", None),
        P("expert", None),
        P(),
        P("expert", None, None),
        P("expert", None, None),
        P(),
        P(),
        P("expert", None),
        P("expert", None),
        P("expert", "dp", None),
        P("expert", "dp", None),
    )
    out_specs = (
        P(("dp", "expert"), None),
        P(("dp", "expert"), None),
        P(),
        P(),
        P("expert", None),
        P("expert", None),
        P("expert", "dp", None),
        P("expert", "dp", None),
        P(),
        P(),
        P(),
        P(),
        P("expert", None),
        P("expert", None),
        P("expert", None),
        P("expert", None),
        P("expert", "dp", None),
        P("expert", "dp", None),
        P("expert", "dp", None),
        P("expert", "dp", None),
    )
    return jax.shard_map(body, mesh=mesh, in_specs=in_specs, out_specs=out_specs, check_vma=False)
```

```python
import functools
import math

import jax
import jax.numpy as jnp
from jax import lax
from jax.experimental import pallas as pl
from jax.experimental.pallas import tpu as pltpu
from jax.sharding import PartitionSpec as P

HEADS = 12
NS_STEPS = 5
SEQ = 197


quintic_one = 3.4445
quintic_two = -4.775
quintic_three = 2.0315
decay_rate = 0.9
matrix_rate = 0.2
norm_rate = 0.004
norm_eps = 1e-06
frob_eps = 1e-07
highest = lax.Precision.HIGHEST
contract_last = (((1,), (1,)), ((), ()))
contract_first = (((0,), (0,)), ((), ()))


def gelu_slope(preact):
    return (
        0.5 * (1.0 + lax.erf(preact * 0.7071067811865476))
        + preact * jnp.exp(-0.5 * preact * preact) * 0.3989422804014327
    )


def layer_stats(token_rows, gain, bias):
    centre = token_rows - jnp.mean(token_rows, axis=-1, keepdims=True)
    inverse = lax.rsqrt(jnp.mean(centre * centre, axis=-1, keepdims=True) + norm_eps)
    scaled = centre * inverse
    return (scaled, inverse, scaled * gain + bias)


def slot_index(choice_ids, order_rows, experts, capacity, stride):
    token_count = choice_ids.shape[0]
    ranks = jnp.arange(token_count, dtype=jnp.int32)
    turn = jnp.sum(
        jnp.where(order_rows[:, None] == ranks[None, :], ranks[:, None], 0), axis=0, dtype=jnp.int32
    )
    earlier = (turn[None, :] < turn[:, None]).astype(jnp.bfloat16)
    columns = jnp.arange(experts, dtype=jnp.int32)[None, :]
    first = (choice_ids[:, 0:1] == columns).astype(jnp.bfloat16)
    second = (choice_ids[:, 1:2] == columns).astype(jnp.bfloat16)
    counts = jnp.dot(
        earlier, jnp.concatenate([first, second], axis=1), preferred_element_type=jnp.float32
    )
    first_float, second_float = first.astype(jnp.float32), second.astype(jnp.float32)
    first_slot = jnp.sum(counts[:, :experts] * first_float, axis=1)
    second_slot = jnp.sum(
        (counts[:, experts:] + jnp.sum(first_float, axis=0, keepdims=True)) * second_float, axis=1
    )
    slot_values = jnp.stack([first_slot, second_slot], axis=1).astype(jnp.int32)
    return jnp.where(
        slot_values < capacity, choice_ids * stride + slot_values, experts * stride
    )


def gates_of(logits, choice_ids):
    columns = jnp.arange(logits.shape[1], dtype=jnp.int32)[None, :]
    first_logit = jnp.sum(jnp.where(choice_ids[:, 0:1] == columns, logits, 0.0), axis=1)
    second_logit = jnp.sum(jnp.where(choice_ids[:, 1:2] == columns, logits, 0.0), axis=1)
    first_gate = jax.nn.sigmoid(first_logit - second_logit)
    return jnp.stack([first_gate, 1.0 - first_gate], axis=1)


def input_grad(base_grad, normed_grad, scaled, inverse, gain):
    lifted = normed_grad * gain
    centred = (
        lifted
        - jnp.mean(lifted, axis=-1, keepdims=True)
        - scaled * jnp.mean(lifted * scaled, axis=-1, keepdims=True)
    )
    return base_grad + inverse * centred


def ortho_steps(read, block, tile, iterate, gram, mixer):
    rows, cols = iterate.shape
    tiles = cols // tile

    def begin():
        def squares(index, total):
            part = read(pl.ds(pl.multiple_of(index * tile, tile), tile))
            return total + jnp.sum(part * part, axis=0, keepdims=True)

        total = lax.fori_loop(0, tiles, squares, jnp.zeros((1, tile), jnp.float32))
        norm = jnp.sqrt(jnp.sum(total)) + frob_eps

        @pl.loop(0, tiles)
        def _(index):
            span = pl.ds(pl.multiple_of(index * tile, tile), tile)
            iterate[:, span] = (read(span) / norm).astype(jnp.bfloat16)

    def mirror(target, part, index):
        target[index * block : (index + 1) * block, 0 : (index + 1) * block] = part
        for other in range(index):
            target[other * block : (other + 1) * block, index * block : (index + 1) * block] = part[
                :, other * block : (other + 1) * block
            ].T

    def make_gram():
        for index in range(rows // block):
            mirror(
                gram,
                lax.dot_general(
                    iterate[index * block : (index + 1) * block, :],
                    iterate[0 : (index + 1) * block, :],
                    contract_last,
                    preferred_element_type=jnp.float32,
                ).astype(jnp.bfloat16),
                index,
            )

    def mix(gram_rows, gram_part, gram_columns):
        return (
            quintic_two * gram_part.astype(jnp.float32)
            + quintic_three * jnp.dot(gram_rows, gram_columns, preferred_element_type=jnp.float32)
        ).astype(jnp.bfloat16)

    def apply(mixer_rows, part, columns):
        return (
            quintic_one * part.astype(jnp.float32)
            + jnp.dot(mixer_rows, columns, preferred_element_type=jnp.float32)
        ).astype(jnp.bfloat16)

    def make_mixer():
        for index in range(rows // block):
            span = pl.ds(index * block, block)
            reach = (index + 1) * block
            mirror(mixer, mix(gram[span, :], gram[span, 0:reach], gram[:, 0:reach]), index)

    def advance():
        @pl.loop(0, tiles)
        def _(index):
            span = pl.ds(pl.multiple_of(index * tile, tile), tile)
            columns = iterate[:, span]
            iterate[:, span] = apply(mixer[...], columns, columns)

    def last_rows(own, row_count, out_ref):
        mixer[0:row_count, :] = mix(gram[own, :], gram[own, :], gram[...])

        @pl.loop(0, tiles)
        def _(index):
            span = pl.ds(pl.multiple_of(index * tile, tile), tile)
            out_ref[:, span] = apply(mixer[0:row_count, :], iterate[own, span], iterate[:, span])

    return begin, make_gram, make_mixer, advance, last_rows


def tile_sizes(rows, cols):
    block = next(size for size in (256, 128, rows) if rows % size == 0)
    tile = next(size for size in (1152, 768, 512, 256, 128, cols) if cols % size == 0)
    return block, tile


MESH = pl.DeviceIdType.MESH


def at_expert(index):
    return {"expert": index}


def at_dp(index):
    return {"dp": index}


def remote(source, target, send_sem, recv_sem, device):
    return pltpu.make_async_remote_copy(
        src_ref=source,
        dst_ref=target,
        send_sem=send_sem,
        recv_sem=recv_sem,
        device_id=device,
        device_id_type=MESH,
    )


def greet(devices):
    barrier = pltpu.get_barrier_semaphore()
    for device in devices:
        pl.semaphore_signal(barrier, inc=1, device_id=device, device_id_type=MESH)
    pl.semaphore_wait(barrier, len(devices))


def neighbours(chips, planes):
    me = lax.axis_index("expert")
    core, chip = lax.rem(me, 2), lax.div(me, 2)
    plane = lax.axis_index("dp")
    ahead = [2 * lax.rem(chip + shift, chips) + core for shift in range(1, chips)]
    behind = [2 * lax.rem(chip + chips - shift, chips) + core for shift in range(1, chips)]
    above = [lax.rem(plane + shift, planes) for shift in range(1, planes)]
    return me, core, chip, plane, me + 1 - 2 * core, ahead, behind, above


def spread_start(piece, me, partner, ahead, sems, lane):
    copies = [remote(piece(me), piece(me), sems.at[0, lane, 0], sems.at[1, lane, 0], at_expert(partner))]
    for shift, peer in enumerate(ahead, 1):
        copies.append(
            remote(piece(me), piece(me), sems.at[0, lane, shift], sems.at[1, lane, shift], at_expert(peer))
        )
    for copy in copies:
        copy.start()
    return copies


def spread_relay(piece, copies, partner, behind, sems, lane):
    relays = []
    for shift, source in enumerate(behind, 1):
        copies[shift].wait_recv()
        relay = remote(
            piece(source), piece(source), sems.at[2, lane, shift], sems.at[3, lane, shift], at_expert(partner)
        )
        relay.start()
        relays.append(relay)
    return relays


def spread_finish(copies, relays):
    copies[0].wait_recv()
    for relay in relays:
        relay.wait_recv()
    for copy in copies + relays:
        copy.wait_send()


def weights_kernel(
    chips, planes, qkv_ref, out_ref, moments_ref, qkv_all, out_all, moments_all, spread_sems, moment_sems, local_sems
):
    me, core, chip, plane, partner, ahead, behind, above = neighbours(chips, planes)
    greet([at_expert(i) for i in [partner] + ahead] + [at_dp(i) for i in above])
    own_copies = [
        pltpu.make_async_copy(qkv_ref, qkv_all.at[me], local_sems.at[0]),
        pltpu.make_async_copy(out_ref, out_all.at[me], local_sems.at[1]),
    ]
    lanes = []
    for lane, (source, target) in enumerate(((qkv_ref, qkv_all), (out_ref, out_all))):
        copies = [
            remote(
                source,
                target.at[me],
                spread_sems.at[0, lane, shift],
                spread_sems.at[1, lane, shift],
                at_expert(peer),
            )
            for shift, peer in enumerate([partner] + ahead)
        ]
        for copy in copies[1:] + copies[:1]:
            copy.start()
        lanes.append((lane, target, copies))
    keepers = (planes // 2 - 1, planes // 2)
    for which, keeper in enumerate(keepers):

        @pl.when(plane != keeper)
        def _():
            remote(
                moments_ref.at[which],
                moments_all.at[plane],
                moment_sems.at[0, which],
                moment_sems.at[1, plane],
                at_dp(keeper),
            ).start()

        @pl.when(plane == keeper)
        def _():
            pltpu.make_async_copy(
                moments_ref.at[which], moments_all.at[plane], local_sems.at[2]
            ).start()

    for copy in own_copies:
        copy.start()
    relayed = [
        (copies, spread_relay(lambda i: target.at[i], copies, partner, behind, spread_sems, lane))
        for lane, target, copies in lanes
    ]
    for copies, relays in relayed:
        spread_finish(copies, relays)
    for copy in own_copies:
        copy.wait()
    for which, keeper in enumerate(keepers):

        @pl.when(plane != keeper)
        def _():
            remote(
                moments_ref.at[which],
                moments_all.at[plane],
                moment_sems.at[0, which],
                moment_sems.at[1, plane],
                at_dp(keeper),
            ).wait_send()

        @pl.when(plane == keeper)
        def _():
            pltpu.make_async_copy(
                moments_ref.at[which], moments_all.at[plane], local_sems.at[2]
            ).wait()
            for source in range(planes):
                if source != keeper:
                    remote(
                        moments_ref.at[which],
                        moments_all.at[source],
                        moment_sems.at[0, which],
                        moment_sems.at[1, source],
                        at_dp(source),
                    ).wait_recv()


def gather_weights(qkv_weight, out_weight, moments):
    members, planes = lax.axis_size("expert"), lax.axis_size("dp")
    chips = members // 2
    anywhere = pl.BlockSpec(memory_space=pl.ANY)
    return pl.pallas_call(
        functools.partial(weights_kernel, chips, planes),
        out_shape=(
            jax.ShapeDtypeStruct((members,) + qkv_weight.shape, jnp.bfloat16),
            jax.ShapeDtypeStruct((members,) + out_weight.shape, jnp.bfloat16),
            jax.ShapeDtypeStruct((planes,) + moments.shape[1:], jnp.bfloat16),
        ),
        in_specs=[anywhere] * 3,
        out_specs=[anywhere] * 3,
        scratch_shapes=[
            pltpu.SemaphoreType.DMA((4, 2, chips)),
            pltpu.SemaphoreType.DMA((2, max(2, planes))),
            pltpu.SemaphoreType.DMA((3,)),
        ],
        compiler_params=pltpu.CompilerParams(collective_id=1, has_side_effects=True),
    )(qkv_weight, out_weight, moments)


def expert_kernel(
    members,
    planes,
    blocks_ref,
    packing_ref,
    first_weight,
    second_weight,
    back_ref,
    rows_all,
    hidden,
    arrived,
    leaving,
    outcome,
    go_sems,
    back_sems,
    rows_sems,
):
    me, plane = lax.axis_index("expert"), lax.axis_index("dp")
    others = [lax.rem(me + shift, members) for shift in range(1, members)]
    above = [lax.rem(plane + shift, planes) for shift in range(1, planes)]
    greet([at_expert(i) for i in others] + [at_dp(i) for i in above])

    def exchange(source, target, sems):
        copies = [
            remote(source.at[peer], target.at[me], sems.at[0, i], sems.at[1, i], at_expert(peer))
            for i, peer in enumerate(others)
        ]
        for copy in copies:
            copy.start()
        target[me] = source[me]
        return copies

    depth, units = first_weight.shape
    stride = blocks_ref.shape[1]
    gone = exchange(blocks_ref, arrived, go_sems)
    for copy in gone:
        copy.wait_recv()
    rows_all[plane] = jnp.dot(
        packing_ref[...],
        arrived[...].reshape(members * stride, 2 * depth),
        preferred_element_type=jnp.float32,
    ).astype(jnp.bfloat16)
    last = planes - 1

    def hop(way, number, block):
        return remote(
            rows_all.at[block],
            rows_all.at[block],
            rows_sems.at[0, way, number],
            rows_sems.at[1, way, number],
            at_dp(lax.rem(plane + planes + 1 - 2 * way, planes)),
        )

    def can_send(way, number):
        if way == 0:
            return (plane < last) & (plane >= number)
        return (plane > 0) & (plane + number <= last)

    def block_of(way, number):
        return plane - number if way == 0 else plane + number

    for way in range(2):

        @pl.when(can_send(way, 0))
        def _():
            hop(way, 0, plane).start()

    block = tile_sizes(depth, units)[0]

    def hidden_rows(source):
        @pl.loop(0, units // block)
        def _(index):
            span = pl.ds(pl.multiple_of(index * block, block), block)
            preact = jnp.dot(
                rows_all[source, :, 0:depth], first_weight[:, span], preferred_element_type=jnp.float32
            )
            act_grad = jnp.dot(
                rows_all[source, :, depth : 2 * depth],
                second_weight[:, span],
                preferred_element_type=jnp.float32,
            )
            share = 0.5 * (1.0 + lax.erf(preact * 0.7071067811865476))
            slope = share + preact * jnp.exp(-0.5 * preact * preact) * 0.3989422804014327
            hidden[0, source, :, span] = (act_grad * slope).astype(jnp.bfloat16)
            hidden[1, source, :, span] = (preact * share).astype(jnp.bfloat16)

    hidden_rows(plane)
    for part, weight in enumerate((second_weight, first_weight)):
        for start in range(0, depth, block):
            outcome[:, part * depth + start : part * depth + start + block] = lax.dot_general(
                hidden[1 - part, plane],
                weight[start : start + block, :],
                contract_last,
                preferred_element_type=jnp.float32,
            ).astype(jnp.bfloat16)
    leaving[...] = (
        lax.dot_general(
            packing_ref[...], outcome[...], contract_first, preferred_element_type=jnp.float32
        )
        .astype(jnp.bfloat16)
        .reshape(members, stride, 2 * depth)
    )
    returned = exchange(leaving, back_ref, back_sems)
    for number in range(1, planes):
        arrives = (plane >= number, plane + number <= last)
        for way in range(2):

            @pl.when(arrives[way])
            def _():
                source = block_of(way, number)
                hop(way, number - 1, source).wait_recv()

            if number < last:

                @pl.when(can_send(way, number))
                def _():
                    hop(way, number, block_of(way, number)).start()

        for way in range(2):

            @pl.when(arrives[way])
            def _():
                hidden_rows(block_of(way, number))

    for copy in returned:
        copy.wait_recv()
    for copy in gone + returned:
        copy.wait_send()
    for number in range(last):
        for way in range(2):

            @pl.when(can_send(way, number))
            def _():
                hop(way, number, block_of(way, number)).wait_send()


def run_experts(blocks, packing, first_weight, second_weight):
    members, planes = lax.axis_size("expert"), lax.axis_size("dp")
    slots = packing.shape[0]
    depth, units = first_weight.shape
    local = pl.BlockSpec(memory_space=pltpu.VMEM)
    dma = pltpu.SemaphoreType.DMA
    wide = jnp.bfloat16
    return pl.pallas_call(
        functools.partial(expert_kernel, members, planes),
        out_shape=(
            jax.ShapeDtypeStruct(blocks.shape, wide),
            jax.ShapeDtypeStruct((planes, slots, 2 * depth), wide),
            jax.ShapeDtypeStruct((2, planes, slots, units), wide),
        ),
        in_specs=[local] * 4,
        out_specs=[local] * 3,
        scratch_shapes=[
            pltpu.VMEM(blocks.shape, wide),
            pltpu.VMEM(blocks.shape, wide),
            pltpu.VMEM((slots, 2 * depth), wide),
            dma((2, members - 1)),
            dma((2, members - 1)),
            dma((2, 2, planes - 1)),
        ],
        compiler_params=pltpu.CompilerParams(
            collective_id=3, has_side_effects=True, vmem_limit_bytes=48 << 20
        ),
    )(blocks, packing, first_weight, second_weight)


def attention_kernel(
    chips,
    planes,
    split,
    qkv_term,
    out_term,
    qkv_moment,
    out_moment,
    small_ref,
    rows_all,
    hidden,
    expert_moment,
    router_moment,
    grad_qkv,
    grad_out,
    new_qkv_moment,
    new_out_moment,
    small_out,
    iter_qkv,
    iter_out,
    expert_grads,
    iter_expert,
    iter_router,
    qkv_all,
    out_all,
    iterate,
    wide_iterate,
    expert_total,
    gram,
    mixer,
    crossed,
    leaving,
    landed,
    plane_out,
    plane_in,
    plane_all,
    small_pair,
    small_chip,
    small_plane,
    cross_sems,
    chip_sems,
    plane_sems,
    share_sems,
    spread_sems,
    small_sems,
    iter_sems,
    local_sems,
):
    width = out_term.shape[2]
    lanes = qkv_term.shape[2] // width + 1
    me, core, chip, plane, partner, ahead, behind, above = neighbours(chips, planes)
    greet([at_expert(i) for i in [partner] + ahead] + [at_dp(i) for i in above])

    def cut(pair, lane):
        if lane == lanes - 1:
            return pair[1], pl.ds(0, width)
        return pair[0], pl.ds(lane * width, width)

    def term(lane, index):
        ref, columns = cut((qkv_term, out_term), lane)
        return ref[index, :, columns].astype(jnp.float32)

    order = [lanes - 1] + list(range(lanes - 1))
    crosses = {}
    for lane in order:
        for shift in range(chips):
            target = lax.rem(chip + shift, chips)
            ref, columns = cut((qkv_term, out_term), lane)
            crosses[lane, shift] = remote(
                ref.at[2 * target + 1 - core, :, columns],
                crossed.at[lane, target],
                cross_sems.at[0, lane, shift],
                cross_sems.at[1, lane, shift],
                at_expert(partner),
            )
        for shift in list(range(1, chips)) + [0]:
            crosses[lane, shift].start()
    small_copy = remote(small_ref, small_pair, small_sems.at[0, 0], small_sems.at[1, 0], at_expert(partner))
    small_copy.start()
    sends = list(crosses.values()) + [small_copy]
    moment_copy = pltpu.make_async_copy(expert_moment, iterate, local_sems.at[0])
    moment_copy.start()

    chip_copies = {}

    def to_chips(lane):
        for shift in range(1, chips):
            target = lax.rem(chip + shift, chips)
            crosses[lane, shift].wait_recv()
            leaving[lane, shift - 1] = (
                term(lane, 2 * target + core) + crossed[lane, target].astype(jnp.float32)
            ).astype(jnp.bfloat16)
            copy = remote(
                leaving.at[lane, shift - 1],
                landed.at[lane, shift - 1],
                chip_sems.at[0, lane, shift - 1],
                chip_sems.at[1, lane, shift - 1],
                at_expert(ahead[shift - 1]),
            )
            copy.start()
            chip_copies[lane, shift] = copy
            sends.append(copy)

    small_chip_copies = []

    def small_to_chips():
        small_copy.wait_recv()
        small_chip[chip] = small_ref[...] + small_pair[...]
        for shift, peer in enumerate(ahead, 1):
            copy = remote(
                small_chip.at[chip],
                small_chip.at[chip],
                small_sems.at[0, shift],
                small_sems.at[1, shift],
                at_expert(peer),
            )
            copy.start()
            small_chip_copies.append(copy)
            sends.append(copy)

    small_plane_copies = []

    def small_to_planes():
        for copy in small_chip_copies:
            copy.wait_recv()
        small_plane[plane] = sum(small_chip[i] for i in range(chips))
        for i, peer in enumerate(above):
            copy = remote(
                small_plane.at[plane],
                small_plane.at[plane],
                small_sems.at[0, chips + i],
                small_sems.at[1, chips + i],
                at_dp(peer),
            )
            copy.start()
            small_plane_copies.append(copy)
            sends.append(copy)

    def small_finish():
        for copy in small_plane_copies:
            copy.wait_recv()
        small_out[...] = sum(small_plane[i] for i in range(planes))
        count = router_moment.shape[0]
        fresh = decay_rate * router_moment[...] + small_out[0:count, :]
        norm = jnp.sqrt(jnp.sum(fresh * fresh)) + frob_eps

        def rounded(values):
            return values.astype(jnp.bfloat16).astype(jnp.float32)

        turned = rounded(fresh / norm)
        for _ in range(NS_STEPS):
            product = rounded(
                lax.dot_general(turned, turned, contract_last, preferred_element_type=jnp.float32)
            )
            blend = rounded(
                quintic_two * product
                + quintic_three * jnp.dot(product, product, preferred_element_type=jnp.float32)
            )
            turned = rounded(
                quintic_one * turned + jnp.dot(blend, turned, preferred_element_type=jnp.float32)
            )
        iter_router[...] = turned

    part = plane_out.shape[2]
    plane_copies = {}

    def to_planes(lane):
        crosses[lane, 0].wait_recv()
        total = term(lane, me) + crossed[lane, chip].astype(jnp.float32)
        for shift in range(1, chips):
            chip_copies[lane, shift].wait_recv()
            total = total + landed[lane, shift - 1].astype(jnp.float32)
        if split:
            for i in range(planes):
                plane_out[lane, i] = total[i * part : (i + 1) * part].astype(jnp.bfloat16)
        else:
            plane_in[lane, plane] = total.astype(jnp.bfloat16)
        plane_copies[lane] = []
        for i, peer in enumerate(above):
            copy = remote(
                plane_out.at[lane, peer] if split else plane_in.at[lane, plane],
                plane_in.at[lane, plane],
                plane_sems.at[0, lane, i],
                plane_sems.at[1, lane, i],
                at_dp(peer),
            )
            copy.start()
            plane_copies[lane].append(copy)
            sends.append(copy)

    share_copies = {}

    def share_planes(lane):
        share_copies[lane] = []
        if not split:
            return
        for copy in plane_copies[lane]:
            copy.wait_recv()
        plane_in[lane, plane] = plane_out[lane, plane]
        total = plane_in[lane, 0].astype(jnp.float32)
        for i in range(1, planes):
            total = total + plane_in[lane, i].astype(jnp.float32)
        plane_all[lane, plane] = total.astype(jnp.bfloat16)
        for i, peer in enumerate(above):
            copy = remote(
                plane_all.at[lane, plane],
                plane_all.at[lane, plane],
                share_sems.at[0, lane, i],
                share_sems.at[1, lane, i],
                at_dp(peer),
            )
            copy.start()
            share_copies[lane].append(copy)
            sends.append(copy)

    def piece_of(lane):
        ref, columns = cut((qkv_all, out_all), lane)
        return lambda index: ref.at[index, :, columns]

    spreads, relays = {}, {}

    def make_moment(lane):
        moment, columns = cut((qkv_moment, out_moment), lane)
        grad_target, _ = cut((grad_qkv, grad_out), lane)
        moment_target, _ = cut((new_qkv_moment, new_out_moment), lane)
        whole, _ = cut((qkv_all, out_all), lane)
        if split:
            for copy in share_copies[lane]:
                copy.wait_recv()
            grad = jnp.concatenate(
                [plane_all[lane, i].astype(jnp.float32) for i in range(planes)], axis=0
            )
        else:
            for copy in plane_copies[lane]:
                copy.wait_recv()
            grad = sum(plane_in[lane, i].astype(jnp.float32) for i in range(planes))
        fresh = decay_rate * moment[:, columns] + grad
        grad_target[:, columns] = grad
        moment_target[:, columns] = fresh
        whole[me, :, columns] = fresh.astype(jnp.bfloat16)
        spreads[lane] = spread_start(piece_of(lane), me, partner, ahead, spread_sems, lane)

    def relay(lane):
        relays[lane] = spread_relay(piece_of(lane), spreads[lane], partner, behind, spread_sems, lane)

    depth, units = iterate.shape
    block, tile = tile_sizes(depth, units)
    which = jnp.where(plane == planes // 2 - 1, 0, 1)
    slots = planes * rows_all.shape[1]

    def expert_grad(matrix):
        @pl.loop(0, depth // block)
        def _(index):
            columns = pl.ds(pl.multiple_of(matrix * depth + index * block, block), block)
            left = rows_all[:, :, columns].reshape(slots, block)
            target = pl.ds(pl.multiple_of(index * block, block), block)
            for start in range(0, units, tile):
                expert_total[target, start : start + tile] = lax.dot_general(
                    left,
                    hidden[matrix, :, :, start : start + tile].reshape(slots, tile),
                    contract_first,
                    preferred_element_type=jnp.float32,
                )

        share = expert_grads.shape[1]
        own = pl.ds(pl.multiple_of(plane * share, share), share)
        expert_grads[matrix] = expert_total[own, :]

    def add_moment():
        moment_copy.wait()

        @pl.loop(0, units // tile)
        def _(index):
            span = pl.ds(pl.multiple_of(index * tile, tile), tile)
            expert_total[:, span] = (
                decay_rate * iterate[:, span].astype(jnp.float32) + expert_total[:, span]
            )

    begin, make_gram, make_mixer, advance, last_rows = ortho_steps(
        lambda span: expert_total[:, span], block, tile, iterate, gram, mixer
    )

    def ortho_step():
        make_gram()
        make_mixer()
        advance()

    def begin_ortho():
        add_moment()
        begin()

    work = [functools.partial(expert_grad, 1 - which), functools.partial(expert_grad, which)]
    work += [begin_ortho] + [ortho_step] * NS_STEPS

    expert_share = expert_grads.shape[1]
    keepers = (planes // 2 - 1, planes // 2)

    def iter_copy(keeper, matrix, shift, peer):
        own = pl.ds(pl.multiple_of(peer * expert_share, expert_share), expert_share)
        return remote(
            iterate.at[own, :],
            iter_expert.at[matrix],
            iter_sems.at[0, shift],
            iter_sems.at[1, matrix],
            at_dp(peer),
        )

    def send_iterates():
        for matrix, keeper in enumerate(keepers):

            @pl.when(plane == keeper)
            def _():
                for shift, peer in enumerate(above):
                    iter_copy(keeper, matrix, shift, peer).start()
                iter_expert[matrix] = iterate[keeper * expert_share : (keeper + 1) * expert_share, :]

    def await_iterates():
        for matrix, keeper in enumerate(keepers):

            @pl.when(plane == keeper)
            def _():
                for shift, peer in enumerate(above):
                    iter_copy(keeper, matrix, shift, peer).wait_send()

            @pl.when(plane != keeper)
            def _():
                iter_copy(keeper, matrix, 0, plane).wait_recv()

    def attention_ortho(whole, target):
        cols = whole.shape[2]
        chunk = tile_sizes(depth, cols)[1]
        start, build_gram, build_mixer, step_on, last = ortho_steps(
            lambda span: whole[:, :, span].astype(jnp.float32).reshape(depth, chunk),
            block,
            chunk,
            wide_iterate.at[:, 0:cols],
            gram,
            mixer,
        )
        kept = target.shape[0]

        def advance_once():
            build_gram()
            build_mixer()
            step_on()

        def complete():
            build_gram()
            if kept == depth:
                own = pl.ds(0, depth)
            else:
                own = pl.ds(pl.multiple_of(me * kept, kept), kept)
            last(own, kept, target)

        return start, advance_once, complete

    def begin_out():
        spread_finish(spreads[order[0]], relays[order[0]])
        out_start()

    out_start, out_advance, out_complete = attention_ortho(out_all, iter_out)
    early = work
    turns = {0: early[:3], 1: early[3:5], 2: early[5:7], 3: early[7:]}
    late = max(4, lanes)
    turns[late] = [begin_out, out_advance, out_advance]
    turns[late + 1] = [send_iterates, out_advance, out_advance]
    turns[late + 2] = [out_complete]

    for lane in order:
        to_chips(lane)
        if lane == order[0]:
            small_to_chips()
    stages = [to_planes, share_planes, make_moment, relay]
    for step in range(lanes + len(stages) - 1):
        for number in range(len(stages) - 1, -1, -1):
            if 0 <= step - number < lanes:
                stages[number](order[step - number])
        if step == 0:
            small_to_planes()
        for turn in turns.pop(step, []):
            turn()
        if step == lanes - 1:
            small_finish()
    for step in sorted(turns):
        for turn in turns[step]:
            turn()
    for lane in order[1:]:
        spread_finish(spreads[lane], relays[lane])
    qkv_start, qkv_advance, qkv_complete = attention_ortho(qkv_all, iter_qkv)
    qkv_start()

    @pl.loop(0, NS_STEPS - 1)
    def _(step):
        qkv_advance()

    qkv_complete()
    for copy in sends:
        copy.wait_send()
    await_iterates()


def reduce_attention(
    qkv_term,
    out_term,
    qkv_moment,
    out_moment,
    small,
    rows,
    hidden,
    expert_moment,
    router_moment,
):
    members, planes = lax.axis_size("expert"), lax.axis_size("dp")
    chips = members // 2
    share, width = out_moment.shape
    qkv_width = qkv_moment.shape[1]
    lanes = qkv_width // width + 1
    split = share % (8 * planes) == 0
    part = share // planes if split else share
    depth, units = expert_moment.shape
    kept = share if share % 16 == 0 else depth
    local = pl.BlockSpec(memory_space=pltpu.VMEM)
    dma = pltpu.SemaphoreType.DMA
    wide = jnp.bfloat16
    return pl.pallas_call(
        functools.partial(attention_kernel, chips, planes, split),
        out_shape=(
            jax.ShapeDtypeStruct(qkv_moment.shape, jnp.float32),
            jax.ShapeDtypeStruct(out_moment.shape, jnp.float32),
            jax.ShapeDtypeStruct(qkv_moment.shape, jnp.float32),
            jax.ShapeDtypeStruct(out_moment.shape, jnp.float32),
            jax.ShapeDtypeStruct(small.shape, jnp.float32),
            jax.ShapeDtypeStruct((kept, qkv_width), wide),
            jax.ShapeDtypeStruct((kept, width), wide),
            jax.ShapeDtypeStruct((2, depth // planes, units), jnp.float32),
            jax.ShapeDtypeStruct((2, depth // planes, units), wide),
            jax.ShapeDtypeStruct(router_moment.shape, jnp.float32),
        ),
        in_specs=[local] * 7 + [pl.BlockSpec(memory_space=pl.ANY), local],
        out_specs=[local] * 10,
        scratch_shapes=[
            pltpu.VMEM((members, share, qkv_width), wide),
            pltpu.VMEM((members, share, width), wide),
            pltpu.VMEM((depth, units), wide),
            pltpu.VMEM((depth, qkv_width), wide),
            pltpu.VMEM((depth, units), jnp.float32),
            pltpu.VMEM((depth, depth), wide),
            pltpu.VMEM((depth, depth), wide),
            pltpu.VMEM((lanes, chips, share, width), wide),
            pltpu.VMEM((lanes, chips - 1, share, width), wide),
            pltpu.VMEM((lanes, chips - 1, share, width), wide),
            pltpu.VMEM((lanes, planes, part, width) if split else (1, 1, part, width), wide),
            pltpu.VMEM((lanes, planes, part, width), wide),
            pltpu.VMEM((lanes, planes, part, width) if split else (1, 1, part, width), wide),
            pltpu.VMEM(small.shape, jnp.float32),
            pltpu.VMEM((chips,) + small.shape, jnp.float32),
            pltpu.VMEM((planes,) + small.shape, jnp.float32),
            dma((2, lanes, chips)),
            dma((2, lanes, chips - 1)),
            dma((2, lanes, planes - 1)),
            dma((2, lanes, planes - 1)),
            dma((4, lanes, chips)),
            dma((2, chips + planes - 1)),
            dma((2, max(2, planes - 1))),
            dma((1,)),
        ],
        compiler_params=pltpu.CompilerParams(
            collective_id=2, has_side_effects=True, vmem_limit_bytes=63 << 20
        ),
    )(
        qkv_term,
        out_term,
        qkv_moment,
        out_moment,
        small,
        rows,
        hidden,
        expert_moment,
        router_moment,
    )


def split_heads(qkv_rows, image_count, head_width):
    shaped = qkv_rows.reshape(image_count, SEQ, 3, HEADS, head_width)
    return (shaped[:, :, 0], shaped[:, :, 1], shaped[:, :, 2])


def attention_scores(query_rows, key_rows, score_scale):
    return (
        jnp.einsum("ishd,ithd->ihst", query_rows, key_rows, preferred_element_type=jnp.float32)
        * score_scale
    )


def body(
    tokens,
    cotangent,
    routes,
    priority,
    ln_gains,
    ln_biases,
    qkv_weight,
    out_weight,
    router,
    w_in,
    w_out,
    norm_momentum,
    router_momentum,
    qkv_momentum,
    out_momentum,
    w_in_momentum,
    w_out_momentum,
):
    token_count, model_width = tokens.shape
    experts = router.shape[1]
    hidden_units = w_in.shape[2]
    capacity = (token_count + experts - 1) // experts
    slots_all = experts * capacity
    dp_share = model_width // lax.axis_size("dp")
    image_count = token_count // SEQ
    head_width = model_width // HEADS
    score_scale = 1.0 / math.sqrt(head_width)
    first_weight = w_in[0]
    second_weight = w_out[0]
    cot_float = cotangent.astype(jnp.float32)
    dp_size = lax.axis_size("dp")
    dp_index = lax.axis_index("dp")
    members = lax.axis_size("expert")
    keep_first, keep_second = (dp_size // 2 - 1, dp_size // 2)
    full_qkv, full_out, every_moment = gather_weights(
        qkv_weight, out_weight, jnp.concatenate([w_in_momentum, w_out_momentum]).astype(jnp.bfloat16)
    )
    full_qkv = full_qkv.reshape(model_width, 3 * model_width)
    full_out = full_out.reshape(model_width, model_width)
    every_moment = every_moment.reshape(model_width, hidden_units)
    token_float = tokens.astype(jnp.float32)
    scaled_one, inverse_one, normed_one = layer_stats(token_float, ln_gains[0], ln_biases[0])
    attn_in = normed_one.astype(jnp.bfloat16)
    qkv_rows = jnp.dot(attn_in, full_qkv, preferred_element_type=jnp.float32).astype(jnp.bfloat16)
    query_rows, key_rows, value_rows = split_heads(qkv_rows, image_count, head_width)
    scores = attention_scores(query_rows, key_rows, score_scale)
    log_total = jnp.log(jnp.sum(jnp.exp(scores), axis=3, keepdims=True))
    attn_probs = jnp.exp(scores - log_total).astype(jnp.bfloat16)
    mixed_rows = (
        jnp.einsum("ihst,ithd->ishd", attn_probs, value_rows, preferred_element_type=jnp.float32)
        .astype(jnp.bfloat16)
        .reshape(token_count, model_width)
    )
    middle_rows = token_float + jnp.dot(mixed_rows, full_out, preferred_element_type=jnp.float32)
    stride = capacity + -capacity % 16
    slot_flat = slot_index(routes, priority[0], experts, capacity, stride)
    scaled, inverse, normed = layer_stats(middle_rows, ln_gains[1], ln_biases[1])
    logits = jnp.dot(normed, router, precision=highest)
    gate_values = gates_of(logits, routes)
    position = jnp.arange(experts * stride, dtype=jnp.int32)[:, None]
    pick_first = (slot_flat[:, 0][None, :] == position).astype(jnp.float32)
    pick_second = (slot_flat[:, 1][None, :] == position).astype(jnp.float32)
    placing = (pick_first + pick_second).astype(jnp.bfloat16)
    lean_first, lean_second = (pick_first.astype(jnp.bfloat16), pick_second.astype(jnp.bfloat16))
    gated = jnp.concatenate(
        [
            (gate_values[:, 0:1] * cot_float).astype(jnp.bfloat16),
            (gate_values[:, 1:2] * cot_float).astype(jnp.bfloat16),
        ],
        axis=0,
    )
    dispatch = jnp.dot(
        placing, normed.astype(jnp.bfloat16), preferred_element_type=jnp.float32
    ).astype(jnp.bfloat16)
    sent_grad = jnp.dot(
        jnp.concatenate([lean_first, lean_second], axis=1),
        gated,
        preferred_element_type=jnp.float32,
    ).astype(jnp.bfloat16)

    slot_rows = slots_all + -slots_all % 16
    packed = jnp.arange(slot_rows, dtype=jnp.int32)[:, None]
    packing = (
        (position[:, 0][None, :] == packed // capacity * stride + packed % capacity)
        & (packed < slots_all)
    ).astype(jnp.bfloat16)
    returned, every_rows, every_hidden = run_experts(
        jnp.concatenate([dispatch, sent_grad], axis=1).reshape(experts, stride, 2 * model_width),
        packing,
        first_weight,
        second_weight,
    )
    returned = returned.reshape(experts * stride, 2 * model_width)
    back_first = lax.dot_general(
        lean_first, returned, contract_first, preferred_element_type=jnp.float32
    )
    back_second = lax.dot_general(
        lean_second, returned, contract_first, preferred_element_type=jnp.float32
    )
    picked_first, picked_second = (back_first[:, :model_width], back_second[:, :model_width])
    block_out = middle_rows + (
        gate_values[:, 0:1] * picked_first + gate_values[:, 1:2] * picked_second
    )
    grad_gap = jnp.sum(picked_first * cot_float, axis=1) - jnp.sum(picked_second * cot_float, axis=1)
    logit_step = gate_values[:, 0] * gate_values[:, 1] * grad_gap
    columns = jnp.arange(experts, dtype=jnp.int32)[None, :]
    logit_grad = (
        (routes[:, 0:1] == columns).astype(jnp.float32)
        - (routes[:, 1:2] == columns).astype(jnp.float32)
    ) * logit_step[:, None]
    gathered = back_first[:, model_width:] + back_second[:, model_width:]
    normed_grad = gathered + lax.dot_general(
        logit_grad, router, contract_last, precision=highest
    )
    router_local = lax.dot_general(normed, logit_grad, contract_first, precision=highest)
    middle_grad = input_grad(cot_float, normed_grad, scaled, inverse, ln_gains[1])
    middle_rounded = middle_grad.astype(jnp.bfloat16)
    mixed_grad = lax.dot_general(
        middle_rounded, full_out, contract_last, preferred_element_type=jnp.float32
    ).astype(jnp.bfloat16)
    scores_again = attention_scores(query_rows, key_rows, score_scale)
    probs_again = jnp.exp(scores_again - log_total).astype(jnp.bfloat16)
    grad_heads = mixed_grad.reshape(image_count, SEQ, HEADS, head_width)
    value_grad = jnp.einsum(
        "ihst,ishd->ithd", probs_again, grad_heads, preferred_element_type=jnp.float32
    )
    prob_grad = jnp.einsum(
        "ishd,ithd->ihst", grad_heads, value_rows, preferred_element_type=jnp.float32
    )
    prob_float = probs_again.astype(jnp.float32)
    row_delta = jnp.sum(prob_float * prob_grad, axis=3, keepdims=True)
    score_grad = (prob_float * (prob_grad - row_delta) * score_scale).astype(jnp.bfloat16)
    query_grad = jnp.einsum(
        "ihst,ithd->ishd", score_grad, key_rows, preferred_element_type=jnp.float32
    )
    key_grad = jnp.einsum(
        "ihst,ishd->ithd", score_grad, query_rows, preferred_element_type=jnp.float32
    )
    qkv_grad = (
        jnp.stack([query_grad, key_grad, value_grad], axis=2)
        .astype(jnp.bfloat16)
        .reshape(token_count, 3 * model_width)
    )
    attn_in_grad = lax.dot_general(
        qkv_grad, full_qkv, contract_last, preferred_element_type=jnp.float32
    )
    grad_tokens = input_grad(middle_grad, attn_in_grad, scaled_one, inverse_one, ln_gains[0])
    qkv_term = lax.dot_general(
        attn_in, qkv_grad, contract_first, preferred_element_type=jnp.float32
    )
    out_term = lax.dot_general(
        mixed_rows, middle_rounded, contract_first, preferred_element_type=jnp.float32
    )
    norm_local = jnp.stack(
        [
            jnp.sum(attn_in_grad * scaled_one, axis=0),
            jnp.sum(normed_grad * scaled, axis=0),
            jnp.sum(attn_in_grad, axis=0),
            jnp.sum(normed_grad, axis=0),
        ]
    )
    small = jnp.concatenate([router_local.T, norm_local], axis=0)
    small_rows = experts + 4
    (
        grad_qkv,
        grad_out,
        moment_qkv,
        moment_out,
        small_total,
        iter_qkv,
        iter_out,
        expert_grads,
        iter_expert,
        iter_router,
    ) = reduce_attention(
        qkv_term.astype(jnp.bfloat16).reshape(members, -1, 3 * model_width),
        out_term.astype(jnp.bfloat16).reshape(members, -1, model_width),
        qkv_momentum,
        out_momentum,
        jnp.pad(small, ((0, -small_rows % 8), (0, 0))),
        every_rows,
        every_hidden,
        every_moment,
        router_momentum.T,
    )
    grad_router = small_total[:experts].T
    grad_norm = small_total[experts:small_rows]
    row_base = dp_index * dp_share
    grad_first, grad_second = (expert_grads[0], expert_grads[1])
    moment_first = decay_rate * w_in_momentum[0] + grad_first
    moment_second = decay_rate * w_out_momentum[0] + grad_second
    iter_first, iter_second = (iter_expert[0], iter_expert[1])
    expert_share = qkv_weight.shape[0]
    if iter_out.shape[0] != expert_share:
        expert_base = lax.axis_index("expert") * expert_share
        iter_out = lax.dynamic_slice_in_dim(iter_out, expert_base, expert_share, 0)
        iter_qkv = lax.dynamic_slice_in_dim(iter_qkv, expert_base, expert_share, 0)
    new_norm_momentum = decay_rate * norm_momentum + grad_norm
    new_norm = jnp.concatenate([ln_gains, ln_biases], axis=0) - norm_rate * new_norm_momentum
    new_router_momentum = decay_rate * router_momentum + grad_router
    new_router = router - matrix_rate * iter_router.T

    rows_first = lax.dynamic_slice_in_dim(first_weight, row_base, dp_share, 0).astype(jnp.float32)
    rows_second = lax.dynamic_slice_in_dim(second_weight, row_base, dp_share, 0).astype(jnp.float32)
    widen_factor = math.sqrt(max(1.0, hidden_units / model_width))
    new_first = rows_first - matrix_rate * widen_factor * iter_first.astype(jnp.float32)
    new_second = rows_second - matrix_rate * iter_second.astype(jnp.float32)
    new_qkv = qkv_weight.astype(jnp.float32) - matrix_rate * math.sqrt(3.0) * iter_qkv.astype(
        jnp.float32
    )
    new_out = out_weight.astype(jnp.float32) - matrix_rate * iter_out.astype(jnp.float32)
    return (
        block_out,
        grad_tokens,
        grad_norm,
        grad_router,
        grad_qkv,
        grad_out,
        grad_first[None],
        grad_second[None],
        new_norm,
        new_norm_momentum,
        new_router,
        new_router_momentum,
        new_qkv,
        moment_qkv,
        new_out,
        moment_out,
        new_first[None],
        moment_first[None],
        new_second[None],
        moment_second[None],
    )


def solution(mesh):
    in_specs = (
        P(("dp", "expert"), None),
        P(("dp", "expert"), None),
        P(("dp", "expert"), None),
        P(("dp", "expert"), None),
        P(),
        P(),
        P("expert", None),
        P("expert", None),
        P(),
        P("expert", None, None),
        P("expert", None, None),
        P(),
        P(),
        P("expert", None),
        P("expert", None),
        P("expert", "dp", None),
        P("expert", "dp", None),
    )
    out_specs = (
        P(("dp", "expert"), None),
        P(("dp", "expert"), None),
        P(),
        P(),
        P("expert", None),
        P("expert", None),
        P("expert", "dp", None),
        P("expert", "dp", None),
        P(),
        P(),
        P(),
        P(),
        P("expert", None),
        P("expert", None),
        P("expert", None),
        P("expert", None),
        P("expert", "dp", None),
        P("expert", "dp", None),
        P("expert", "dp", None),
        P("expert", "dp", None),
    )
    return jax.shard_map(body, mesh=mesh, in_specs=in_specs, out_specs=out_specs, check_vma=False)
```
